32 devices in a mesh: rep: 4 (over x, core), own: 8 (over z, y).
Axes of the slice: x: 2, y: 2, z: 4, core: 2. Of those that a mesh axis runs over, the one named last changes fastest.
Arguments:
- weights: float32 [4, 256, 8, 2048], P('rep', 'own'), may hold values from -6 to 6
- anchor: float32 [832, 8, 2048], P('own'), may hold values from -6 to 6
- momentum: float32 [832, 8, 2048], P('own'), may hold values from -3 to 3
- owner: int32 [256], replicated, may hold values from 0 to 7, as said below
- emb_weights: float32 [4, 1024, 2048], P('rep', 'own'), may hold values from -6 to 6
- emb_anchor: float32 [1024, 2048], P('own'), may hold values from -6 to 6
- emb_momentum: float32 [1024, 2048], P('own'), may hold values from -3 to 3
- sketch: float32 [64, 2048], replicated, may hold values from -0.125 to 0.125
- inv_root: float32 [64, 64], replicated
Outputs:
- new_weights: float32 [256, 8, 2048], P('own')
- new_momentum: float32 [832, 8, 2048], P('own')
- new_embedding: float32 [1024, 2048], P('own')
- new_emb_momentum: float32 [1024, 2048], P('own')
The draws below stay inside these ranges and needn't reach their ends.
Inputs may be any that keep to these rules, and one draw needn't show every extreme that they name: Each owner holds at least 8 and at most 104 tiles, and some owner holds exactly 104. Of the 32 tiles of one aligned block, at most 13 have the same owner, and some block reaches 13.
All inputs are finite; a program needn't handle non-finite values.
Results may differ from the reference program's by a relative error of at most 0.0001.
Values sent between devices are 32-bit elements; how exact they have to be, the bound alone decides.
A program may use at most 128 MiB of HBM per device.

```python
import math
import jax
import jax.numpy as jnp
from jax import lax

D = 2048
RANK = 64
TILE_ROWS = 8
TILES_DEV = 32
HALF = 8
HOT = 2
CAP = 104
TILES = 256
SLOTS = 832
EMB = 1024
N_REP = 4
N_OWN = 8


def draw_owner(key, part):
    key_shift, key_hot = jax.random.split(key)
    shifts = jax.random.permutation(key_shift, N_OWN)[:HALF].astype(jnp.int32)
    hot_list = jax.random.permutation(key_hot, N_OWN)[:HOT].astype(jnp.int32)
    block_ids = jnp.arange(N_OWN, dtype=jnp.int32)[:, None]
    column = jnp.arange(TILES_DEV, dtype=jnp.int32)[None, :]
    spread = (block_ids + shifts[jnp.minimum(column, HALF - 1)]) % N_OWN
    crowded = hot_list[(block_ids + column) % HOT]
    return jnp.where(column < HALF, spread, crowded).reshape(-1).astype(jnp.int32)


def draw_inv_root(key, part):
    overall = 1.0 / math.sqrt(1.25 * EMB)
    jitter = jnp.clip(jax.random.normal(key, (RANK, RANK), jnp.float32), -4.0, 4.0)
    return (overall * (jnp.eye(RANK, dtype=jnp.float32) + 0.3 / math.sqrt(RANK) * jitter)).astype(jnp.float32)


def level_of(stream_key, shape, cuts, least, largest):
    gain = 1.0
    for axis_at, blocks in cuts:
        steps = jax.random.uniform(jax.random.fold_in(jax.random.fold_in(stream_key, 6), axis_at), (blocks,), jnp.float32, least / len(cuts), largest / len(cuts))
        gain = gain * jnp.repeat(jnp.exp(steps), shape[axis_at] // blocks).reshape((-1,) + (1,) * (len(shape) - 1 - axis_at))
    return gain


def scatter_about(key, extent, scale, bound, cuts=(), kind=jnp.bfloat16):
    drawn = jax.random.normal(key, extent, jnp.float32) * scale
    if len(cuts) > 0:
        drawn = level_of(key, extent, cuts, -0.22, 0.18) * drawn
    return jnp.clip(drawn, min=-bound, max=bound).astype(kind)


def setup_inputs(seed: int = 0) -> dict:
    key_of = jax.random.split(jax.random.key(seed), 10)
    return {
        "weights": scatter_about(key_of[0], (N_REP, TILES, TILE_ROWS, D), 1.0, 6.0, ((0, 4), (1, 8)), jnp.float32),
        "anchor": scatter_about(key_of[1], (SLOTS, TILE_ROWS, D), 1.0, 6.0, ((0, 8),), jnp.float32),
        "momentum": scatter_about(key_of[2], (SLOTS, TILE_ROWS, D), 0.5, 3.0, ((0, 8),), jnp.float32),
        "owner": draw_owner(jax.random.fold_in(key_of[9], 71), 0),
        "emb_weights": scatter_about(key_of[4], (N_REP, EMB, D), 1.0, 6.0, ((0, 4), (1, 8)), jnp.float32),
        "emb_anchor": scatter_about(key_of[5], (EMB, D), 1.0, 6.0, ((0, 8),), jnp.float32),
        "emb_momentum": scatter_about(key_of[6], (EMB, D), 0.5, 3.0, ((0, 8),), jnp.float32),
        "sketch": scatter_about(key_of[7], (RANK, D), D ** -0.5, 0.125, (), jnp.float32),
        "inv_root": draw_inv_root(jax.random.fold_in(key_of[9], 71), 0),
    }


OUTER_RATE = 0.7
OUTER_MOMENTUM = 0.9


def reference(weights, anchor, momentum, owner, emb_weights, emb_anchor, emb_momentum, sketch, inv_root):
    highest = lax.Precision.HIGHEST
    tile_ids = jnp.arange(owner.shape[0], dtype=jnp.int32)
    same_owner = owner[:, None] == owner[None, :]
    earlier = tile_ids[None, :] < tile_ids[:, None]
    slot_rank = jnp.sum(same_owner & earlier, axis=1).astype(jnp.int32)
    slot = (owner * CAP + slot_rank).astype(jnp.int32)
    anchor_tiles = anchor[slot]
    momentum_tiles = momentum[slot]
    weight_mean = jnp.sum(weights, axis=0) * (1.0 / N_REP)
    outer_grad = anchor_tiles - weight_mean
    moved = OUTER_MOMENTUM * momentum_tiles + outer_grad
    new_weights = anchor_tiles - OUTER_RATE * (outer_grad + OUTER_MOMENTUM * moved)
    new_momentum = jnp.zeros_like(momentum).at[slot].set(moved)
    sketch_total = jnp.zeros((RANK, EMB), jnp.float32)
    for group in range(N_REP):
        emb_diff = emb_anchor - emb_weights[group]
        sketch_total = sketch_total + lax.dot_general(sketch, emb_diff, (((1,), (1,)), ((), ())), precision=highest, preferred_element_type=jnp.float32)
    sketch_mean = sketch_total * (1.0 / N_REP)
    basis_rows = jnp.dot(inv_root, sketch_mean, precision=highest, preferred_element_type=jnp.float32)
    factor_total = jnp.zeros((RANK, D), jnp.float32)
    for group in range(N_REP):
        emb_diff = emb_anchor - emb_weights[group]
        factor_total = factor_total + jnp.dot(basis_rows, emb_diff, precision=highest, preferred_element_type=jnp.float32)
    factor = factor_total * (1.0 / N_REP)
    approx = lax.dot_general(basis_rows, factor, (((0,), (0,)), ((), ())), precision=highest, preferred_element_type=jnp.float32)
    new_emb_momentum = OUTER_MOMENTUM * emb_momentum + approx
    new_embedding = emb_anchor - OUTER_RATE * (approx + OUTER_MOMENTUM * new_emb_momentum)
    return new_weights, new_momentum, new_embedding, new_emb_momentum
```

```python
import functools

import jax
import jax.numpy as jnp
from jax import lax
from jax.experimental import pallas as pl
from jax.experimental.pallas import tpu as pltpu
from jax.sharding import PartitionSpec as P

OUTER_RATE = 0.7
OUTER_MOMENTUM = 0.9
FIXED = 1.0 + OUTER_MOMENTUM
SQUARED = OUTER_MOMENTUM * OUTER_MOMENTUM
LINE = 4
CHUNKS = 4


def owner_tables(owner, tiles_dev, per_pair, capacity, own_index, own_count):
    across = own_count // LINE
    tile_count = owner.shape[0]
    tile_ids = jnp.arange(tile_count, dtype=jnp.int32)
    block_of = tile_ids // tiles_dev
    same_owner = owner[:, None] == owner[None, :]
    earlier = tile_ids[None, :] < tile_ids[:, None]
    slot_rank = jnp.sum(same_owner & earlier, axis=1, dtype=jnp.int32)
    pair_rank = jnp.sum(
        same_owner & earlier & (block_of[:, None] == block_of[None, :]), axis=1, dtype=jnp.int32
    )
    my_z, my_y = own_index // across, own_index % across
    owner_z, turn = owner // across, (owner % across) ^ my_y
    back_key = block_of * per_pair + pair_rank
    held_here = owner == own_index
    pick_key = jnp.where(
        (owner_z == my_z) & (block_of % across == my_y),
        (turn * LINE + block_of // across) * per_pair + pair_rank,
        -1,
    )
    held_key = jnp.where(held_here, back_key, -1)
    slot_key = jnp.where(held_here, slot_rank, -1)
    pair_ids = jnp.arange(own_count * per_pair, dtype=jnp.int32)[:, None]
    slot_ids = jnp.arange(capacity, dtype=jnp.int32)[:, None]

    def look_up(ids, key, value):
        return jnp.sum(jnp.where(key[None, :] == ids, value[None, :], 0), axis=1, dtype=jnp.int32)

    pick = look_up(pair_ids, pick_key, tile_ids % tiles_dev)
    merge = jnp.where(
        owner_z == my_z, turn * per_pair + pair_rank, jnp.where(owner_z < my_z, -1, -2)
    ).astype(jnp.int32)
    owner_pick = look_up(pair_ids, held_key, slot_rank)
    owner_read = look_up(slot_ids, slot_key, back_key + 1)
    return (pick, merge, owner_read, owner_pick)


def flip(index, bits):
    out, unit = index, 1
    while unit <= bits:
        if bits & unit:
            out = out + unit - 2 * unit * ((index // unit) % 2)
        unit *= 2
    return out


def step_kernel(
    own_count, per_pair, rank,
    pick, merge, owner_read, owner_pick, weights, anchor, momentum,
    emb_weights, emb_anchor, emb_momentum, sketch, inv_root,
    new_weights, new_momentum, new_embedding, new_emb_momentum,
    *scratch,
):
    across, chunks = own_count // LINE, CHUNKS
    span = 2 * LINE - 1
    take = iter(scratch)
    local_sem, mine_sem, barrier_pad = next(take), next(take), None
    anchor_part, momentum_part, anchor_all = next(take), next(take), next(take)
    mine, core_in, chip_out, chip_in = next(take), next(take), next(take), next(take)
    core_send, core_recv, chip_send, chip_recv = next(take), next(take), next(take), next(take)
    line = [{d: next(take) for d in range(1 - LINE, LINE)} for _ in range(chunks)]
    line_send, line_recv = next(take), next(take)
    turned = next(take)
    turn_send, turn_recv = next(take), next(take)
    gathered = [next(take) for _ in range(chunks)]
    cross_send, cross_recv, near_send, near_recv, pass_send, pass_recv = (next(take) for _ in range(6))
    held_out = next(take)
    held_in = {d: next(take) for d in range(1 - LINE, LINE)}
    held_send, held_recv = next(take), next(take)
    merged = {d: next(take) for d in range(1 - LINE, LINE) if d}
    below = {d: next(take) for d in range(LINE - 1)}
    above = {-d: next(take) for d in range(LINE - 1)}
    merge_send, merge_recv = next(take), next(take)
    fresh_send, fresh_recv = next(take), next(take)
    emb_w, emb_a, emb_m, sketch_v = next(take), next(take), next(take), next(take)
    diff, sketch_own, sketch_half, sketch_core, sketch_chip, basis_ref = (next(take) for _ in range(6))
    f_own, f_core, f_turn, f_turn_in, f_line, f_line_in, f_chip, f_chip_in, f_all, f_flat = (
        next(take) for _ in range(10)
    )
    emb_send, emb_recv, f_turn_send, f_turn_recv, f_line_send, f_line_recv = (
        next(take) for _ in range(6)
    )
    g_turn_send, g_turn_recv, g_line_send, g_line_recv = (next(take) for _ in range(4))

    rep = lax.axis_index("rep")
    own = lax.axis_index("own")
    core = rep % 2
    z, y = own // across, own % across
    core_peer, chip_peer, far_peer = flip(rep, 1), flip(rep, 2), flip(rep, 3)
    tiles, slots = weights.shape[1], anchor.shape[0]
    width = anchor.shape[2]
    part = width // 4
    w = part // chunks
    f32, highest = jnp.float32, lax.Precision.HIGHEST

    def columns(quarter, c=None):
        if c is None:
            return pl.ds(pl.multiple_of(quarter * part, 128), part)
        return pl.ds(pl.multiple_of(quarter * part + c * w, 128), w)

    def remote(src, dst, send, recv, to_rep, to_own):
        return pltpu.make_async_remote_copy(
            src_ref=src, dst_ref=dst, send_sem=send, recv_sem=recv,
            device_id=(to_rep, to_own), device_id_type=pl.DeviceIdType.MESH,
        )

    def when(*conditions):
        held = conditions[0]
        for condition in conditions[1:]:
            held = held & condition
        return pl.when(held)

    def inside(d):
        return (z + d >= 0) & (z + d <= LINE - 1)

    mine_loads = [
        pltpu.make_async_copy(
            weights.at[0, :, :, columns(quarter, c)], mine.at[c, j], mine_sem.at[c, j]
        )
        for j, quarter in ((1, chip_peer), (0, rep))
        for c in range(chunks)
    ]
    emb_loads = [
        pltpu.make_async_copy(emb_weights.at[0], emb_w, local_sem.at[0]),
        pltpu.make_async_copy(emb_anchor, emb_a, local_sem.at[1]),
        pltpu.make_async_copy(sketch, sketch_v, local_sem.at[2]),
    ]
    part_loads = [
        pltpu.make_async_copy(anchor.at[:, :, columns(rep)], anchor_part, local_sem.at[3]),
        pltpu.make_async_copy(momentum.at[:, :, columns(rep)], momentum_part, local_sem.at[4]),
    ]
    late_loads = [
        pltpu.make_async_copy(anchor, anchor_all, local_sem.at[5]),
        pltpu.make_async_copy(momentum, new_momentum, local_sem.at[6]),
        pltpu.make_async_copy(emb_momentum, emb_m, local_sem.at[7]),
    ]
    for copy in emb_loads + mine_loads + part_loads:
        copy.start()

    barrier = pltpu.get_barrier_semaphore()
    peers = [(core_peer, own), (chip_peer, own)]
    peers += [(rep, flip(own, k)) for k in range(1, across)]
    peers += [(rep, flip(own, k * across)) for k in range(1, LINE)]
    for peer in peers:
        pl.semaphore_signal(barrier, inc=1, device_id=peer, device_id_type=pl.DeviceIdType.MESH)

    for copy in emb_loads:
        copy.wait()
    diff[...] = emb_a[...] - emb_w[...]
    sketched = jnp.zeros(sketch_own.shape, f32)
    for q in range(4):
        at = slice(q * part, (q + 1) * part)
        sketched = sketched + lax.dot_general(
            sketch_v[:, at], diff[:, at], (((1,), (1,)), ((), ())),
            precision=highest, preferred_element_type=f32,
        )
    sketch_own[...] = sketched
    pl.semaphore_wait(barrier, len(peers))

    core_copies = [
        remote(
            weights.at[0, :, :, columns(quarter, c)], core_in.at[c, j],
            core_send.at[c, j], core_recv.at[c, j], core_peer, own,
        )
        for j, quarter in ((1, far_peer), (0, core_peer))
        for c in range(chunks)
    ]
    for copy in core_copies[:chunks]:
        copy.start()
    sketch_copies = [
        remote(sketch_own, sketch_core, emb_send.at[0], emb_recv.at[0], core_peer, own),
        remote(sketch_half, sketch_chip, emb_send.at[1], emb_recv.at[1], chip_peer, own),
    ]
    sketch_copies[0].start()
    for copy in core_copies[chunks:]:
        copy.start()

    def held_copy(d, k):
        return remote(
            held_out.at[z + d, k - 1], held_in[d].at[pl.ds(k * per_pair, per_pair)],
            held_send.at[d + LINE - 1, k], held_recv.at[d + LINE - 1, k], rep, flip(own, k),
        )

    def held_fill(d, k):
        block = flip(own, k) + d * across

        def fill(p, carry):
            slot = owner_pick[block * per_pair + p]
            a = anchor_part[slot]
            value = a - OUTER_RATE * (FIXED * a + SQUARED * momentum_part[slot])
            if k:
                held_out[z + d, k - 1, p] = value
            else:
                held_in[d][p] = value
            return carry

        lax.fori_loop(0, per_pair, fill, 0)

    far_first = [s * e for s in range(LINE - 1, 0, -1) for e in (1, -1)] + [0]

    chip_copies = [
        remote(chip_out.at[c], chip_in.at[c], chip_send.at[c], chip_recv.at[c], chip_peer, own)
        for c in range(chunks)
    ]

    def half_sum(c):
        mine_loads[c].wait()
        core_copies[c].wait_recv()
        chip_out[c] = mine[c, 1] + core_in[c, 1]
        chip_copies[c].start()

    for c in range(2):
        half_sum(c)
    sketch_copies[0].wait_recv()
    sketch_half[...] = sketch_own[...] + sketch_core[...]
    sketch_copies[1].start()
    for c in range(2, chunks):
        half_sum(c)
    for copy in part_loads:
        copy.wait()
    for d in far_first:
        @when(inside(d))
        def _(d=d):
            for k in range(1, across):
                held_fill(d, k)
                held_copy(d, k).start()
            held_fill(d, 0)
    for copy in late_loads:
        copy.start()

    turn_rows, line_width = rank // across, 2 * part // LINE

    def emb_core():
        return remote(f_own.at[1 - core], f_core, emb_send.at[2], emb_recv.at[2], core_peer, own)

    def emb_turn(k):
        return remote(
            f_turn.at[flip(y, k)], f_turn_in.at[k], f_turn_send.at[k], f_turn_recv.at[k],
            rep, flip(own, k),
        )

    def emb_line(k):
        return remote(
            f_line.at[flip(z, k)], f_line_in.at[k], f_line_send.at[k], f_line_recv.at[k],
            rep, flip(own, k * across),
        )

    def emb_chip():
        return remote(f_chip, f_chip_in, emb_send.at[3], emb_recv.at[3], chip_peer, own)

    def back_line(k):
        here = f_all.at[core, y, z]
        return remote(here, here, g_line_send.at[k], g_line_recv.at[k], rep, flip(own, k * across))

    def back_turn(k):
        here = f_all.at[core, y]
        return remote(here, here, g_turn_send.at[k], g_turn_recv.at[k], rep, flip(own, k))

    def back_core():
        here = f_all.at[core]
        return remote(here, here, emb_send.at[4], emb_recv.at[4], core_peer, own)

    def emb_0():
        sketch_copies[1].wait_recv()
        mean_sketch = (sketch_half[...] + sketch_chip[...]) * 0.25
        basis = jnp.dot(inv_root[...], mean_sketch, precision=highest, preferred_element_type=f32)
        basis_ref[...] = basis
        for q in range(4):
            f_own[q % 2, :, (q // 2) * part : (q // 2 + 1) * part] = jnp.dot(
                basis, diff[:, q * part : (q + 1) * part],
                precision=highest, preferred_element_type=f32,
            )
        emb_core().start()

    def emb_1():
        emb_core().wait_recv()
        for b in range(across):
            rows = slice(b * turn_rows, (b + 1) * turn_rows)
            f_turn[b] = f_own[core, rows] + f_core[rows]
        for k in range(1, across):
            emb_turn(k).start()

    def emb_2():
        for k in range(1, across):
            emb_turn(k).wait_recv()
        total = f_turn[y]
        for k in range(1, across):
            total = total + f_turn_in[k]
        for a in range(LINE):
            f_line[a] = total[:, a * line_width : (a + 1) * line_width]
        for k in range(1, LINE):
            emb_line(k).start()

    def emb_3():
        for k in range(1, LINE):
            emb_line(k).wait_recv()
        total = f_line[z]
        for k in range(1, LINE):
            total = total + f_line_in[k]
        f_chip[...] = total
        emb_chip().start()

    def emb_4():
        emb_chip().wait_recv()
        f_all[core, y, z] = (f_chip[...] + f_chip_in[...]) * 0.25
        for k in range(1, LINE):
            back_line(k).start()

    def emb_5():
        for k in range(1, LINE):
            back_line(k).wait_recv()
        for k in range(1, across):
            back_turn(k).start()

    def emb_6():
        for k in range(1, across):
            back_turn(k).wait_recv()
        back_core().start()

    def emb_7():
        late_loads[2].wait()
        back_core().wait_recv()
        for h in range(2):
            for b in range(across):
                for a in range(LINE):
                    quarter = h + 2 * ((a * line_width) // part)
                    at = quarter * part + (a * line_width) % part
                    f_flat[b * turn_rows : (b + 1) * turn_rows, at : at + line_width] = f_all[h, b, a]
        for q in range(4):
            at = slice(q * part, (q + 1) * part)
            approx = lax.dot_general(
                basis_ref[...], f_flat[:, at], (((0,), (0,)), ((), ())),
                precision=highest, preferred_element_type=f32,
            )
            moved = OUTER_MOMENTUM * emb_m[:, at] + approx
            new_emb_momentum[:, at] = moved
            new_embedding[:, at] = emb_a[:, at] - OUTER_RATE * (approx + OUTER_MOMENTUM * moved)

    def line_copy(c, d):
        step = 1 if d > 0 else -1
        return remote(
            line[c][d - step], line[c][d], line_send.at[c, d + LINE - 1],
            line_recv.at[c, d + LINE - 1], rep, own - step * across,
        )

    def line_sends(d):
        step = 1 if d > 0 else -1
        return (z - step >= 0) & (z - step <= LINE - 1) & inside(d - step)

    def rows_of(d, k):
        return pl.ds((flip(own, k) + d * across) * per_pair, per_pair)

    def turn_copy(c, d, k, sending):
        return remote(
            turned.at[c, z + d, k - 1], gathered[c].at[rep, rows_of(d, 0 if sending else k)],
            turn_send.at[c, d + LINE - 1, k], turn_recv.at[c, d + LINE - 1, k], rep, flip(own, k),
        )

    def item_copy(c, d, k, kind):
        at = (c, d + LINE - 1, k)
        if kind == "pass":
            there = gathered[c].at[chip_peer, rows_of(d, k)]
            return remote(there, there, pass_send.at[at], pass_recv.at[at], core_peer, own)
        here = gathered[c].at[rep, rows_of(d, k)]
        if kind == "cross":
            return remote(here, here, cross_send.at[at], cross_recv.at[at], chip_peer, own)
        return remote(here, here, near_send.at[at], near_recv.at[at], core_peer, own)

    def choose(c, d, k):
        block = (k * LINE + z + d) * per_pair
        first = (own + d * across) * per_pair

        def fill(p, carry):
            value = line[c][d][pick[block + p]]
            if k:
                turned[c, z + d, k - 1, p] = value
            else:
                gathered[c][rep, first + p] = value
            return carry

        lax.fori_loop(0, per_pair, fill, 0)

    def spread(c, d):
        for k in range(1, across):
            choose(c, d, k)
            turn_copy(c, d, k, True).start()
        choose(c, d, 0)
        item_copy(c, d, 0, "cross").start()
        item_copy(c, d, 0, "near").start()

    def mean_ready(c):
        mine_loads[chunks + c].wait()
        core_copies[chunks + c].wait_recv()
        chip_copies[c].wait_recv()
        line[c][0][...] = (mine[c, 0] + core_in[c, 0] + chip_in[c]) * 0.25
        for d in (1, -1):
            @when(line_sends(d))
            def _(d=d):
                line_copy(c, d).start()
        spread(c, 0)

    def line_arrived(c, d):
        step = 1 if d > 0 else -1

        @when(inside(d))
        def _():
            line_copy(c, d).wait_recv()
            if abs(d) < LINE - 1:
                @when(line_sends(d + step))
                def _():
                    line_copy(c, d + step).start()
            spread(c, d)

    def turn_arrived(c, d):
        @when(inside(d))
        def _():
            for k in range(1, across):
                turn_copy(c, d, k, False).wait_recv()
                item_copy(c, d, k, "cross").start()
                item_copy(c, d, k, "near").start()

    def pass_on(c, d):
        @when(inside(d))
        def _():
            for k in range(across):
                item_copy(c, d, k, "cross").wait_recv()
                item_copy(c, d, k, "pass").start()

    def base_rows(first, count):
        def body(s, carry):
            for q in range(4):
                at = pl.ds(q * part, part)
                new_momentum[s, :, at] = OUTER_MOMENTUM * new_momentum[s, :, at] + anchor_all[s, :, at]
            return carry

        lax.fori_loop(first, first + count, body, 0)

    def advance(c):
        for d in range(1 - LINE, LINE):
            @when(inside(d))
            def _(d=d):
                for k in range(across):
                    item_copy(c, d, k, "near").wait_recv()
                    item_copy(c, d, k, "pass").wait_recv()

        def body(s, carry):
            found = owner_read[s]
            row = jnp.maximum(found - 1, 0)
            kept = jnp.full((new_momentum.shape[1], w), found, jnp.int32) > 0
            for q in range(4):
                at = pl.ds(q * part + c * w, w)
                new_momentum[s, :, at] = jnp.where(
                    kept, new_momentum[s, :, at] - gathered[c][q, row], 0.0
                )
            return carry

        lax.fori_loop(0, slots, body, 0)

    def merge_copy(d, c):
        step = 1 if d > 0 else -1
        target = (below if d > 0 else above)[d - step]
        at = (c, d + LINE - 1)
        return remote(
            merged[d].at[c], target.at[c], merge_send.at[at], merge_recv.at[at], rep, own + step * across
        )

    def merge_tiles(d, c, store, incoming):
        first = (own + d * across) * tiles
        at = pl.ds(c * w, w)

        def body(t, carry):
            key = merge[first + t]
            value = held_in[d][jnp.maximum(key, 0), :, at]
            if incoming is not None:
                keys = jnp.full((value.shape[0], w), key, jnp.int32)
                value = jnp.where(keys >= 0, value, incoming(t, keys))
            store(t, value)
            return carry

        lax.fori_loop(0, tiles, body, 0)

    def merge_step(d, c):
        step = 1 if d > 0 else -1
        source = (below if d > 0 else above).get(d)
        has_source = (z >= 1) if d > 0 else (z <= LINE - 2)

        def store(t, value):
            merged[d][c, t] = value

        def landed():
            if c == 0:
                for k in range(1, across):
                    held_copy(d, k).wait_recv()

        @when(inside(d), jnp.logical_not(has_source))
        def _():
            landed()
            merge_tiles(d, c, store, None)
            merge_copy(d, c).start()

        if source is not None:
            @when(inside(d), has_source)
            def _():
                landed()
                merge_copy(d + step, c).wait_recv()
                merge_tiles(d, c, store, lambda t, keys: source[c, t])
                merge_copy(d, c).start()

    def fresh_copy(c, kind):
        at = {"cross": 0, "near": 1, "pass": 2}[kind]
        here = new_weights.at[:, :, columns(chip_peer if kind == "pass" else rep, c)]
        return remote(
            here, here, fresh_send.at[at, c], fresh_recv.at[at, c],
            chip_peer if kind == "cross" else core_peer, own,
        )

    def renew(c):
        @when(z >= 1)
        def _():
            merge_copy(1, c).wait_recv()

        @when(z <= LINE - 2)
        def _():
            merge_copy(-1, c).wait_recv()

        if c == 0:
            for k in range(1, across):
                held_copy(0, k).wait_recv()

        def incoming(t, keys):
            return jnp.where(keys == -1, below[0][c, t], above[0][c, t])

        def store(t, value):
            new_weights[t, :, columns(rep, c)] = value + (OUTER_RATE * FIXED) * line[c][0][t]

        merge_tiles(0, c, store, incoming)
        fresh_copy(c, "cross").start()
        fresh_copy(c, "near").start()

    def fresh_pass(c):
        fresh_copy(c, "cross").wait_recv()
        fresh_copy(c, "pass").start()

    events = []

    def at_time(time, step, *arguments):
        events.append((time, len(events), step, arguments))

    schedule(at_time, chunks, slots, locals())
    for _, _, step, arguments in sorted(events, key=lambda event: event[:2]):
        step(*arguments)

    for c in range(chunks):
        fresh_copy(c, "near").wait_recv()
        fresh_copy(c, "pass").wait_recv()
    for copy in core_copies + chip_copies + sketch_copies:
        copy.wait_send()
    for k in range(1, across):
        emb_turn(k).wait_send()
        back_turn(k).wait_send()
    for k in range(1, LINE):
        emb_line(k).wait_send()
        back_line(k).wait_send()
    for copy in (emb_core(), emb_chip(), back_core()):
        copy.wait_send()
    for c in range(chunks):
        for kind in ("cross", "near", "pass"):
            fresh_copy(c, kind).wait_send()
    for d in range(1 - LINE, LINE):
        @when(inside(d))
        def _(d=d):
            for k in range(1, across):
                held_copy(d, k).wait_send()
            for c in range(chunks):
                for k in range(across):
                    if k:
                        turn_copy(c, d, k, True).wait_send()
                    for kind in ("cross", "near", "pass"):
                        item_copy(c, d, k, kind).wait_send()
                if d:
                    merge_copy(d, c).wait_send()

        if d:
            @when(line_sends(d))
            def _(d=d):
                for c in range(chunks):
                    line_copy(c, d).wait_send()


def schedule(at_time, chunks, slots, steps):
    grain = 4.0 / chunks
    both = (1, -1)
    first = 8.0
    for c in range(chunks):
        ready = first + 2.85 * grain * c
        at_time(ready, steps["mean_ready"], c)
        at_time(ready + 4.0, steps["turn_arrived"], c, 0)
        arrive = {1: ready + 4.9, 2: 20.0 + 4.3 * grain * c, 3: 26.0 + 6.0 * grain * c}
        for s in range(1, LINE):
            for e in both:
                at_time(arrive[s], steps["line_arrived"], c, s * e)
                at_time(arrive[s] + 4.0, steps["turn_arrived"], c, s * e)
        later = {0: 22.0 + 2.4 * grain * c, 1: 30.0 + 4.8 * grain * c, 2: 36.0 + 5.0 * grain * c, 3: 38.0 + 6.0 * grain * c}
        for s in range(LINE):
            for e in both if s else (1,):
                at_time(later[s], steps["pass_on"], c, s * e)
        at_time(max(later.values()) + 1.5, steps["advance"], c)
        pieces = slots // chunks
        extra = slots - pieces * chunks if c == chunks - 1 else 0
        if c == 0:
            at_time(first + 3.0, lambda: (steps["late_loads"][0].wait(), steps["late_loads"][1].wait()))
        at_time(first + 3.1 + 2.85 * c, steps["base_rows"], c * pieces, pieces + extra)
        merge_at = {3: 17.5 + 0.5 * c, 2: 24.5 + 8.5 * grain * c, 1: 36.0 + 6.5 * grain * c}
        for s in range(1, LINE):
            for e in both:
                at_time(merge_at[s], steps["merge_step"], s * e, c)
        at_time(47.0 + 4.0 * grain * c, steps["renew"], c)
        at_time(60.0 + c * 0.5, steps["fresh_pass"], c)
    for n, time in enumerate((7.9, 11.5, 17.0, 23.0, 33.0, 39.0, 44.0, 49.0)):
        at_time(time, steps["emb_%d" % n])


def step_call(weights, anchor, momentum, embed, tables, own_count, per_pair):
    tiles, rows, width = weights.shape[1:]
    slots, part = anchor.shape[0], width // 4
    across, chunks = own_count // LINE, CHUNKS
    w, span = part // chunks, 2 * LINE - 1
    pairs = own_count * per_pair
    f32, dma = jnp.float32, pltpu.SemaphoreType.DMA
    emb_rows, rank = embed[1].shape[0], embed[3].shape[0]
    vmem = lambda *shape: pltpu.VMEM(shape, f32)
    turn_rows, line_width = rank // across, 2 * part // LINE
    scratch = [
        dma((8,)), dma((chunks, 2)),
        vmem(slots, rows, part), vmem(slots, rows, part), vmem(slots, rows, width),
        vmem(chunks, 2, tiles, rows, w), vmem(chunks, 2, tiles, rows, w),
        vmem(chunks, tiles, rows, w), vmem(chunks, tiles, rows, w),
        dma((chunks, 2)), dma((chunks, 2)), dma((chunks,)), dma((chunks,)),
    ]
    scratch += [vmem(tiles, rows, w) for _ in range(chunks * span)]
    scratch += [dma((chunks, span)), dma((chunks, span))]
    scratch += [vmem(chunks, LINE, across - 1, per_pair, rows, w)]
    scratch += [dma((chunks, span, across)), dma((chunks, span, across))]
    scratch += [vmem(4, pairs, rows, w) for _ in range(chunks)]
    scratch += [dma((chunks, span, across)) for _ in range(6)]
    scratch += [vmem(LINE, across - 1, per_pair, rows, part)]
    scratch += [vmem(across * per_pair, rows, part) for _ in range(span)]
    scratch += [dma((span, across)), dma((span, across))]
    scratch += [vmem(chunks, tiles, rows, w) for _ in range(span - 1)]
    scratch += [vmem(chunks, tiles, rows, w) for _ in range(2 * (LINE - 1))]
    scratch += [dma((chunks, span)), dma((chunks, span)), dma((3, chunks)), dma((3, chunks))]
    scratch += [
        vmem(emb_rows, width), vmem(emb_rows, width), vmem(emb_rows, width), vmem(rank, width),
        vmem(emb_rows, width),
    ]
    scratch += [vmem(rank, emb_rows) for _ in range(5)]
    scratch += [
        vmem(2, rank, 2 * part), vmem(rank, 2 * part),
        vmem(across, turn_rows, 2 * part), vmem(across, turn_rows, 2 * part),
        vmem(LINE, turn_rows, line_width), vmem(LINE, turn_rows, line_width),
        vmem(turn_rows, line_width), vmem(turn_rows, line_width),
        vmem(2, across, LINE, turn_rows, line_width), vmem(rank, width),
        dma((5,)), dma((5,)), dma((across,)), dma((across,)), dma((LINE,)), dma((LINE,)),
        dma((across,)), dma((across,)), dma((LINE,)), dma((LINE,)),
    ]
    return pl.pallas_call(
        functools.partial(step_kernel, own_count, per_pair, rank),
        out_shape=(
            pltpu.VMEM((tiles, rows, width), f32),
            pltpu.VMEM((slots, rows, width), f32),
            pltpu.VMEM((emb_rows, width), f32),
            pltpu.VMEM((emb_rows, width), f32),
        ),
        in_specs=[pl.BlockSpec(memory_space=pltpu.SMEM)] * 4 + [pl.BlockSpec(memory_space=pltpu.HBM)] * 7
        + [pl.BlockSpec(memory_space=pltpu.VMEM)],
        out_specs=(pl.BlockSpec(memory_space=pltpu.VMEM),) * 4,
        scratch_shapes=scratch,
        compiler_params=pltpu.CompilerParams(
            collective_id=0, has_side_effects=True, vmem_limit_bytes=50 * 1024 * 1024
        ),
        cost_estimate=pl.CostEstimate(flops=20000000, bytes_accessed=300000000, transcendentals=0),
    )(*tables, weights, anchor, momentum, *embed)


def local(
    weights, anchor, momentum, owner, emb_weights, emb_anchor, emb_momentum, sketch, inv_root
):
    own_count = lax.axis_size("own")
    own_index = lax.axis_index("own")
    tiles_dev = weights.shape[1]
    half_tiles = min(tiles_dev // 2, own_count)
    hot_count = max(own_count // 4, 1)
    per_pair = (tiles_dev - half_tiles) // hot_count + 1
    tables = owner_tables(owner, tiles_dev, per_pair, anchor.shape[0], own_index, own_count)
    embed = (emb_weights, emb_anchor, emb_momentum, sketch, inv_root)
    return step_call(weights, anchor, momentum, embed, tables, own_count, per_pair)


def solution(mesh):
    placed = (
        P("rep", "own", None, None),
        P("own", None, None),
        P("own", None, None),
        P(),
        P("rep", "own", None),
        P("own", None),
        P("own", None),
        P(),
        P(),
    )
    return jax.shard_map(
        local,
        mesh=mesh,
        in_specs=placed,
        out_specs=(P("own", None, None), P("own", None, None), P("own", None), P("own", None)),
        check_vma=False,
    )
```

```python
import functools

import jax
import jax.numpy as jnp
from jax import lax
from jax.experimental import pallas as pl
from jax.experimental.pallas import tpu as pltpu
from jax.sharding import PartitionSpec as P

OUTER_RATE = 0.7
OUTER_MOMENTUM = 0.9
FIXED = 1.0 + OUTER_MOMENTUM
SQUARED = OUTER_MOMENTUM * OUTER_MOMENTUM
LINE = 4
CHUNKS = 4
(
    HALF, SKETCH, HELD, LATE, MEAN, LINED, TURNED, PASS, BASE,
    ADVANCE, MERGE, RENEW, FRESH, EMBED,
) = range(14)
ORDER = (
    (HELD, 0), (HELD, -3), (HALF, 1), (HALF, 0), (HALF, 2), (HELD, 3), (HELD, 1), (SKETCH,), (HELD, -2),
    (MEAN, 1), (HALF, 3), (MEAN, 0), (MEAN, 2), (MERGE, 0, -3), (LINED, 1, 1), (LATE,), (MERGE, 0, 3),
    (EMBED, 0), (LINED, 0, -1), (EMBED, 1), (MEAN, 3), (HELD, 2), (MERGE, 1, 3), (LINED, 1, -1),
    (TURNED, 1, 1), (TURNED, 2, 0), (LINED, 0, 1), (LINED, 2, 1), (TURNED, 0, 0), (MERGE, 2, 3), (BASE, 0),
    (LINED, 0, -2), (MERGE, 0, -2), (EMBED, 2), (PASS, 2, 0), (LINED, 2, -1), (LINED, 3, -1), (TURNED, 3, 0),
    (TURNED, 1, 0), (LINED, 0, 2), (LINED, 1, 2), (MERGE, 2, -3), (MERGE, 0, 2), (LINED, 1, -2),
    (LINED, 0, -3), (LINED, 2, 2), (MERGE, 1, -3), (TURNED, 2, -1), (MERGE, 2, -2), (TURNED, 0, 1),
    (HELD, -1), (TURNED, 0, -2), (LINED, 2, -2), (LINED, 3, 1), (MERGE, 1, -2), (MERGE, 1, 2), (TURNED, 0, 2),
    (MERGE, 3, -3), (EMBED, 3), (TURNED, 0, -3), (MERGE, 0, 1), (LINED, 0, 3), (TURNED, 1, -1),
    (TURNED, 1, 2), (BASE, 3), (LINED, 1, -3), (MERGE, 3, 3), (LINED, 2, 3), (LINED, 3, -2), (PASS, 0, -2),
    (LINED, 1, 3), (MERGE, 1, 1), (TURNED, 0, -1), (MERGE, 0, -1), (LINED, 3, 2), (TURNED, 1, -2), (EMBED, 4),
    (MERGE, 3, -2), (TURNED, 0, 3), (BASE, 1), (TURNED, 2, 1), (TURNED, 2, 3), (TURNED, 1, 3), (LINED, 2, -3),
    (TURNED, 2, 2), (MERGE, 2, 2), (TURNED, 3, -2), (PASS, 0, 2), (RENEW, 0), (PASS, 1, 2), (PASS, 1, -2),
    (PASS, 2, -1), (MERGE, 3, 2), (MERGE, 1, -1), (TURNED, 3, 1), (TURNED, 1, -3), (LINED, 3, 3),
    (LINED, 3, -3), (PASS, 0, 3), (TURNED, 3, -1), (PASS, 1, 3), (PASS, 2, 1), (MERGE, 2, -1),
    (TURNED, 2, -2), (TURNED, 3, -3), (MERGE, 2, 1), (PASS, 0, -3), (MERGE, 3, -1), (TURNED, 2, -3),
    (PASS, 1, -1), (PASS, 1, 1), (EMBED, 5), (PASS, 3, 0), (PASS, 1, -3), (PASS, 3, -2), (PASS, 1, 0),
    (TURNED, 3, 2), (BASE, 2), (PASS, 0, 0), (MERGE, 3, 1), (RENEW, 1), (FRESH, 0), (ADVANCE, 1),
    (PASS, 3, 2), (PASS, 2, -3), (PASS, 2, 3), (EMBED, 6), (PASS, 2, -2), (PASS, 2, 2), (PASS, 0, -1),
    (TURNED, 3, 3), (PASS, 3, -3), (PASS, 3, -1), (RENEW, 2), (PASS, 0, 1), (FRESH, 1), (RENEW, 3),
    (EMBED, 7), (ADVANCE, 2), (FRESH, 2), (PASS, 3, 3), (PASS, 3, 1), (ADVANCE, 0), (FRESH, 3), (ADVANCE, 3),
)


def owner_tables(owner, tiles_dev, per_pair, capacity, own_index, own_count):
    across = own_count // LINE
    tile_count = owner.shape[0]
    tile_ids = jnp.arange(tile_count, dtype=jnp.int32)
    block_of = tile_ids // tiles_dev
    same_owner = owner[:, None] == owner[None, :]
    earlier = tile_ids[None, :] < tile_ids[:, None]
    slot_rank = jnp.sum(same_owner & earlier, axis=1, dtype=jnp.int32)
    pair_rank = jnp.sum(
        same_owner & earlier & (block_of[:, None] == block_of[None, :]), axis=1, dtype=jnp.int32
    )
    my_z, my_y = own_index // across, own_index % across
    owner_z, turn = owner // across, (owner % across) ^ my_y
    back_key = block_of * per_pair + pair_rank
    held_here = owner == own_index
    pick_key = jnp.where(
        (owner_z == my_z) & (block_of % across == my_y),
        (turn * LINE + block_of // across) * per_pair + pair_rank,
        -1,
    )
    held_key = jnp.where(held_here, back_key, -1)
    slot_key = jnp.where(held_here, slot_rank, -1)
    pair_ids = jnp.arange(own_count * per_pair, dtype=jnp.int32)[:, None]
    slot_ids = jnp.arange(capacity, dtype=jnp.int32)[:, None]

    def look_up(ids, key, value):
        return jnp.sum(jnp.where(key[None, :] == ids, value[None, :], 0), axis=1, dtype=jnp.int32)

    pick = look_up(pair_ids, pick_key, tile_ids % tiles_dev)
    merge = jnp.where(
        owner_z == my_z, turn * per_pair + pair_rank, jnp.where(owner_z < my_z, -1, -2)
    ).astype(jnp.int32)
    owner_pick = look_up(pair_ids, held_key, slot_rank)
    owner_read = look_up(slot_ids, slot_key, back_key + 1)
    return (pick, merge, owner_read, owner_pick)


def flip(index, bits):
    out, unit = index, 1
    while unit <= bits:
        if bits & unit:
            out = out + unit - 2 * unit * ((index // unit) % 2)
        unit *= 2
    return out


def step_kernel(
    own_count, per_pair, rank,
    pick, merge, owner_read, owner_pick, weights, anchor, momentum,
    emb_weights, emb_anchor, emb_momentum, sketch, inv_root,
    new_weights, new_momentum, new_embedding, new_emb_momentum,
    *scratch,
):
    across, chunks = own_count // LINE, CHUNKS
    take = iter(scratch)
    local_sem, mine_sem = next(take), next(take)
    held_order = [at[1] for at in ORDER if at[0] == HELD]
    merge_order = {at[2]: at[1] for at in reversed(ORDER) if at[0] == MERGE}
    renew_order = [at[1] for at in ORDER if at[0] == RENEW]
    base_order = [at[1] for at in ORDER if at[0] == BASE]
    anchor_part, momentum_part, anchor_all = next(take), next(take), next(take)
    mine, core_in, chip_out, chip_in = next(take), next(take), next(take), next(take)
    core_send, core_recv, chip_send, chip_recv = next(take), next(take), next(take), next(take)
    line = [{d: next(take) for d in range(1 - LINE, LINE)} for _ in range(chunks)]
    line_send, line_recv = next(take), next(take)
    turned = next(take)
    turn_send, turn_recv = next(take), next(take)
    gathered = [next(take) for _ in range(chunks)]
    cross_send, cross_recv, near_send, near_recv, pass_send, pass_recv = (next(take) for _ in range(6))
    held_out = next(take)
    held_in = {d: next(take) for d in range(1 - LINE, LINE)}
    held_send, held_recv = next(take), next(take)
    merged = {d: next(take) for d in range(1 - LINE, LINE) if d}
    below = {d: next(take) for d in range(LINE - 1)}
    above = {-d: next(take) for d in range(LINE - 1)}
    merge_send, merge_recv = next(take), next(take)
    fresh_send, fresh_recv = next(take), next(take)
    emb_w, emb_a, emb_m, sketch_v = next(take), next(take), next(take), next(take)
    diff, sketch_own, sketch_half, sketch_core, sketch_chip, basis_ref = (next(take) for _ in range(6))
    f_own, f_core, f_turn, f_turn_in, f_line, f_line_in, f_chip, f_chip_in, f_all, f_flat = (
        next(take) for _ in range(10)
    )
    emb_send, emb_recv, f_turn_send, f_turn_recv, f_line_send, f_line_recv = (
        next(take) for _ in range(6)
    )
    g_turn_send, g_turn_recv, g_line_send, g_line_recv = (next(take) for _ in range(4))

    rep = lax.axis_index("rep")
    own = lax.axis_index("own")
    core = rep % 2
    z, y = own // across, own % across
    core_peer, chip_peer, far_peer = flip(rep, 1), flip(rep, 2), flip(rep, 3)
    tiles, slots = weights.shape[1], anchor.shape[0]
    width = anchor.shape[2]
    part = width // 4
    w = part // chunks
    f32, highest = jnp.float32, lax.Precision.HIGHEST

    def columns(quarter, c=None):
        if c is None:
            return pl.ds(pl.multiple_of(quarter * part, 128), part)
        return pl.ds(pl.multiple_of(quarter * part + c * w, 128), w)

    def remote(src, dst, send, recv, to_rep, to_own):
        return pltpu.make_async_remote_copy(
            src_ref=src, dst_ref=dst, send_sem=send, recv_sem=recv,
            device_id=(to_rep, to_own), device_id_type=pl.DeviceIdType.MESH,
        )

    def when(*conditions):
        held = conditions[0]
        for condition in conditions[1:]:
            held = held & condition
        return pl.when(held)

    def inside(d):
        return (z + d >= 0) & (z + d <= LINE - 1)

    mine_loads = [
        pltpu.make_async_copy(
            weights.at[0, :, :, columns(quarter, c)], mine.at[c, j], mine_sem.at[c, j]
        )
        for j, quarter in ((1, chip_peer), (0, rep))
        for c in range(chunks)
    ]
    emb_loads = [
        pltpu.make_async_copy(emb_weights.at[0], emb_w, local_sem.at[0]),
        pltpu.make_async_copy(emb_anchor, emb_a, local_sem.at[1]),
        pltpu.make_async_copy(sketch, sketch_v, local_sem.at[2]),
    ]
    part_loads = [
        pltpu.make_async_copy(anchor.at[:, :, columns(rep)], anchor_part, local_sem.at[3]),
        pltpu.make_async_copy(momentum.at[:, :, columns(rep)], momentum_part, local_sem.at[4]),
    ]
    late_loads = [
        pltpu.make_async_copy(anchor, anchor_all, local_sem.at[5]),
        pltpu.make_async_copy(momentum, new_momentum, local_sem.at[6]),
        pltpu.make_async_copy(emb_momentum, emb_m, local_sem.at[7]),
    ]
    for copy in emb_loads + mine_loads + part_loads:
        copy.start()

    barrier = pltpu.get_barrier_semaphore()
    peers = [(core_peer, own), (chip_peer, own)]
    peers += [(rep, flip(own, k)) for k in range(1, across)]
    peers += [(rep, flip(own, k * across)) for k in range(1, LINE)]
    for peer in peers:
        pl.semaphore_signal(barrier, inc=1, device_id=peer, device_id_type=pl.DeviceIdType.MESH)

    for copy in emb_loads:
        copy.wait()
    diff[...] = emb_a[...] - emb_w[...]
    sketched = jnp.zeros(sketch_own.shape, f32)
    for q in range(4):
        at = slice(q * part, (q + 1) * part)
        sketched = sketched + lax.dot_general(
            sketch_v[:, at], diff[:, at], (((1,), (1,)), ((), ())),
            precision=highest, preferred_element_type=f32,
        )
    sketch_own[...] = sketched
    pl.semaphore_wait(barrier, len(peers))

    core_copies = [
        remote(
            weights.at[0, :, :, columns(quarter, c)], core_in.at[c, j],
            core_send.at[c, j], core_recv.at[c, j], core_peer, own,
        )
        for j, quarter in ((1, far_peer), (0, core_peer))
        for c in range(chunks)
    ]
    sketch_copies = [
        remote(sketch_own, sketch_core, emb_send.at[0], emb_recv.at[0], core_peer, own),
        remote(sketch_half, sketch_chip, emb_send.at[1], emb_recv.at[1], chip_peer, own),
    ]
    for copy in core_copies[:chunks] + sketch_copies[:1] + core_copies[chunks:]:
        copy.start()

    def held_copy(d, k):
        return remote(
            held_out.at[z + d, k - 1], held_in[d].at[pl.ds(k * per_pair, per_pair)],
            held_send.at[d + LINE - 1, k], held_recv.at[d + LINE - 1, k], rep, flip(own, k),
        )

    def held_fill(d, k):
        block = flip(own, k) + d * across

        def fill(p, carry):
            slot = owner_pick[block * per_pair + p]
            a = anchor_part[slot]
            value = a - OUTER_RATE * (FIXED * a + SQUARED * momentum_part[slot])
            if k:
                held_out[z + d, k - 1, p] = value
            else:
                held_in[d][p] = value
            return carry

        lax.fori_loop(0, per_pair, fill, 0)

    def held_start(d):
        if d == held_order[0]:
            for copy in part_loads:
                copy.wait()

        @when(inside(d))
        def _():
            for k in range(1, across):
                held_fill(d, k)
                held_copy(d, k).start()
            held_fill(d, 0)

    chip_copies = [
        remote(chip_out.at[c], chip_in.at[c], chip_send.at[c], chip_recv.at[c], chip_peer, own)
        for c in range(chunks)
    ]

    def half_sum(c):
        mine_loads[c].wait()
        core_copies[c].wait_recv()
        chip_out[c] = mine[c, 1] + core_in[c, 1]
        chip_copies[c].start()

    def sketch_sum():
        sketch_copies[0].wait_recv()
        sketch_half[...] = sketch_own[...] + sketch_core[...]
        sketch_copies[1].start()

    def late_start():
        for copy in late_loads:
            copy.start()

    turn_rows, line_width = rank // across, 2 * part // LINE

    def emb_core():
        return remote(f_own.at[1 - core], f_core, emb_send.at[2], emb_recv.at[2], core_peer, own)

    def emb_turn(k):
        return remote(
            f_turn.at[flip(y, k)], f_turn_in.at[k], f_turn_send.at[k], f_turn_recv.at[k],
            rep, flip(own, k),
        )

    def emb_line(k):
        return remote(
            f_line.at[flip(z, k)], f_line_in.at[k], f_line_send.at[k], f_line_recv.at[k],
            rep, flip(own, k * across),
        )

    def emb_chip():
        return remote(f_chip, f_chip_in, emb_send.at[3], emb_recv.at[3], chip_peer, own)

    def back_line(k):
        here = f_all.at[core, y, z]
        return remote(here, here, g_line_send.at[k], g_line_recv.at[k], rep, flip(own, k * across))

    def back_turn(k):
        here = f_all.at[core, y]
        return remote(here, here, g_turn_send.at[k], g_turn_recv.at[k], rep, flip(own, k))

    def back_core():
        here = f_all.at[core]
        return remote(here, here, emb_send.at[4], emb_recv.at[4], core_peer, own)

    def embed_step(n):
        (emb_0, emb_1, emb_2, emb_3, emb_4, emb_5, emb_6, emb_7)[n]()

    def emb_0():
        sketch_copies[1].wait_recv()
        mean_sketch = (sketch_half[...] + sketch_chip[...]) * 0.25
        basis = jnp.dot(inv_root[...], mean_sketch, precision=highest, preferred_element_type=f32)
        basis_ref[...] = basis
        for q in range(4):
            f_own[q % 2, :, (q // 2) * part : (q // 2 + 1) * part] = jnp.dot(
                basis, diff[:, q * part : (q + 1) * part],
                precision=highest, preferred_element_type=f32,
            )
        emb_core().start()

    def emb_1():
        emb_core().wait_recv()
        for b in range(across):
            rows = slice(b * turn_rows, (b + 1) * turn_rows)
            f_turn[b] = f_own[core, rows] + f_core[rows]
        for k in range(1, across):
            emb_turn(k).start()

    def emb_2():
        for k in range(1, across):
            emb_turn(k).wait_recv()
        total = f_turn[y]
        for k in range(1, across):
            total = total + f_turn_in[k]
        for a in range(LINE):
            f_line[a] = total[:, a * line_width : (a + 1) * line_width]
        for k in range(1, LINE):
            emb_line(k).start()

    def emb_3():
        for k in range(1, LINE):
            emb_line(k).wait_recv()
        total = f_line[z]
        for k in range(1, LINE):
            total = total + f_line_in[k]
        f_chip[...] = total
        emb_chip().start()

    def emb_4():
        emb_chip().wait_recv()
        f_all[core, y, z] = (f_chip[...] + f_chip_in[...]) * 0.25
        for k in range(1, LINE):
            back_line(k).start()

    def emb_5():
        for k in range(1, LINE):
            back_line(k).wait_recv()
        for k in range(1, across):
            back_turn(k).start()

    def emb_6():
        for k in range(1, across):
            back_turn(k).wait_recv()
        back_core().start()

    def emb_7():
        late_loads[2].wait()
        back_core().wait_recv()
        for h in range(2):
            for b in range(across):
                for a in range(LINE):
                    quarter = h + 2 * ((a * line_width) // part)
                    at = quarter * part + (a * line_width) % part
                    f_flat[b * turn_rows : (b + 1) * turn_rows, at : at + line_width] = f_all[h, b, a]
        for q in range(4):
            at = slice(q * part, (q + 1) * part)
            approx = lax.dot_general(
                basis_ref[...], f_flat[:, at], (((0,), (0,)), ((), ())),
                precision=highest, preferred_element_type=f32,
            )
            moved = OUTER_MOMENTUM * emb_m[:, at] + approx
            new_emb_momentum[:, at] = moved
            new_embedding[:, at] = emb_a[:, at] - OUTER_RATE * (approx + OUTER_MOMENTUM * moved)

    def line_copy(c, d):
        step = 1 if d > 0 else -1
        return remote(
            line[c][d - step], line[c][d], line_send.at[c, d + LINE - 1],
            line_recv.at[c, d + LINE - 1], rep, own - step * across,
        )

    def line_sends(d):
        step = 1 if d > 0 else -1
        return (z - step >= 0) & (z - step <= LINE - 1) & inside(d - step)

    def rows_of(d, k):
        return pl.ds((flip(own, k) + d * across) * per_pair, per_pair)

    def turn_copy(c, d, k, sending):
        return remote(
            turned.at[c, z + d, k - 1], gathered[c].at[rep, rows_of(d, 0 if sending else k)],
            turn_send.at[c, d + LINE - 1, k], turn_recv.at[c, d + LINE - 1, k], rep, flip(own, k),
        )

    def item_copy(c, d, k, kind):
        at = (c, d + LINE - 1, k)
        if kind == "pass":
            there = gathered[c].at[chip_peer, rows_of(d, k)]
            return remote(there, there, pass_send.at[at], pass_recv.at[at], core_peer, own)
        here = gathered[c].at[rep, rows_of(d, k)]
        if kind == "cross":
            return remote(here, here, cross_send.at[at], cross_recv.at[at], chip_peer, own)
        return remote(here, here, near_send.at[at], near_recv.at[at], core_peer, own)

    def choose(c, d, k):
        block = (k * LINE + z + d) * per_pair
        first = (own + d * across) * per_pair

        def fill(p, carry):
            value = line[c][d][pick[block + p]]
            if k:
                turned[c, z + d, k - 1, p] = value
            else:
                gathered[c][rep, first + p] = value
            return carry

        lax.fori_loop(0, per_pair, fill, 0)

    def spread(c, d):
        for k in range(1, across):
            choose(c, d, k)
            turn_copy(c, d, k, True).start()
        choose(c, d, 0)
        item_copy(c, d, 0, "cross").start()
        item_copy(c, d, 0, "near").start()

    def mean_ready(c):
        mine_loads[chunks + c].wait()
        core_copies[chunks + c].wait_recv()
        chip_copies[c].wait_recv()
        line[c][0][...] = (mine[c, 0] + core_in[c, 0] + chip_in[c]) * 0.25
        for d in (1, -1):
            @when(line_sends(d))
            def _(d=d):
                line_copy(c, d).start()
        spread(c, 0)

    def line_arrived(c, d):
        step = 1 if d > 0 else -1

        @when(inside(d))
        def _():
            line_copy(c, d).wait_recv()
            if abs(d) < LINE - 1:
                @when(line_sends(d + step))
                def _():
                    line_copy(c, d + step).start()
            spread(c, d)

    def turn_arrived(c, d):
        @when(inside(d))
        def _():
            for k in range(1, across):
                turn_copy(c, d, k, False).wait_recv()
                item_copy(c, d, k, "cross").start()
                item_copy(c, d, k, "near").start()

    def pass_on(c, d):
        @when(inside(d))
        def _():
            for k in range(across):
                item_copy(c, d, k, "cross").wait_recv()
                item_copy(c, d, k, "pass").start()

    def base_rows(piece):
        if piece == base_order[0]:
            late_loads[0].wait()
            late_loads[1].wait()
        first = piece * (slots // chunks)
        count = slots - first if piece == chunks - 1 else slots // chunks

        def body(s, carry):
            for q in range(4):
                at = pl.ds(q * part, part)
                new_momentum[s, :, at] = OUTER_MOMENTUM * new_momentum[s, :, at] + anchor_all[s, :, at]
            return carry

        lax.fori_loop(first, first + count, body, 0)

    def advance(c):
        for d in range(1 - LINE, LINE):
            @when(inside(d))
            def _(d=d):
                for k in range(across):
                    item_copy(c, d, k, "near").wait_recv()
                    item_copy(c, d, k, "pass").wait_recv()

        def body(s, carry):
            found = owner_read[s]
            row = jnp.maximum(found - 1, 0)
            kept = jnp.full((new_momentum.shape[1], w), found, jnp.int32) > 0
            for q in range(4):
                at = pl.ds(q * part + c * w, w)
                new_momentum[s, :, at] = jnp.where(
                    kept, new_momentum[s, :, at] - gathered[c][q, row], 0.0
                )
            return carry

        lax.fori_loop(0, slots, body, 0)

    def merge_copy(d, c):
        step = 1 if d > 0 else -1
        target = (below if d > 0 else above)[d - step]
        at = (c, d + LINE - 1)
        return remote(
            merged[d].at[c], target.at[c], merge_send.at[at], merge_recv.at[at], rep, own + step * across
        )

    def merge_tiles(d, c, store, incoming):
        first = (own + d * across) * tiles
        at = pl.ds(c * w, w)

        def body(t, carry):
            key = merge[first + t]
            value = held_in[d][jnp.maximum(key, 0), :, at]
            if incoming is not None:
                keys = jnp.full((value.shape[0], w), key, jnp.int32)
                value = jnp.where(keys >= 0, value, incoming(t, keys))
            store(t, value)
            return carry

        lax.fori_loop(0, tiles, body, 0)

    def merge_step(c, d):
        step = 1 if d > 0 else -1
        source = (below if d > 0 else above).get(d)
        has_source = (z >= 1) if d > 0 else (z <= LINE - 2)

        def store(t, value):
            merged[d][c, t] = value

        def landed():
            if merge_order[d] == c:
                for k in range(1, across):
                    held_copy(d, k).wait_recv()

        @when(inside(d), jnp.logical_not(has_source))
        def _():
            landed()
            merge_tiles(d, c, store, None)
            merge_copy(d, c).start()

        if source is not None:
            @when(inside(d), has_source)
            def _():
                landed()
                merge_copy(d + step, c).wait_recv()
                merge_tiles(d, c, store, lambda t, keys: source[c, t])
                merge_copy(d, c).start()

    def fresh_copy(c, kind):
        at = {"cross": 0, "near": 1, "pass": 2}[kind]
        here = new_weights.at[:, :, columns(chip_peer if kind == "pass" else rep, c)]
        return remote(
            here, here, fresh_send.at[at, c], fresh_recv.at[at, c],
            chip_peer if kind == "cross" else core_peer, own,
        )

    def renew(c):
        @when(z >= 1)
        def _():
            merge_copy(1, c).wait_recv()

        @when(z <= LINE - 2)
        def _():
            merge_copy(-1, c).wait_recv()

        if renew_order[0] == c:
            for k in range(1, across):
                held_copy(0, k).wait_recv()

        def incoming(t, keys):
            return jnp.where(keys == -1, below[0][c, t], above[0][c, t])

        def store(t, value):
            new_weights[t, :, columns(rep, c)] = value + (OUTER_RATE * FIXED) * line[c][0][t]

        merge_tiles(0, c, store, incoming)
        fresh_copy(c, "cross").start()
        fresh_copy(c, "near").start()

    def fresh_pass(c):
        fresh_copy(c, "cross").wait_recv()
        fresh_copy(c, "pass").start()

    steps = {
        HALF: half_sum, SKETCH: sketch_sum, HELD: held_start, LATE: late_start, MEAN: mean_ready,
        LINED: line_arrived, TURNED: turn_arrived, PASS: pass_on, BASE: base_rows, ADVANCE: advance,
        MERGE: merge_step, RENEW: renew, FRESH: fresh_pass, EMBED: embed_step,
    }
    for step, *arguments in ORDER:
        steps[step](*arguments)

    for c in range(chunks):
        fresh_copy(c, "near").wait_recv()
        fresh_copy(c, "pass").wait_recv()
    for copy in core_copies + chip_copies + sketch_copies:
        copy.wait_send()
    for k in range(1, across):
        emb_turn(k).wait_send()
        back_turn(k).wait_send()
    for k in range(1, LINE):
        emb_line(k).wait_send()
        back_line(k).wait_send()
    for copy in (emb_core(), emb_chip(), back_core()):
        copy.wait_send()
    for c in range(chunks):
        for kind in ("cross", "near", "pass"):
            fresh_copy(c, kind).wait_send()
    for d in range(1 - LINE, LINE):
        @when(inside(d))
        def _(d=d):
            for k in range(1, across):
                held_copy(d, k).wait_send()
            for c in range(chunks):
                for k in range(across):
                    if k:
                        turn_copy(c, d, k, True).wait_send()
                    for kind in ("cross", "near", "pass"):
                        item_copy(c, d, k, kind).wait_send()
                if d:
                    merge_copy(d, c).wait_send()

        if d:
            @when(line_sends(d))
            def _(d=d):
                for c in range(chunks):
                    line_copy(c, d).wait_send()


def step_call(weights, anchor, momentum, embed, tables, own_count, per_pair):
    tiles, rows, width = weights.shape[1:]
    slots, part = anchor.shape[0], width // 4
    across, chunks = own_count // LINE, CHUNKS
    w, span = part // chunks, 2 * LINE - 1
    pairs = own_count * per_pair
    f32, dma = jnp.float32, pltpu.SemaphoreType.DMA
    emb_rows, rank = embed[1].shape[0], embed[3].shape[0]
    vmem = lambda *shape: pltpu.VMEM(shape, f32)
    turn_rows, line_width = rank // across, 2 * part // LINE
    scratch = [
        dma((8,)), dma((chunks, 2)),
        vmem(slots, rows, part), vmem(slots, rows, part), vmem(slots, rows, width),
        vmem(chunks, 2, tiles, rows, w), vmem(chunks, 2, tiles, rows, w),
        vmem(chunks, tiles, rows, w), vmem(chunks, tiles, rows, w),
        dma((chunks, 2)), dma((chunks, 2)), dma((chunks,)), dma((chunks,)),
    ]
    scratch += [vmem(tiles, rows, w) for _ in range(chunks * span)]
    scratch += [dma((chunks, span)), dma((chunks, span))]
    scratch += [vmem(chunks, LINE, across - 1, per_pair, rows, w)]
    scratch += [dma((chunks, span, across)), dma((chunks, span, across))]
    scratch += [vmem(4, pairs, rows, w) for _ in range(chunks)]
    scratch += [dma((chunks, span, across)) for _ in range(6)]
    scratch += [vmem(LINE, across - 1, per_pair, rows, part)]
    scratch += [vmem(across * per_pair, rows, part) for _ in range(span)]
    scratch += [dma((span, across)), dma((span, across))]
    scratch += [vmem(chunks, tiles, rows, w) for _ in range(span - 1)]
    scratch += [vmem(chunks, tiles, rows, w) for _ in range(2 * (LINE - 1))]
    scratch += [dma((chunks, span)), dma((chunks, span)), dma((3, chunks)), dma((3, chunks))]
    scratch += [
        vmem(emb_rows, width), vmem(emb_rows, width), vmem(emb_rows, width), vmem(rank, width),
        vmem(emb_rows, width),
    ]
    scratch += [vmem(rank, emb_rows) for _ in range(5)]
    scratch += [
        vmem(2, rank, 2 * part), vmem(rank, 2 * part),
        vmem(across, turn_rows, 2 * part), vmem(across, turn_rows, 2 * part),
        vmem(LINE, turn_rows, line_width), vmem(LINE, turn_rows, line_width),
        vmem(turn_rows, line_width), vmem(turn_rows, line_width),
        vmem(2, across, LINE, turn_rows, line_width), vmem(rank, width),
        dma((5,)), dma((5,)), dma((across,)), dma((across,)), dma((LINE,)), dma((LINE,)),
        dma((across,)), dma((across,)), dma((LINE,)), dma((LINE,)),
    ]
    return pl.pallas_call(
        functools.partial(step_kernel, own_count, per_pair, rank),
        out_shape=(
            pltpu.VMEM((tiles, rows, width), f32),
            pltpu.VMEM((slots, rows, width), f32),
            pltpu.VMEM((emb_rows, width), f32),
            pltpu.VMEM((emb_rows, width), f32),
        ),
        in_specs=[pl.BlockSpec(memory_space=pltpu.SMEM)] * 4 + [pl.BlockSpec(memory_space=pltpu.HBM)] * 7
        + [pl.BlockSpec(memory_space=pltpu.VMEM)],
        out_specs=(pl.BlockSpec(memory_space=pltpu.VMEM),) * 4,
        scratch_shapes=scratch,
        compiler_params=pltpu.CompilerParams(
            collective_id=0, has_side_effects=True, vmem_limit_bytes=50 * 1024 * 1024
        ),
        cost_estimate=pl.CostEstimate(flops=20000000, bytes_accessed=300000000, transcendentals=0),
    )(*tables, weights, anchor, momentum, *embed)


def local(
    weights, anchor, momentum, owner, emb_weights, emb_anchor, emb_momentum, sketch, inv_root
):
    own_count = lax.axis_size("own")
    own_index = lax.axis_index("own")
    tiles_dev = weights.shape[1]
    half_tiles = min(tiles_dev // 2, own_count)
    hot_count = max(own_count // 4, 1)
    per_pair = (tiles_dev - half_tiles) // hot_count + 1
    tables = owner_tables(owner, tiles_dev, per_pair, anchor.shape[0], own_index, own_count)
    embed = (emb_weights, emb_anchor, emb_momentum, sketch, inv_root)
    return step_call(weights, anchor, momentum, embed, tables, own_count, per_pair)


def solution(mesh):
    placed = (
        P("rep", "own", None, None),
        P("own", None, None),
        P("own", None, None),
        P(),
        P("rep", "own", None),
        P("own", None),
        P("own", None),
        P(),
        P(),
    )
    return jax.shard_map(
        local,
        mesh=mesh,
        in_specs=placed,
        out_specs=(P("own", None, None), P("own", None, None), P("own", None), P("own", None)),
        check_vma=False,
    )
```

```python
import functools

import jax
import jax.numpy as jnp
from jax import lax
from jax.experimental import pallas as pl
from jax.experimental.pallas import tpu as pltpu
from jax.sharding import PartitionSpec as P

OUTER_RATE = 0.7
OUTER_MOMENTUM = 0.9
FIXED = 1.0 + OUTER_MOMENTUM
SQUARED = OUTER_MOMENTUM * OUTER_MOMENTUM
LINE = 4
CHUNKS = 4
(
    HALF, SKETCH, HELD, LATE, MEAN, LINED, TURNED, PASS, BASE,
    ADVANCE, MERGE, RENEW, FRESH, EMBED,
) = range(14)
ORDER = (
    (HELD, 3), (HELD, -2), (HALF, 1), (HELD, 1), (HALF, 0), (HELD, 2), (HELD, -3), (HALF, 2), (MEAN, 1),
    (MEAN, 0), (SKETCH,), (MERGE, 0, -3), (MERGE, 0, 3), (MEAN, 2), (LINED, 1, 1), (HALF, 3), (LINED, 1, -1),
    (LATE,), (MERGE, 3, 3), (LINED, 0, 1), (LINED, 0, -1), (EMBED, 0), (EMBED, 1), (MERGE, 2, -3),
    (TURNED, 1, -1), (TURNED, 1, 0), (LINED, 2, -1), (LINED, 2, 1), (LINED, 1, -2), (BASE, 0), (TURNED, 2, 0),
    (MERGE, 2, 3), (MEAN, 3), (BASE, 1), (EMBED, 2), (TURNED, 0, 1), (MERGE, 1, 3), (LINED, 0, 2),
    (MERGE, 0, -2), (LINED, 2, -2), (LINED, 0, -2), (MERGE, 3, -3), (MERGE, 0, 2), (LINED, 2, 2),
    (LINED, 1, -3), (TURNED, 0, -1), (TURNED, 2, -2), (BASE, 2), (LINED, 3, -1), (MERGE, 1, -3),
    (TURNED, 1, 1), (LINED, 1, 2), (TURNED, 1, -3), (LINED, 3, 1), (PASS, 2, 0), (HELD, -1), (MERGE, 2, -2),
    (EMBED, 3), (BASE, 3), (MERGE, 2, 2), (PASS, 1, 0), (PASS, 0, 1), (MERGE, 1, -2), (TURNED, 0, -2),
    (TURNED, 2, 1), (TURNED, 0, 0), (LINED, 2, -3), (TURNED, 3, 0), (LINED, 0, 3), (TURNED, 1, -2),
    (LINED, 0, -3), (LINED, 3, -2), (TURNED, 3, 1), (MERGE, 1, 2), (EMBED, 4), (LINED, 2, 3), (TURNED, 2, -3),
    (PASS, 2, -2), (MERGE, 0, -1), (MERGE, 0, 1), (HELD, 0), (TURNED, 0, 3), (LINED, 1, 3), (TURNED, 1, 2),
    (PASS, 1, 1), (MERGE, 3, -2), (TURNED, 2, 2), (TURNED, 0, -3), (TURNED, 2, -1), (LINED, 3, 2),
    (MERGE, 2, -1), (TURNED, 2, 3), (MERGE, 1, -1), (TURNED, 0, 2), (LINED, 3, -3), (MERGE, 2, 1),
    (MERGE, 3, 2), (PASS, 0, 0), (PASS, 0, 3), (TURNED, 1, 3), (PASS, 2, -3), (PASS, 1, -2), (EMBED, 5),
    (TURNED, 3, -2), (TURNED, 3, 2), (PASS, 0, -2), (MERGE, 1, 1), (PASS, 0, -1), (RENEW, 0), (TURNED, 3, -3),
    (PASS, 2, 1), (MERGE, 3, -1), (EMBED, 6), (PASS, 2, 2), (TURNED, 3, -1), (PASS, 0, -3), (LINED, 3, 3),
    (PASS, 1, 3), (PASS, 2, -1), (PASS, 3, 1), (PASS, 2, 3), (PASS, 0, 2), (PASS, 3, -2), (RENEW, 2),
    (PASS, 1, 2), (MERGE, 3, 1), (ADVANCE, 2), (PASS, 3, -3), (FRESH, 0), (TURNED, 3, 3), (PASS, 1, -1),
    (RENEW, 1), (PASS, 3, -1), (PASS, 3, 2), (EMBED, 7), (PASS, 1, -3), (PASS, 3, 3), (RENEW, 3),
    (ADVANCE, 0), (PASS, 3, 0), (ADVANCE, 3), (FRESH, 1), (FRESH, 2), (FRESH, 3), (ADVANCE, 1),
)


def fill_tables(owner, table, own_index, own_count, tiles_dev, per_pair, slots):
    across_bits, tile_bits = (own_count // LINE).bit_length() - 1, tiles_dev.bit_length() - 1
    count, step = owner.shape[1], min(256, owner.shape[1])
    lanes = table.shape[1]
    owner_row = owner[...]
    my_z, my_y = own_index // (own_count // LINE), own_index % (own_count // LINE)
    y_mask = (1 << across_bits) - 1
    row_ids = lax.broadcasted_iota(jnp.int32, (step, count), 1)
    out_ids = lax.broadcasted_iota(jnp.int32, (step, lanes), 1)
    totals = None
    for first in range(0, count, step):
        ids = lax.broadcasted_iota(jnp.int32, (step, count), 0) + first
        column = jnp.sum(jnp.where(ids == row_ids, owner_row, 0), axis=1, keepdims=True)
        before = (column == owner_row) & (row_ids < ids)
        near = before & ((row_ids >> tile_bits) == (ids >> tile_bits))
        slot_rank = jnp.sum(before.astype(jnp.int32), axis=1, keepdims=True)
        pair_rank = jnp.sum(near.astype(jnp.int32), axis=1, keepdims=True)
        tile = lax.broadcasted_iota(jnp.int32, (step, 1), 0) + first
        block = tile >> tile_bits
        owner_z, turn = column >> across_bits, (column & y_mask) ^ my_y
        back_key = block * per_pair + pair_rank
        held = column == own_index
        pick_key = jnp.where(
            (owner_z == my_z) & ((block & y_mask) == my_y),
            (turn * LINE + (block >> across_bits)) * per_pair + pair_rank,
            -1,
        )
        merge = jnp.where(
            owner_z == my_z, turn * per_pair + pair_rank, jnp.where(owner_z < my_z, -1, -2)
        )
        pairs = (
            (pick_key, tile & (tiles_dev - 1)),
            (tile, merge),
            (jnp.where(held, slot_rank, -1), back_key + 1),
            (jnp.where(held, back_key, -1), slot_rank),
        )
        found = [
            jnp.sum(jnp.where(key == out_ids, value, 0), axis=0, keepdims=True)
            for key, value in pairs
        ]
        totals = found if totals is None else [a + b for a, b in zip(totals, found)]
    across = own_count // LINE
    limits = (tiles_dev - 1, across * per_pair - 1, own_count * per_pair, slots - 1)
    for n, (total, limit) in enumerate(zip(totals, limits)):
        table[n : n + 1, :] = jnp.minimum(total, limit)


def flip(index, bits):
    out, unit = index, 1
    while unit <= bits:
        if bits & unit:
            out = out + unit - 2 * unit * ((index // unit) % 2)
        unit *= 2
    return out


def step_kernel(
    own_count, per_pair, rank,
    owner, weights, anchor, momentum,
    emb_weights, emb_anchor, emb_momentum, sketch, inv_root,
    new_weights, new_momentum, new_embedding, new_emb_momentum,
    *scratch,
):
    across, chunks = own_count // LINE, CHUNKS
    take = iter(scratch)
    local_sem, mine_sem = next(take), next(take)
    table, table_read = next(take), next(take)
    held_order = [at[1] for at in ORDER if at[0] == HELD]
    merge_order = {at[2]: at[1] for at in reversed(ORDER) if at[0] == MERGE}
    renew_order = [at[1] for at in ORDER if at[0] == RENEW]
    base_order = [at[1] for at in ORDER if at[0] == BASE]
    anchor_part, momentum_part, anchor_all = next(take), next(take), next(take)
    mine, core_in, chip_out, chip_in = next(take), next(take), next(take), next(take)
    core_send, core_recv, chip_send, chip_recv = next(take), next(take), next(take), next(take)
    line = [{d: next(take) for d in range(1 - LINE, LINE)} for _ in range(chunks)]
    line_send, line_recv = next(take), next(take)
    turned = next(take)
    turn_send, turn_recv = next(take), next(take)
    gathered = [next(take) for _ in range(chunks)]
    cross_send, cross_recv, near_send, near_recv, pass_send, pass_recv = (next(take) for _ in range(6))
    held_out = next(take)
    held_in = {d: next(take) for d in range(1 - LINE, LINE)}
    held_send, held_recv = next(take), next(take)
    merged = {d: next(take) for d in range(1 - LINE, LINE) if d}
    below = {d: next(take) for d in range(LINE - 1)}
    above = {-d: next(take) for d in range(LINE - 1)}
    merge_send, merge_recv = next(take), next(take)
    fresh_send, fresh_recv = next(take), next(take)
    emb_w, emb_a, emb_m, sketch_v = next(take), next(take), next(take), next(take)
    diff, sketch_own, sketch_half, sketch_core, sketch_chip, basis_ref = (next(take) for _ in range(6))
    f_own, f_core, f_turn, f_turn_in, f_line, f_line_in, f_chip, f_chip_in, f_all, f_flat = (
        next(take) for _ in range(10)
    )
    emb_send, emb_recv, f_turn_send, f_turn_recv, f_line_send, f_line_recv = (
        next(take) for _ in range(6)
    )
    g_turn_send, g_turn_recv, g_line_send, g_line_recv = (next(take) for _ in range(4))

    rep = lax.axis_index("rep")
    own = lax.axis_index("own")
    core = rep % 2
    z, y = own // across, own % across
    core_peer, chip_peer, far_peer = flip(rep, 1), flip(rep, 2), flip(rep, 3)
    tiles, slots = weights.shape[1], anchor.shape[0]
    width = anchor.shape[2]
    part = width // 4
    w = part // chunks
    f32, highest = jnp.float32, lax.Precision.HIGHEST

    def columns(quarter, c=None):
        if c is None:
            return pl.ds(pl.multiple_of(quarter * part, 128), part)
        return pl.ds(pl.multiple_of(quarter * part + c * w, 128), w)

    def remote(src, dst, send, recv, to_rep, to_own):
        return pltpu.make_async_remote_copy(
            src_ref=src, dst_ref=dst, send_sem=send, recv_sem=recv,
            device_id=(to_rep, to_own), device_id_type=pl.DeviceIdType.MESH,
        )

    def when(*conditions):
        held = conditions[0]
        for condition in conditions[1:]:
            held = held & condition
        return pl.when(held)

    def inside(d):
        return (z + d >= 0) & (z + d <= LINE - 1)

    mine_loads = [
        pltpu.make_async_copy(
            weights.at[0, :, :, columns(quarter, c)], mine.at[c, j], mine_sem.at[c, j]
        )
        for j, quarter in ((1, chip_peer), (0, rep))
        for c in range(chunks)
    ]
    emb_loads = [
        pltpu.make_async_copy(emb_weights.at[0], emb_w, local_sem.at[0]),
        pltpu.make_async_copy(emb_anchor, emb_a, local_sem.at[1]),
        pltpu.make_async_copy(sketch, sketch_v, local_sem.at[2]),
    ]
    part_loads = [
        pltpu.make_async_copy(anchor.at[:, :, columns(rep)], anchor_part, local_sem.at[3]),
        pltpu.make_async_copy(momentum.at[:, :, columns(rep)], momentum_part, local_sem.at[4]),
    ]
    late_loads = [
        pltpu.make_async_copy(anchor, anchor_all, local_sem.at[5]),
        pltpu.make_async_copy(momentum, new_momentum, local_sem.at[6]),
        pltpu.make_async_copy(emb_momentum, emb_m, local_sem.at[7]),
    ]
    for copy in emb_loads + mine_loads + part_loads:
        copy.start()

    barrier = pltpu.get_barrier_semaphore()
    peers = [(core_peer, own), (chip_peer, own)]
    peers += [(rep, flip(own, k)) for k in range(1, across)]
    peers += [(rep, flip(own, k * across)) for k in range(1, LINE)]
    for peer in peers:
        pl.semaphore_signal(barrier, inc=1, device_id=peer, device_id_type=pl.DeviceIdType.MESH)

    fill_tables(owner, table, own, own_count, tiles, per_pair, slots)
    table_load = pltpu.make_async_copy(table, table_read, local_sem.at[8])
    table_load.start()
    for copy in emb_loads:
        copy.wait()
    diff[...] = emb_a[...] - emb_w[...]
    sketched = jnp.zeros(sketch_own.shape, f32)
    for q in range(4):
        at = slice(q * part, (q + 1) * part)
        sketched = sketched + lax.dot_general(
            sketch_v[:, at], diff[:, at], (((1,), (1,)), ((), ())),
            precision=highest, preferred_element_type=f32,
        )
    sketch_own[...] = sketched
    table_load.wait()
    pl.semaphore_wait(barrier, len(peers))

    core_copies = [
        remote(
            weights.at[0, :, :, columns(quarter, c)], core_in.at[c, j],
            core_send.at[c, j], core_recv.at[c, j], core_peer, own,
        )
        for j, quarter in ((1, far_peer), (0, core_peer))
        for c in range(chunks)
    ]
    sketch_copies = [
        remote(sketch_own, sketch_core, emb_send.at[0], emb_recv.at[0], core_peer, own),
        remote(sketch_half, sketch_chip, emb_send.at[1], emb_recv.at[1], chip_peer, own),
    ]
    for copy in core_copies[:chunks] + sketch_copies[:1] + core_copies[chunks:]:
        copy.start()

    def held_copy(d, k):
        return remote(
            held_out.at[z + d, k - 1], held_in[d].at[pl.ds(k * per_pair, per_pair)],
            held_send.at[d + LINE - 1, k], held_recv.at[d + LINE - 1, k], rep, flip(own, k),
        )

    def held_fill(d, k):
        block = flip(own, k) + d * across

        def fill(p, carry):
            slot = table_read[3, block * per_pair + p]
            a = anchor_part[slot]
            value = a - OUTER_RATE * (FIXED * a + SQUARED * momentum_part[slot])
            if k:
                held_out[z + d, k - 1, p] = value
            else:
                held_in[d][p] = value
            return carry

        lax.fori_loop(0, per_pair, fill, 0)

    def held_start(d):
        if d == held_order[0]:
            for copy in part_loads:
                copy.wait()

        @when(inside(d))
        def _():
            for k in range(1, across):
                held_fill(d, k)
                held_copy(d, k).start()
            held_fill(d, 0)

    chip_copies = [
        remote(chip_out.at[c], chip_in.at[c], chip_send.at[c], chip_recv.at[c], chip_peer, own)
        for c in range(chunks)
    ]

    def half_sum(c):
        mine_loads[c].wait()
        core_copies[c].wait_recv()
        chip_out[c] = mine[c, 1] + core_in[c, 1]
        chip_copies[c].start()

    def sketch_sum():
        sketch_copies[0].wait_recv()
        sketch_half[...] = sketch_own[...] + sketch_core[...]
        sketch_copies[1].start()

    def late_start():
        for copy in late_loads:
            copy.start()

    turn_rows, line_width = rank // across, 2 * part // LINE

    def emb_core():
        return remote(f_own.at[1 - core], f_core, emb_send.at[2], emb_recv.at[2], core_peer, own)

    def emb_turn(k):
        return remote(
            f_turn.at[flip(y, k)], f_turn_in.at[k], f_turn_send.at[k], f_turn_recv.at[k],
            rep, flip(own, k),
        )

    def emb_line(k):
        return remote(
            f_line.at[flip(z, k)], f_line_in.at[k], f_line_send.at[k], f_line_recv.at[k],
            rep, flip(own, k * across),
        )

    def emb_chip():
        return remote(f_chip, f_chip_in, emb_send.at[3], emb_recv.at[3], chip_peer, own)

    def back_line(k):
        here = f_all.at[core, y, z]
        return remote(here, here, g_line_send.at[k], g_line_recv.at[k], rep, flip(own, k * across))

    def back_turn(k):
        here = f_all.at[core, y]
        return remote(here, here, g_turn_send.at[k], g_turn_recv.at[k], rep, flip(own, k))

    def back_core():
        here = f_all.at[core]
        return remote(here, here, emb_send.at[4], emb_recv.at[4], core_peer, own)

    def embed_step(n):
        (emb_0, emb_1, emb_2, emb_3, emb_4, emb_5, emb_6, emb_7)[n]()

    def emb_0():
        sketch_copies[1].wait_recv()
        mean_sketch = (sketch_half[...] + sketch_chip[...]) * 0.25
        basis = jnp.dot(inv_root[...], mean_sketch, precision=highest, preferred_element_type=f32)
        basis_ref[...] = basis
        for q in range(4):
            f_own[q % 2, :, (q // 2) * part : (q // 2 + 1) * part] = jnp.dot(
                basis, diff[:, q * part : (q + 1) * part],
                precision=highest, preferred_element_type=f32,
            )
        emb_core().start()

    def emb_1():
        emb_core().wait_recv()
        for b in range(across):
            rows = slice(b * turn_rows, (b + 1) * turn_rows)
            f_turn[b] = f_own[core, rows] + f_core[rows]
        for k in range(1, across):
            emb_turn(k).start()

    def emb_2():
        for k in range(1, across):
            emb_turn(k).wait_recv()
        total = f_turn[y]
        for k in range(1, across):
            total = total + f_turn_in[k]
        for a in range(LINE):
            f_line[a] = total[:, a * line_width : (a + 1) * line_width]
        for k in range(1, LINE):
            emb_line(k).start()

    def emb_3():
        for k in range(1, LINE):
            emb_line(k).wait_recv()
        total = f_line[z]
        for k in range(1, LINE):
            total = total + f_line_in[k]
        f_chip[...] = total
        emb_chip().start()

    def emb_4():
        emb_chip().wait_recv()
        f_all[core, y, z] = (f_chip[...] + f_chip_in[...]) * 0.25
        for k in range(1, LINE):
            back_line(k).start()

    def emb_5():
        for k in range(1, LINE):
            back_line(k).wait_recv()
        for k in range(1, across):
            back_turn(k).start()

    def emb_6():
        for k in range(1, across):
            back_turn(k).wait_recv()
        back_core().start()

    def emb_7():
        late_loads[2].wait()
        back_core().wait_recv()
        for h in range(2):
            for b in range(across):
                for a in range(LINE):
                    quarter = h + 2 * ((a * line_width) // part)
                    at = quarter * part + (a * line_width) % part
                    f_flat[b * turn_rows : (b + 1) * turn_rows, at : at + line_width] = f_all[h, b, a]
        for q in range(4):
            at = slice(q * part, (q + 1) * part)
            approx = lax.dot_general(
                basis_ref[...], f_flat[:, at], (((0,), (0,)), ((), ())),
                precision=highest, preferred_element_type=f32,
            )
            moved = OUTER_MOMENTUM * emb_m[:, at] + approx
            new_emb_momentum[:, at] = moved
            new_embedding[:, at] = emb_a[:, at] - OUTER_RATE * (approx + OUTER_MOMENTUM * moved)

    def line_copy(c, d):
        step = 1 if d > 0 else -1
        return remote(
            line[c][d - step], line[c][d], line_send.at[c, d + LINE - 1],
            line_recv.at[c, d + LINE - 1], rep, own - step * across,
        )

    def line_sends(d):
        step = 1 if d > 0 else -1
        return (z - step >= 0) & (z - step <= LINE - 1) & inside(d - step)

    def rows_of(d, k):
        return pl.ds((flip(own, k) + d * across) * per_pair, per_pair)

    def turn_copy(c, d, k, sending):
        return remote(
            turned.at[c, z + d, k - 1], gathered[c].at[rep, rows_of(d, 0 if sending else k)],
            turn_send.at[c, d + LINE - 1, k], turn_recv.at[c, d + LINE - 1, k], rep, flip(own, k),
        )

    def item_copy(c, d, k, kind):
        at = (c, d + LINE - 1, k)
        if kind == "pass":
            there = gathered[c].at[chip_peer, rows_of(d, k)]
            return remote(there, there, pass_send.at[at], pass_recv.at[at], core_peer, own)
        here = gathered[c].at[rep, rows_of(d, k)]
        if kind == "cross":
            return remote(here, here, cross_send.at[at], cross_recv.at[at], chip_peer, own)
        return remote(here, here, near_send.at[at], near_recv.at[at], core_peer, own)

    def choose(c, d, k):
        block = (k * LINE + z + d) * per_pair
        first = (own + d * across) * per_pair

        def fill(p, carry):
            value = line[c][d][table_read[0, block + p]]
            if k:
                turned[c, z + d, k - 1, p] = value
            else:
                gathered[c][rep, first + p] = value
            return carry

        lax.fori_loop(0, per_pair, fill, 0)

    def spread(c, d):
        for k in range(1, across):
            choose(c, d, k)
            turn_copy(c, d, k, True).start()
        choose(c, d, 0)
        item_copy(c, d, 0, "cross").start()
        item_copy(c, d, 0, "near").start()

    def mean_ready(c):
        mine_loads[chunks + c].wait()
        core_copies[chunks + c].wait_recv()
        chip_copies[c].wait_recv()
        line[c][0][...] = (mine[c, 0] + core_in[c, 0] + chip_in[c]) * 0.25
        for d in (1, -1):
            @when(line_sends(d))
            def _(d=d):
                line_copy(c, d).start()
        spread(c, 0)

    def line_arrived(c, d):
        step = 1 if d > 0 else -1

        @when(inside(d))
        def _():
            line_copy(c, d).wait_recv()
            if abs(d) < LINE - 1:
                @when(line_sends(d + step))
                def _():
                    line_copy(c, d + step).start()
            spread(c, d)

    def turn_arrived(c, d):
        @when(inside(d))
        def _():
            for k in range(1, across):
                turn_copy(c, d, k, False).wait_recv()
                item_copy(c, d, k, "cross").start()
                item_copy(c, d, k, "near").start()

    def pass_on(c, d):
        @when(inside(d))
        def _():
            for k in range(across):
                item_copy(c, d, k, "cross").wait_recv()
                item_copy(c, d, k, "pass").start()

    def base_rows(piece):
        if piece == base_order[0]:
            late_loads[0].wait()
            late_loads[1].wait()
        first = piece * (slots // chunks)
        count = slots - first if piece == chunks - 1 else slots // chunks

        def body(s, carry):
            for q in range(4):
                at = pl.ds(q * part, part)
                new_momentum[s, :, at] = OUTER_MOMENTUM * new_momentum[s, :, at] + anchor_all[s, :, at]
            return carry

        lax.fori_loop(first, first + count, body, 0)

    def advance(c):
        for d in range(1 - LINE, LINE):
            @when(inside(d))
            def _(d=d):
                for k in range(across):
                    item_copy(c, d, k, "near").wait_recv()
                    item_copy(c, d, k, "pass").wait_recv()

        def body(s, carry):
            found = table_read[2, s]
            row = jnp.maximum(found - 1, 0)
            kept = jnp.full((new_momentum.shape[1], w), found, jnp.int32) > 0
            for q in range(4):
                at = pl.ds(q * part + c * w, w)
                new_momentum[s, :, at] = jnp.where(
                    kept, new_momentum[s, :, at] - gathered[c][q, row], 0.0
                )
            return carry

        lax.fori_loop(0, slots, body, 0)

    def merge_copy(d, c):
        step = 1 if d > 0 else -1
        target = (below if d > 0 else above)[d - step]
        at = (c, d + LINE - 1)
        return remote(
            merged[d].at[c], target.at[c], merge_send.at[at], merge_recv.at[at], rep, own + step * across
        )

    def merge_tiles(d, c, store, incoming):
        first = (own + d * across) * tiles
        at = pl.ds(c * w, w)

        def body(t, carry):
            key = table_read[1, first + t]
            value = held_in[d][jnp.maximum(key, 0), :, at]
            if incoming is not None:
                keys = jnp.full((value.shape[0], w), key, jnp.int32)
                value = jnp.where(keys >= 0, value, incoming(t, keys))
            store(t, value)
            return carry

        lax.fori_loop(0, tiles, body, 0)

    def merge_step(c, d):
        step = 1 if d > 0 else -1
        source = (below if d > 0 else above).get(d)
        has_source = (z >= 1) if d > 0 else (z <= LINE - 2)

        def store(t, value):
            merged[d][c, t] = value

        def landed():
            if merge_order[d] == c:
                for k in range(1, across):
                    held_copy(d, k).wait_recv()

        @when(inside(d), jnp.logical_not(has_source))
        def _():
            landed()
            merge_tiles(d, c, store, None)
            merge_copy(d, c).start()

        if source is not None:
            @when(inside(d), has_source)
            def _():
                landed()
                merge_copy(d + step, c).wait_recv()
                merge_tiles(d, c, store, lambda t, keys: source[c, t])
                merge_copy(d, c).start()

    def fresh_copy(c, kind):
        at = {"cross": 0, "near": 1, "pass": 2}[kind]
        here = new_weights.at[:, :, columns(chip_peer if kind == "pass" else rep, c)]
        return remote(
            here, here, fresh_send.at[at, c], fresh_recv.at[at, c],
            chip_peer if kind == "cross" else core_peer, own,
        )

    def renew(c):
        @when(z >= 1)
        def _():
            merge_copy(1, c).wait_recv()

        @when(z <= LINE - 2)
        def _():
            merge_copy(-1, c).wait_recv()

        if renew_order[0] == c:
            for k in range(1, across):
                held_copy(0, k).wait_recv()

        def incoming(t, keys):
            return jnp.where(keys == -1, below[0][c, t], above[0][c, t])

        def store(t, value):
            new_weights[t, :, columns(rep, c)] = value + (OUTER_RATE * FIXED) * line[c][0][t]

        merge_tiles(0, c, store, incoming)
        fresh_copy(c, "cross").start()
        fresh_copy(c, "near").start()

    def fresh_pass(c):
        fresh_copy(c, "cross").wait_recv()
        fresh_copy(c, "pass").start()

    steps = {
        HALF: half_sum, SKETCH: sketch_sum, HELD: held_start, LATE: late_start, MEAN: mean_ready,
        LINED: line_arrived, TURNED: turn_arrived, PASS: pass_on, BASE: base_rows, ADVANCE: advance,
        MERGE: merge_step, RENEW: renew, FRESH: fresh_pass, EMBED: embed_step,
    }
    for step, *arguments in ORDER:
        steps[step](*arguments)

    for c in range(chunks):
        fresh_copy(c, "near").wait_recv()
        fresh_copy(c, "pass").wait_recv()
    for copy in core_copies + chip_copies + sketch_copies:
        copy.wait_send()
    for k in range(1, across):
        emb_turn(k).wait_send()
        back_turn(k).wait_send()
    for k in range(1, LINE):
        emb_line(k).wait_send()
        back_line(k).wait_send()
    for copy in (emb_core(), emb_chip(), back_core()):
        copy.wait_send()
    for c in range(chunks):
        for kind in ("cross", "near", "pass"):
            fresh_copy(c, kind).wait_send()
    for d in range(1 - LINE, LINE):
        @when(inside(d))
        def _(d=d):
            for k in range(1, across):
                held_copy(d, k).wait_send()
            for c in range(chunks):
                for k in range(across):
                    if k:
                        turn_copy(c, d, k, True).wait_send()
                    for kind in ("cross", "near", "pass"):
                        item_copy(c, d, k, kind).wait_send()
                if d:
                    merge_copy(d, c).wait_send()

        if d:
            @when(line_sends(d))
            def _(d=d):
                for c in range(chunks):
                    line_copy(c, d).wait_send()


def step_call(weights, anchor, momentum, embed, owner, own_count, per_pair):
    tiles, rows, width = weights.shape[1:]
    slots, part = anchor.shape[0], width // 4
    across, chunks = own_count // LINE, CHUNKS
    w, span = part // chunks, 2 * LINE - 1
    pairs = own_count * per_pair
    lanes = max(owner.shape[1], -(-max(pairs, slots) // 128) * 128)
    f32, dma = jnp.float32, pltpu.SemaphoreType.DMA
    emb_rows, rank = embed[1].shape[0], embed[3].shape[0]
    vmem = lambda *shape: pltpu.VMEM(shape, f32)
    turn_rows, line_width = rank // across, 2 * part // LINE
    scratch = [
        dma((9,)), dma((chunks, 2)),
        pltpu.VMEM((8, lanes), jnp.int32), pltpu.SMEM((8, lanes), jnp.int32),
        vmem(slots, rows, part), vmem(slots, rows, part), vmem(slots, rows, width),
        vmem(chunks, 2, tiles, rows, w), vmem(chunks, 2, tiles, rows, w),
        vmem(chunks, tiles, rows, w), vmem(chunks, tiles, rows, w),
        dma((chunks, 2)), dma((chunks, 2)), dma((chunks,)), dma((chunks,)),
    ]
    scratch += [vmem(tiles, rows, w) for _ in range(chunks * span)]
    scratch += [dma((chunks, span)), dma((chunks, span))]
    scratch += [vmem(chunks, LINE, across - 1, per_pair, rows, w)]
    scratch += [dma((chunks, span, across)), dma((chunks, span, across))]
    scratch += [vmem(4, pairs, rows, w) for _ in range(chunks)]
    scratch += [dma((chunks, span, across)) for _ in range(6)]
    scratch += [vmem(LINE, across - 1, per_pair, rows, part)]
    scratch += [vmem(across * per_pair, rows, part) for _ in range(span)]
    scratch += [dma((span, across)), dma((span, across))]
    scratch += [vmem(chunks, tiles, rows, w) for _ in range(span - 1)]
    scratch += [vmem(chunks, tiles, rows, w) for _ in range(2 * (LINE - 1))]
    scratch += [dma((chunks, span)), dma((chunks, span)), dma((3, chunks)), dma((3, chunks))]
    scratch += [
        vmem(emb_rows, width), vmem(emb_rows, width), vmem(emb_rows, width), vmem(rank, width),
        vmem(emb_rows, width),
    ]
    scratch += [vmem(rank, emb_rows) for _ in range(5)]
    scratch += [
        vmem(2, rank, 2 * part), vmem(rank, 2 * part),
        vmem(across, turn_rows, 2 * part), vmem(across, turn_rows, 2 * part),
        vmem(LINE, turn_rows, line_width), vmem(LINE, turn_rows, line_width),
        vmem(turn_rows, line_width), vmem(turn_rows, line_width),
        vmem(2, across, LINE, turn_rows, line_width), vmem(rank, width),
        dma((5,)), dma((5,)), dma((across,)), dma((across,)), dma((LINE,)), dma((LINE,)),
        dma((across,)), dma((across,)), dma((LINE,)), dma((LINE,)),
    ]
    return pl.pallas_call(
        functools.partial(step_kernel, own_count, per_pair, rank),
        out_shape=(
            pltpu.VMEM((tiles, rows, width), f32),
            pltpu.VMEM((slots, rows, width), f32),
            pltpu.VMEM((emb_rows, width), f32),
            pltpu.VMEM((emb_rows, width), f32),
        ),
        in_specs=[pl.BlockSpec(memory_space=pltpu.VMEM)] + [pl.BlockSpec(memory_space=pltpu.HBM)] * 7
        + [pl.BlockSpec(memory_space=pltpu.VMEM)],
        out_specs=(pl.BlockSpec(memory_space=pltpu.VMEM),) * 4,
        scratch_shapes=scratch,
        compiler_params=pltpu.CompilerParams(
            collective_id=0, has_side_effects=True, vmem_limit_bytes=50 * 1024 * 1024
        ),
        cost_estimate=pl.CostEstimate(flops=20000000, bytes_accessed=300000000, transcendentals=0),
    )(owner, weights, anchor, momentum, *embed)


def write_kernel(parts, *refs):
    count = len(parts)
    sources, targets, sem = refs[:count], refs[count : 2 * count], refs[2 * count]
    copies = []
    for source, target, pieces in zip(sources, targets, parts):
        size = source.shape[0] // pieces
        for n in range(pieces):
            at = pl.ds(n * size, size)
            copies.append(pltpu.make_async_copy(source.at[at], target.at[at], sem.at[len(copies)]))
    for copy in copies:
        copy.start()
    for copy in copies:
        copy.wait()


def write_out(results):
    parts = tuple(8 if r.ndim == 3 and r.shape[0] % 8 == 0 else 2 for r in results)
    return pl.pallas_call(
        functools.partial(write_kernel, parts),
        out_shape=tuple(jax.ShapeDtypeStruct(r.shape, r.dtype) for r in results),
        in_specs=[pl.BlockSpec(memory_space=pltpu.VMEM)] * len(results),
        out_specs=(pl.BlockSpec(memory_space=pltpu.HBM),) * len(results),
        scratch_shapes=[pltpu.SemaphoreType.DMA((sum(parts),))],
        compiler_params=pltpu.CompilerParams(vmem_limit_bytes=1024 * 1024),
        cost_estimate=pl.CostEstimate(flops=0, bytes_accessed=11000000, transcendentals=0),
    )(*results)


def local(
    weights, anchor, momentum, owner, emb_weights, emb_anchor, emb_momentum, sketch, inv_root
):
    own_count = lax.axis_size("own")
    tiles_dev = weights.shape[1]
    half_tiles = min(tiles_dev // 2, own_count)
    hot_count = max(own_count // 4, 1)
    per_pair = (tiles_dev - half_tiles) // hot_count + 1
    embed = (emb_weights, emb_anchor, emb_momentum, sketch, inv_root)
    results = step_call(weights, anchor, momentum, embed, owner[None, :], own_count, per_pair)
    return write_out(results)


def solution(mesh):
    placed = (
        P("rep", "own", None, None),
        P("own", None, None),
        P("own", None, None),
        P(),
        P("rep", "own", None),
        P("own", None),
        P("own", None),
        P(),
        P(),
    )
    return jax.shard_map(
        local,
        mesh=mesh,
        in_specs=placed,
        out_specs=(P("own", None, None), P("own", None, None), P("own", None), P("own", None)),
        check_vma=False,
    )
```

```python
import functools

import jax
import jax.numpy as jnp
from jax import lax
from jax.experimental import pallas as pl
from jax.experimental.pallas import tpu as pltpu
from jax.sharding import PartitionSpec as P

OUTER_RATE = 0.7
OUTER_MOMENTUM = 0.9
FIXED = 1.0 + OUTER_MOMENTUM
SQUARED = OUTER_MOMENTUM * OUTER_MOMENTUM
LINE = 4
CHUNKS = 4
(
    HALF, DIFF, SKETCH, HELD, LATE, RELAY, MEAN, LINED, TURNED,
    PASS, BASE, ADVANCE, MERGE, RENEW, FRESH, EMBED, CLOSE,
) = range(17)
ORDER = (
    (HELD, 3), (HELD, -2), (HALF, 1), (HELD, 1), (HALF, 0), (DIFF,), (RELAY, 2), (HELD, 2), (HELD, -3),
    (HALF, 2), (MEAN, 1), (RELAY, 3), (MEAN, 0), (SKETCH,), (MERGE, 0, -3), (MERGE, 0, 3), (MEAN, 2),
    (LINED, 1, 1), (HALF, 3), (LINED, 1, -1), (LATE,), (MERGE, 3, 3), (LINED, 0, 1), (LINED, 0, -1),
    (EMBED, 0), (EMBED, 1), (MERGE, 2, -3), (TURNED, 1, -1), (TURNED, 1, 0), (LINED, 2, -1), (LINED, 2, 1),
    (LINED, 1, -2), (BASE, 0), (TURNED, 2, 0), (MERGE, 2, 3), (MEAN, 3), (BASE, 1), (EMBED, 2),
    (TURNED, 0, 1), (MERGE, 1, 3), (LINED, 0, 2), (MERGE, 0, -2), (LINED, 2, -2), (LINED, 0, -2),
    (MERGE, 3, -3), (MERGE, 0, 2), (LINED, 2, 2), (LINED, 1, -3), (TURNED, 0, -1), (TURNED, 2, -2), (BASE, 2),
    (LINED, 3, -1), (MERGE, 1, -3), (TURNED, 1, 1), (LINED, 1, 2), (TURNED, 1, -3), (LINED, 3, 1),
    (PASS, 2, 0), (HELD, -1), (MERGE, 2, -2), (EMBED, 3), (BASE, 3), (MERGE, 2, 2), (PASS, 1, 0),
    (PASS, 0, 1), (MERGE, 1, -2), (TURNED, 0, -2), (TURNED, 2, 1), (TURNED, 0, 0), (LINED, 2, -3),
    (TURNED, 3, 0), (LINED, 0, 3), (TURNED, 1, -2), (LINED, 0, -3), (LINED, 3, -2), (TURNED, 3, 1),
    (MERGE, 1, 2), (EMBED, 4), (LINED, 2, 3), (TURNED, 2, -3), (PASS, 2, -2), (MERGE, 0, -1), (MERGE, 0, 1),
    (HELD, 0), (TURNED, 0, 3), (LINED, 1, 3), (TURNED, 1, 2), (PASS, 1, 1), (MERGE, 3, -2), (TURNED, 2, 2),
    (TURNED, 0, -3), (TURNED, 2, -1), (LINED, 3, 2), (MERGE, 2, -1), (TURNED, 2, 3), (MERGE, 1, -1),
    (TURNED, 0, 2), (LINED, 3, -3), (MERGE, 2, 1), (MERGE, 3, 2), (PASS, 0, 0), (PASS, 0, 3), (TURNED, 1, 3),
    (PASS, 2, -3), (PASS, 1, -2), (EMBED, 5), (TURNED, 3, -2), (TURNED, 3, 2), (PASS, 0, -2), (MERGE, 1, 1),
    (PASS, 0, -1), (RENEW, 0), (TURNED, 3, -3), (PASS, 2, 1), (MERGE, 3, -1), (EMBED, 6), (PASS, 2, 2),
    (TURNED, 3, -1), (PASS, 0, -3), (LINED, 3, 3), (PASS, 1, 3), (PASS, 2, -1), (PASS, 3, 1), (PASS, 2, 3),
    (PASS, 0, 2), (PASS, 3, -2), (RENEW, 2), (PASS, 1, 2), (MERGE, 3, 1), (ADVANCE, 2), (PASS, 3, -3),
    (FRESH, 0), (TURNED, 3, 3), (PASS, 1, -1), (RENEW, 1), (PASS, 3, -1), (PASS, 3, 2), (EMBED, 7),
    (PASS, 1, -3), (PASS, 3, 3), (RENEW, 3), (ADVANCE, 0), (PASS, 3, 0), (ADVANCE, 3), (FRESH, 1), (FRESH, 2),
    (FRESH, 3), (ADVANCE, 1), (CLOSE,),
)


def fill_tables(owner, table, own_index, own_count, tiles_dev, per_pair, slots):
    across_bits, tile_bits = (own_count // LINE).bit_length() - 1, tiles_dev.bit_length() - 1
    count, step = owner.shape[1], min(256, owner.shape[1])
    lanes = table.shape[1]
    owner_row = owner[...]
    my_z, my_y = own_index // (own_count // LINE), own_index % (own_count // LINE)
    y_mask = (1 << across_bits) - 1
    row_ids = lax.broadcasted_iota(jnp.int32, (step, count), 1)
    out_ids = lax.broadcasted_iota(jnp.int32, (step, lanes), 1)
    totals = None
    for first in range(0, count, step):
        ids = lax.broadcasted_iota(jnp.int32, (step, count), 0) + first
        column = jnp.sum(jnp.where(ids == row_ids, owner_row, 0), axis=1, keepdims=True)
        before = (column == owner_row) & (row_ids < ids)
        near = before & ((row_ids >> tile_bits) == (ids >> tile_bits))
        slot_rank = jnp.sum(before.astype(jnp.int32), axis=1, keepdims=True)
        pair_rank = jnp.sum(near.astype(jnp.int32), axis=1, keepdims=True)
        tile = lax.broadcasted_iota(jnp.int32, (step, 1), 0) + first
        block = tile >> tile_bits
        owner_z, turn = column >> across_bits, (column & y_mask) ^ my_y
        back_key = block * per_pair + pair_rank
        held = column == own_index
        pick_key = jnp.where(
            (owner_z == my_z) & ((block & y_mask) == my_y),
            (turn * LINE + (block >> across_bits)) * per_pair + pair_rank,
            -1,
        )
        merge = jnp.where(
            owner_z == my_z, turn * per_pair + pair_rank, jnp.where(owner_z < my_z, -1, -2)
        )
        pairs = (
            (pick_key, tile & (tiles_dev - 1)),
            (tile, merge),
            (jnp.where(held, slot_rank, -1), back_key + 1),
            (jnp.where(held, back_key, -1), slot_rank),
        )
        found = [
            jnp.sum(jnp.where(key == out_ids, value, 0), axis=0, keepdims=True)
            for key, value in pairs
        ]
        totals = found if totals is None else [a + b for a, b in zip(totals, found)]
    across = own_count // LINE
    limits = (tiles_dev - 1, across * per_pair - 1, own_count * per_pair, slots - 1)
    for n, (total, limit) in enumerate(zip(totals, limits)):
        table[n : n + 1, :] = jnp.minimum(total, limit)


def flip(index, bits):
    out, unit = index, 1
    while unit <= bits:
        if bits & unit:
            out = out + unit - 2 * unit * ((index // unit) % 2)
        unit *= 2
    return out


def step_kernel(
    own_count, per_pair, rank,
    owner, weights, anchor, momentum,
    emb_weights, emb_anchor, emb_momentum, sketch, inv_root,
    new_weights, new_momentum, new_embedding, new_emb_momentum,
    *scratch,
):
    across, chunks = own_count // LINE, CHUNKS
    take = iter(scratch)
    local_sem, mine_sem = next(take), next(take)
    table, table_read = next(take), next(take)
    news = {d: next(take) for d in range(1 - LINE, LINE) if abs(d) > 1}
    held_order = [at[1] for at in ORDER if at[0] == HELD]
    merge_order = {at[2]: at[1] for at in reversed(ORDER) if at[0] == MERGE}
    renew_order = [at[1] for at in ORDER if at[0] == RENEW]
    base_order = [at[1] for at in ORDER if at[0] == BASE]
    anchor_part, momentum_part, anchor_all = next(take), next(take), next(take)
    mine, core_in, chip_out, chip_in = next(take), next(take), next(take), next(take)
    core_send, core_recv, chip_send, chip_recv = next(take), next(take), next(take), next(take)
    line = [{d: next(take) for d in range(1 - LINE, LINE)} for _ in range(chunks)]
    line_send, line_recv = next(take), next(take)
    turned = next(take)
    turn_send, turn_recv = next(take), next(take)
    gathered = [next(take) for _ in range(chunks)]
    cross_send, cross_recv, near_send, near_recv, pass_send, pass_recv = (next(take) for _ in range(6))
    held_out = next(take)
    held_in = {d: next(take) for d in range(1 - LINE, LINE)}
    held_send, held_recv = next(take), next(take)
    merged = {d: next(take) for d in range(1 - LINE, LINE) if d}
    below = {d: next(take) for d in range(LINE - 1)}
    above = {-d: next(take) for d in range(LINE - 1)}
    merge_send, merge_recv = next(take), next(take)
    fresh_send, fresh_recv = next(take), next(take)
    emb_w, emb_a, emb_m, sketch_v = next(take), next(take), next(take), next(take)
    diff, sketch_own, sketch_half, sketch_core, sketch_chip, basis_ref = (next(take) for _ in range(6))
    f_own, f_core, f_turn, f_turn_in, f_line, f_line_in, f_chip, f_chip_in, f_all, f_flat = (
        next(take) for _ in range(10)
    )
    emb_send, emb_recv, f_turn_send, f_turn_recv, f_line_send, f_line_recv = (
        next(take) for _ in range(6)
    )
    g_turn_send, g_turn_recv, g_line_send, g_line_recv = (next(take) for _ in range(4))

    rep = lax.axis_index("rep")
    own = lax.axis_index("own")
    core = rep % 2
    z, y = own // across, own % across
    core_peer, chip_peer, far_peer = flip(rep, 1), flip(rep, 2), flip(rep, 3)
    tiles, slots = weights.shape[1], anchor.shape[0]
    width = anchor.shape[2]
    part = width // 4
    w = part // chunks
    f32, highest = jnp.float32, lax.Precision.HIGHEST

    def columns(quarter, c=None):
        if c is None:
            return pl.ds(pl.multiple_of(quarter * part, 128), part)
        return pl.ds(pl.multiple_of(quarter * part + c * w, 128), w)

    def remote(src, dst, send, recv, to_rep, to_own):
        return pltpu.make_async_remote_copy(
            src_ref=src, dst_ref=dst, send_sem=send, recv_sem=recv,
            device_id=(to_rep, to_own), device_id_type=pl.DeviceIdType.MESH,
        )

    def when(*conditions):
        held = conditions[0]
        for condition in conditions[1:]:
            held = held & condition
        return pl.when(held)

    def inside(d):
        return (z + d >= 0) & (z + d <= LINE - 1)

    mine_loads = [
        pltpu.make_async_copy(
            weights.at[0, :, :, columns(quarter, c)], mine.at[c, j], mine_sem.at[c, j]
        )
        for j, quarter in ((1, chip_peer), (0, rep))
        for c in range(chunks)
    ]
    emb_loads = [
        pltpu.make_async_copy(emb_weights.at[0], emb_w, local_sem.at[0]),
        pltpu.make_async_copy(emb_anchor, emb_a, local_sem.at[1]),
        pltpu.make_async_copy(sketch, sketch_v, local_sem.at[2]),
    ]
    part_loads = [
        pltpu.make_async_copy(anchor.at[:, :, columns(rep)], anchor_part, local_sem.at[3]),
        pltpu.make_async_copy(momentum.at[:, :, columns(rep)], momentum_part, local_sem.at[4]),
    ]
    late_loads = [
        pltpu.make_async_copy(anchor, anchor_all, local_sem.at[5]),
        pltpu.make_async_copy(momentum, new_momentum, local_sem.at[6]),
        pltpu.make_async_copy(emb_momentum, emb_m, local_sem.at[7]),
    ]
    for copy in emb_loads + mine_loads + part_loads:
        copy.start()

    barrier = pltpu.get_barrier_semaphore()
    peers = [(core_peer, own), (chip_peer, own)]
    peers += [(rep, flip(own, k)) for k in range(1, across)]
    for peer in peers:
        pl.semaphore_signal(barrier, inc=1, device_id=peer, device_id_type=pl.DeviceIdType.MESH)
    inner = (z >= 1) & (z <= LINE - 2)

    def tell(sem, step):
        pl.semaphore_signal(
            sem, inc=1, device_id=(rep, own + step * across), device_id_type=pl.DeviceIdType.MESH
        )

    for step in (1, -1):
        @pl.when(inside(step))
        def _(step=step):
            tell(barrier, step)

    fill_tables(owner, table, own, own_count, tiles, per_pair, slots)
    table_load = pltpu.make_async_copy(table, table_read, local_sem.at[8])
    table_load.start()
    table_load.wait()
    pl.semaphore_wait(barrier, len(peers) + 1 + jnp.where(inner, 1, 0))

    core_copies = [
        remote(
            weights.at[0, :, :, columns(quarter, c)], core_in.at[c, j],
            core_send.at[c, j], core_recv.at[c, j], core_peer, own,
        )
        for j, quarter in ((1, far_peer), (0, core_peer))
        for c in range(chunks)
    ]
    sketch_copies = [
        remote(sketch_own, sketch_core, emb_send.at[0], emb_recv.at[0], core_peer, own),
        remote(sketch_half, sketch_chip, emb_send.at[1], emb_recv.at[1], chip_peer, own),
    ]
    for copy in core_copies:
        copy.start()

    def held_copy(d, k):
        return remote(
            held_out.at[z + d, k - 1], held_in[d].at[pl.ds(k * per_pair, per_pair)],
            held_send.at[d + LINE - 1, k], held_recv.at[d + LINE - 1, k], rep, flip(own, k),
        )

    def held_fill(d, k):
        block = flip(own, k) + d * across

        def fill(p, carry):
            slot = table_read[3, block * per_pair + p]
            a = anchor_part[slot]
            value = a - OUTER_RATE * (FIXED * a + SQUARED * momentum_part[slot])
            if k:
                held_out[z + d, k - 1, p] = value
            else:
                held_in[d][p] = value
            return carry

        lax.fori_loop(0, per_pair, fill, 0)

    def held_start(d):
        if d == held_order[0]:
            for copy in part_loads:
                copy.wait()

        @when(inside(d))
        def _():
            for k in range(1, across):
                held_fill(d, k)
                held_copy(d, k).start()
            held_fill(d, 0)

    chip_copies = [
        remote(chip_out.at[c], chip_in.at[c], chip_send.at[c], chip_recv.at[c], chip_peer, own)
        for c in range(chunks)
    ]

    def half_sum(c):
        mine_loads[c].wait()
        core_copies[c].wait_recv()
        chip_out[c] = mine[c, 1] + core_in[c, 1]
        chip_copies[c].start()

    def sketch_start():
        for copy in emb_loads:
            copy.wait()
        diff[...] = emb_a[...] - emb_w[...]
        sketched = jnp.zeros(sketch_own.shape, f32)
        for q in range(4):
            at = slice(q * part, (q + 1) * part)
            sketched = sketched + lax.dot_general(
                sketch_v[:, at], diff[:, at], (((1,), (1,)), ((), ())),
                precision=highest, preferred_element_type=f32,
            )
        sketch_own[...] = sketched
        sketch_copies[0].start()

    def sketch_sum():
        sketch_copies[0].wait_recv()
        sketch_half[...] = sketch_own[...] + sketch_core[...]
        sketch_copies[1].start()

    def late_start():
        for copy in late_loads:
            copy.start()

    def relay(distance):
        for step in (1, -1):
            d = step * distance
            if distance > 2:
                @when(inside(d - step))
                def _(d=d, step=step):
                    pl.semaphore_wait(news[d - step], 1)

            @when(inside(d - step), inside(-step))
            def _(d=d, step=step):
                tell(news[d], -step)

    turn_rows, line_width = rank // across, 2 * part // LINE

    def emb_core():
        return remote(f_own.at[1 - core], f_core, emb_send.at[2], emb_recv.at[2], core_peer, own)

    def emb_turn(k):
        return remote(
            f_turn.at[flip(y, k)], f_turn_in.at[k], f_turn_send.at[k], f_turn_recv.at[k],
            rep, flip(own, k),
        )

    def emb_line(k):
        return remote(
            f_line.at[flip(z, k)], f_line_in.at[k], f_line_send.at[k], f_line_recv.at[k],
            rep, flip(own, k * across),
        )

    def emb_chip():
        return remote(f_chip, f_chip_in, emb_send.at[3], emb_recv.at[3], chip_peer, own)

    def back_line(k):
        here = f_all.at[core, y, z]
        return remote(here, here, g_line_send.at[k], g_line_recv.at[k], rep, flip(own, k * across))

    def back_turn(k):
        here = f_all.at[core, y]
        return remote(here, here, g_turn_send.at[k], g_turn_recv.at[k], rep, flip(own, k))

    def back_core():
        here = f_all.at[core]
        return remote(here, here, emb_send.at[4], emb_recv.at[4], core_peer, own)

    def embed_step(n):
        (emb_0, emb_1, emb_2, emb_3, emb_4, emb_5, emb_6, emb_7)[n]()

    def emb_0():
        sketch_copies[1].wait_recv()
        mean_sketch = (sketch_half[...] + sketch_chip[...]) * 0.25
        basis = jnp.dot(inv_root[...], mean_sketch, precision=highest, preferred_element_type=f32)
        basis_ref[...] = basis
        for q in range(4):
            f_own[q % 2, :, (q // 2) * part : (q // 2 + 1) * part] = jnp.dot(
                basis, diff[:, q * part : (q + 1) * part],
                precision=highest, preferred_element_type=f32,
            )
        emb_core().start()

    def emb_1():
        emb_core().wait_recv()
        for b in range(across):
            rows = slice(b * turn_rows, (b + 1) * turn_rows)
            f_turn[b] = f_own[core, rows] + f_core[rows]
        for k in range(1, across):
            emb_turn(k).start()

    def emb_2():
        for k in range(1, across):
            emb_turn(k).wait_recv()
        total = f_turn[y]
        for k in range(1, across):
            total = total + f_turn_in[k]
        for step in (1, -1):
            @when(inside(step * (LINE - 1)))
            def _(step=step):
                pl.semaphore_wait(news[step * (LINE - 1)], 1)

        for a in range(LINE):
            f_line[a] = total[:, a * line_width : (a + 1) * line_width]
        for k in range(1, LINE):
            emb_line(k).start()

    def emb_3():
        for k in range(1, LINE):
            emb_line(k).wait_recv()
        total = f_line[z]
        for k in range(1, LINE):
            total = total + f_line_in[k]
        f_chip[...] = total
        emb_chip().start()

    def emb_4():
        emb_chip().wait_recv()
        f_all[core, y, z] = (f_chip[...] + f_chip_in[...]) * 0.25
        for k in range(1, LINE):
            back_line(k).start()

    def emb_5():
        for k in range(1, LINE):
            back_line(k).wait_recv()
        for k in range(1, across):
            back_turn(k).start()

    def emb_6():
        for k in range(1, across):
            back_turn(k).wait_recv()
        back_core().start()

    def emb_7():
        late_loads[2].wait()
        back_core().wait_recv()
        for h in range(2):
            for b in range(across):
                for a in range(LINE):
                    quarter = h + 2 * ((a * line_width) // part)
                    at = quarter * part + (a * line_width) % part
                    f_flat[b * turn_rows : (b + 1) * turn_rows, at : at + line_width] = f_all[h, b, a]
        for q in range(4):
            at = slice(q * part, (q + 1) * part)
            approx = lax.dot_general(
                basis_ref[...], f_flat[:, at], (((0,), (0,)), ((), ())),
                precision=highest, preferred_element_type=f32,
            )
            moved = OUTER_MOMENTUM * emb_m[:, at] + approx
            new_emb_momentum[:, at] = moved
            new_embedding[:, at] = emb_a[:, at] - OUTER_RATE * (approx + OUTER_MOMENTUM * moved)

    def line_copy(c, d):
        step = 1 if d > 0 else -1
        return remote(
            line[c][d - step], line[c][d], line_send.at[c, d + LINE - 1],
            line_recv.at[c, d + LINE - 1], rep, own - step * across,
        )

    def line_sends(d):
        step = 1 if d > 0 else -1
        return (z - step >= 0) & (z - step <= LINE - 1) & inside(d - step)

    def rows_of(d, k):
        return pl.ds((flip(own, k) + d * across) * per_pair, per_pair)

    def turn_copy(c, d, k, sending):
        return remote(
            turned.at[c, z + d, k - 1], gathered[c].at[rep, rows_of(d, 0 if sending else k)],
            turn_send.at[c, d + LINE - 1, k], turn_recv.at[c, d + LINE - 1, k], rep, flip(own, k),
        )

    def item_copy(c, d, k, kind):
        at = (c, d + LINE - 1, k)
        if kind == "pass":
            there = gathered[c].at[chip_peer, rows_of(d, k)]
            return remote(there, there, pass_send.at[at], pass_recv.at[at], core_peer, own)
        here = gathered[c].at[rep, rows_of(d, k)]
        if kind == "cross":
            return remote(here, here, cross_send.at[at], cross_recv.at[at], chip_peer, own)
        return remote(here, here, near_send.at[at], near_recv.at[at], core_peer, own)

    def choose(c, d, k):
        block = (k * LINE + z + d) * per_pair
        first = (own + d * across) * per_pair

        def fill(p, carry):
            value = line[c][d][table_read[0, block + p]]
            if k:
                turned[c, z + d, k - 1, p] = value
            else:
                gathered[c][rep, first + p] = value
            return carry

        lax.fori_loop(0, per_pair, fill, 0, unroll=True)

    def spread(c, d):
        for k in range(1, across):
            choose(c, d, k)
            turn_copy(c, d, k, True).start()
        choose(c, d, 0)
        item_copy(c, d, 0, "cross").start()
        item_copy(c, d, 0, "near").start()

    def mean_ready(c):
        mine_loads[chunks + c].wait()
        core_copies[chunks + c].wait_recv()
        chip_copies[c].wait_recv()
        line[c][0][...] = (mine[c, 0] + core_in[c, 0] + chip_in[c]) * 0.25
        for d in (1, -1):
            @when(line_sends(d))
            def _(d=d):
                line_copy(c, d).start()
        spread(c, 0)

    def line_arrived(c, d):
        step = 1 if d > 0 else -1

        @when(inside(d))
        def _():
            line_copy(c, d).wait_recv()
            if abs(d) < LINE - 1:
                @when(line_sends(d + step))
                def _():
                    line_copy(c, d + step).start()
            spread(c, d)

    def turn_arrived(c, d):
        @when(inside(d))
        def _():
            for k in range(1, across):
                turn_copy(c, d, k, False).wait_recv()
                item_copy(c, d, k, "cross").start()
                item_copy(c, d, k, "near").start()

    def pass_on(c, d):
        @when(inside(d))
        def _():
            for k in range(across):
                item_copy(c, d, k, "cross").wait_recv()
                item_copy(c, d, k, "pass").start()

    def base_rows(piece):
        if piece == base_order[0]:
            late_loads[0].wait()
            late_loads[1].wait()
        first = piece * (slots // chunks)
        count = slots - first if piece == chunks - 1 else slots // chunks

        def body(s, carry):
            for q in range(4):
                at = pl.ds(q * part, part)
                new_momentum[s, :, at] = OUTER_MOMENTUM * new_momentum[s, :, at] + anchor_all[s, :, at]
            return carry

        lax.fori_loop(first, first + count, body, 0)

    def advance(c):
        for d in range(1 - LINE, LINE):
            @when(inside(d))
            def _(d=d):
                for k in range(across):
                    item_copy(c, d, k, "near").wait_recv()
                    item_copy(c, d, k, "pass").wait_recv()

        def one(s):
            found = table_read[2, s]
            row = jnp.maximum(found - 1, 0)
            kept = jnp.full((new_momentum.shape[1], w), found, jnp.int32) > 0
            for q in range(4):
                at = pl.ds(q * part + c * w, w)
                new_momentum[s, :, at] = jnp.where(
                    kept, new_momentum[s, :, at] - gathered[c][q, row], 0.0
                )

        unit = 8 if slots % 8 == 0 else 1

        def body(n, carry):
            for i in range(unit):
                one(n * unit + i)
            return carry

        lax.fori_loop(0, slots // unit, body, 0)

    def merge_copy(d, c):
        step = 1 if d > 0 else -1
        target = (below if d > 0 else above)[d - step]
        at = (c, d + LINE - 1)
        return remote(
            merged[d].at[c], target.at[c], merge_send.at[at], merge_recv.at[at], rep, own + step * across
        )

    def merge_tiles(d, c, store, incoming):
        first = (own + d * across) * tiles
        at = pl.ds(c * w, w)

        def body(t, carry):
            key = table_read[1, first + t]
            value = held_in[d][jnp.maximum(key, 0), :, at]
            if incoming is not None:
                keys = jnp.full((value.shape[0], w), key, jnp.int32)
                value = jnp.where(keys >= 0, value, incoming(t, keys))
            store(t, value)
            return carry

        lax.fori_loop(0, tiles, body, 0, unroll=True)

    def merge_step(c, d):
        step = 1 if d > 0 else -1
        source = (below if d > 0 else above).get(d)
        has_source = (z >= 1) if d > 0 else (z <= LINE - 2)

        def store(t, value):
            merged[d][c, t] = value

        def landed():
            if merge_order[d] == c:
                for k in range(1, across):
                    held_copy(d, k).wait_recv()

        @when(inside(d), jnp.logical_not(has_source))
        def _():
            landed()
            merge_tiles(d, c, store, None)
            merge_copy(d, c).start()

        if source is not None:
            @when(inside(d), has_source)
            def _():
                landed()
                merge_copy(d + step, c).wait_recv()
                merge_tiles(d, c, store, lambda t, keys: source[c, t])
                merge_copy(d, c).start()

    def fresh_copy(c, kind):
        at = {"cross": 0, "near": 1, "pass": 2}[kind]
        here = new_weights.at[:, :, columns(chip_peer if kind == "pass" else rep, c)]
        return remote(
            here, here, fresh_send.at[at, c], fresh_recv.at[at, c],
            chip_peer if kind == "cross" else core_peer, own,
        )

    def renew(c):
        @when(z >= 1)
        def _():
            merge_copy(1, c).wait_recv()

        @when(z <= LINE - 2)
        def _():
            merge_copy(-1, c).wait_recv()

        if renew_order[0] == c:
            for k in range(1, across):
                held_copy(0, k).wait_recv()

        def incoming(t, keys):
            return jnp.where(keys == -1, below[0][c, t], above[0][c, t])

        def store(t, value):
            new_weights[t, :, columns(rep, c)] = value + (OUTER_RATE * FIXED) * line[c][0][t]

        merge_tiles(0, c, store, incoming)
        fresh_copy(c, "cross").start()
        fresh_copy(c, "near").start()

    def fresh_pass(c):
        fresh_copy(c, "cross").wait_recv()
        fresh_copy(c, "pass").start()

    def close():
        for copy in core_copies + chip_copies + sketch_copies:
            copy.wait_send()
        for k in range(1, across):
            emb_turn(k).wait_send()
            back_turn(k).wait_send()
        for k in range(1, LINE):
            emb_line(k).wait_send()
            back_line(k).wait_send()
        for copy in (emb_core(), emb_chip(), back_core()):
            copy.wait_send()
        for d in range(1 - LINE, LINE):
            @when(inside(d))
            def _(d=d):
                for k in range(1, across):
                    held_copy(d, k).wait_send()
                for c in range(chunks):
                    for k in range(across):
                        if k:
                            turn_copy(c, d, k, True).wait_send()
                        for kind in ("cross", "near", "pass"):
                            item_copy(c, d, k, kind).wait_send()
                    if d:
                        merge_copy(d, c).wait_send()

            if d:
                @when(line_sends(d))
                def _(d=d):
                    for c in range(chunks):
                        line_copy(c, d).wait_send()

    steps = {
        HALF: half_sum, DIFF: sketch_start, SKETCH: sketch_sum, HELD: held_start, LATE: late_start, RELAY: relay, MEAN: mean_ready,
        LINED: line_arrived, TURNED: turn_arrived, PASS: pass_on, BASE: base_rows, ADVANCE: advance,
        MERGE: merge_step, RENEW: renew, FRESH: fresh_pass, EMBED: embed_step, CLOSE: close,
    }
    for step, *arguments in ORDER:
        steps[step](*arguments)

    for c in range(chunks):
        fresh_copy(c, "near").wait_recv()
        fresh_copy(c, "pass").wait_recv()
    for c in range(chunks):
        for kind in ("cross", "near", "pass"):
            fresh_copy(c, kind).wait_send()


def step_call(weights, anchor, momentum, embed, owner, own_count, per_pair):
    tiles, rows, width = weights.shape[1:]
    slots, part = anchor.shape[0], width // 4
    across, chunks = own_count // LINE, CHUNKS
    w, span = part // chunks, 2 * LINE - 1
    pairs = own_count * per_pair
    lanes = max(owner.shape[1], -(-max(pairs, slots) // 128) * 128)
    f32, dma = jnp.float32, pltpu.SemaphoreType.DMA
    emb_rows, rank = embed[1].shape[0], embed[3].shape[0]
    vmem = lambda *shape: pltpu.VMEM(shape, f32)
    turn_rows, line_width = rank // across, 2 * part // LINE
    scratch = [
        dma((9,)), dma((chunks, 2)),
        pltpu.VMEM((8, lanes), jnp.int32), pltpu.SMEM((8, lanes), jnp.int32),
        *[pltpu.SemaphoreType.REGULAR for _ in range(2 * (LINE - 2))],
        vmem(slots, rows, part), vmem(slots, rows, part), vmem(slots, rows, width),
        vmem(chunks, 2, tiles, rows, w), vmem(chunks, 2, tiles, rows, w),
        vmem(chunks, tiles, rows, w), vmem(chunks, tiles, rows, w),
        dma((chunks, 2)), dma((chunks, 2)), dma((chunks,)), dma((chunks,)),
    ]
    scratch += [vmem(tiles, rows, w) for _ in range(chunks * span)]
    scratch += [dma((chunks, span)), dma((chunks, span))]
    scratch += [vmem(chunks, LINE, across - 1, per_pair, rows, w)]
    scratch += [dma((chunks, span, across)), dma((chunks, span, across))]
    scratch += [vmem(4, pairs, rows, w) for _ in range(chunks)]
    scratch += [dma((chunks, span, across)) for _ in range(6)]
    scratch += [vmem(LINE, across - 1, per_pair, rows, part)]
    scratch += [vmem(across * per_pair, rows, part) for _ in range(span)]
    scratch += [dma((span, across)), dma((span, across))]
    scratch += [vmem(chunks, tiles, rows, w) for _ in range(span - 1)]
    scratch += [vmem(chunks, tiles, rows, w) for _ in range(2 * (LINE - 1))]
    scratch += [dma((chunks, span)), dma((chunks, span)), dma((3, chunks)), dma((3, chunks))]
    scratch += [
        vmem(emb_rows, width), vmem(emb_rows, width), vmem(emb_rows, width), vmem(rank, width),
        vmem(emb_rows, width),
    ]
    scratch += [vmem(rank, emb_rows) for _ in range(5)]
    scratch += [
        vmem(2, rank, 2 * part), vmem(rank, 2 * part),
        vmem(across, turn_rows, 2 * part), vmem(across, turn_rows, 2 * part),
        vmem(LINE, turn_rows, line_width), vmem(LINE, turn_rows, line_width),
        vmem(turn_rows, line_width), vmem(turn_rows, line_width),
        vmem(2, across, LINE, turn_rows, line_width), vmem(rank, width),
        dma((5,)), dma((5,)), dma((across,)), dma((across,)), dma((LINE,)), dma((LINE,)),
        dma((across,)), dma((across,)), dma((LINE,)), dma((LINE,)),
    ]
    return pl.pallas_call(
        functools.partial(step_kernel, own_count, per_pair, rank),
        out_shape=(
            pltpu.VMEM((tiles, rows, width), f32),
            pltpu.VMEM((slots, rows, width), f32),
            pltpu.VMEM((emb_rows, width), f32),
            pltpu.VMEM((emb_rows, width), f32),
        ),
        in_specs=[pl.BlockSpec(memory_space=pltpu.VMEM)] + [pl.BlockSpec(memory_space=pltpu.HBM)] * 7
        + [pl.BlockSpec(memory_space=pltpu.VMEM)],
        out_specs=(pl.BlockSpec(memory_space=pltpu.VMEM),) * 4,
        scratch_shapes=scratch,
        compiler_params=pltpu.CompilerParams(
            collective_id=0, has_side_effects=True, vmem_limit_bytes=50 * 1024 * 1024
        ),
        cost_estimate=pl.CostEstimate(flops=20000000, bytes_accessed=300000000, transcendentals=0),
    )(owner, weights, anchor, momentum, *embed)


def write_kernel(parts, *refs):
    count = len(parts)
    sources, targets, sem = refs[:count], refs[count : 2 * count], refs[2 * count]
    copies = []
    for source, target, pieces in zip(sources, targets, parts):
        size = source.shape[0] // pieces
        for n in range(pieces):
            at = pl.ds(n * size, size)
            copies.append(pltpu.make_async_copy(source.at[at], target.at[at], sem.at[len(copies)]))
    for copy in copies:
        copy.start()
    for copy in copies:
        copy.wait()


def write_out(results):
    parts = tuple(8 if r.ndim == 3 and r.shape[0] % 8 == 0 else 2 for r in results)
    return pl.pallas_call(
        functools.partial(write_kernel, parts),
        out_shape=tuple(jax.ShapeDtypeStruct(r.shape, r.dtype) for r in results),
        in_specs=[pl.BlockSpec(memory_space=pltpu.VMEM)] * len(results),
        out_specs=(pl.BlockSpec(memory_space=pltpu.HBM),) * len(results),
        scratch_shapes=[pltpu.SemaphoreType.DMA((sum(parts),))],
        compiler_params=pltpu.CompilerParams(vmem_limit_bytes=1024 * 1024),
        cost_estimate=pl.CostEstimate(flops=0, bytes_accessed=11000000, transcendentals=0),
    )(*results)


def local(
    weights, anchor, momentum, owner, emb_weights, emb_anchor, emb_momentum, sketch, inv_root
):
    own_count = lax.axis_size("own")
    tiles_dev = weights.shape[1]
    half_tiles = min(tiles_dev // 2, own_count)
    hot_count = max(own_count // 4, 1)
    per_pair = (tiles_dev - half_tiles) // hot_count + 1
    embed = (emb_weights, emb_anchor, emb_momentum, sketch, inv_root)
    results = step_call(weights, anchor, momentum, embed, owner[None, :], own_count, per_pair)
    return write_out(results)


def solution(mesh):
    placed = (
        P("rep", "own", None, None),
        P("own", None, None),
        P("own", None, None),
        P(),
        P("rep", "own", None),
        P("own", None),
        P("own", None),
        P(),
        P(),
    )
    return jax.shard_map(
        local,
        mesh=mesh,
        in_specs=placed,
        out_specs=(P("own", None, None), P("own", None, None), P("own", None), P("own", None)),
        check_vma=False,
    )
```

```python
import functools

import jax
import jax.numpy as jnp
from jax import lax
from jax.experimental import pallas as pl
from jax.experimental.pallas import tpu as pltpu
from jax.sharding import PartitionSpec as P

OUTER_RATE = 0.7
OUTER_MOMENTUM = 0.9
FIXED = 1.0 + OUTER_MOMENTUM
SQUARED = OUTER_MOMENTUM * OUTER_MOMENTUM
LINE = 4
CHUNKS = 4
(
    HALF, DIFF, SKETCH, HELD, LATE, RELAY, MEAN, LINED, TURNED,
    PASS, BASE, ADVANCE, MERGE, RENEW, FRESH, EMBED, CLOSE,
) = range(17)
ORDER = (
    (HELD, 3), (HELD, -3), (HALF, 1), (HELD, 1), (LATE,), (HALF, 0), (HALF, 2), (HELD, 2), (DIFF,),
    (RELAY, 2), (HELD, -2), (MEAN, 1), (RELAY, 3), (SKETCH,), (MEAN, 0), (BASE, 1), (MEAN, 2), (MERGE, 0, 3),
    (LINED, 1, 1), (MERGE, 0, -3), (MERGE, 2, -3), (HALF, 3), (LINED, 0, 1), (LINED, 1, -1), (MERGE, 2, 3),
    (EMBED, 0), (MERGE, 3, 3), (TURNED, 1, 0), (MERGE, 1, -3), (LINED, 2, -1), (LINED, 0, -1), (EMBED, 1),
    (LINED, 2, 1), (TURNED, 1, 1), (MEAN, 3), (TURNED, 1, -1), (TURNED, 0, -1), (LINED, 2, -2),
    (TURNED, 2, 0), (BASE, 0), (LINED, 0, 2), (HELD, -1), (EMBED, 2), (LINED, 2, 2), (LINED, 1, -2),
    (MERGE, 0, 2), (TURNED, 0, 1), (TURNED, 2, -1), (MERGE, 0, -2), (LINED, 1, 2), (BASE, 2), (MERGE, 1, 3),
    (MERGE, 2, -2), (TURNED, 3, 0), (BASE, 3), (LINED, 3, -1), (TURNED, 2, 1), (MERGE, 3, 2), (LINED, 0, -2),
    (LINED, 0, 3), (PASS, 1, -1), (LINED, 2, -3), (PASS, 1, 0), (MERGE, 2, 2), (EMBED, 3), (LINED, 3, 1),
    (MERGE, 3, -3), (TURNED, 0, 0), (PASS, 1, 1), (MERGE, 1, -2), (LINED, 1, -3), (TURNED, 2, 2),
    (PASS, 2, 0), (TURNED, 2, -2), (LINED, 2, 3), (MERGE, 1, 2), (LINED, 1, 3), (TURNED, 1, -2),
    (TURNED, 2, 3), (TURNED, 3, 1), (LINED, 3, 2), (MERGE, 3, -2), (TURNED, 1, -3), (LINED, 3, -2),
    (PASS, 0, 1), (TURNED, 2, -3), (PASS, 2, -1), (TURNED, 0, -2), (PASS, 0, -1), (TURNED, 0, 2),
    (LINED, 0, -3), (TURNED, 3, -1), (HELD, 0), (EMBED, 4), (MERGE, 0, -1), (MERGE, 0, 1), (TURNED, 0, 3),
    (MERGE, 2, -1), (MERGE, 2, 1), (TURNED, 3, -2), (MERGE, 1, 1), (LINED, 3, 3), (MERGE, 3, 1), (PASS, 2, 1),
    (PASS, 1, -3), (TURNED, 1, 2), (PASS, 2, 2), (TURNED, 3, 2), (TURNED, 1, 3), (PASS, 0, 3), (PASS, 0, 0),
    (PASS, 1, -2), (PASS, 2, 3), (TURNED, 0, -3), (MERGE, 1, -1), (PASS, 3, 0), (PASS, 3, 1), (PASS, 2, -2),
    (PASS, 2, -3), (LINED, 3, -3), (MERGE, 3, -1), (PASS, 0, 2), (EMBED, 5), (TURNED, 3, 3), (RENEW, 0),
    (ADVANCE, 2), (PASS, 0, -2), (PASS, 0, -3), (PASS, 1, 2), (PASS, 1, 3), (TURNED, 3, -3), (PASS, 3, -2),
    (RENEW, 2), (ADVANCE, 0), (PASS, 3, -1), (RENEW, 1), (PASS, 3, 3), (EMBED, 6), (PASS, 3, -3),
    (PASS, 3, 2), (CLOSE,), (FRESH, 0), (RENEW, 3), (ADVANCE, 1), (FRESH, 2), (ADVANCE, 3), (FRESH, 1),
    (EMBED, 7), (FRESH, 3),
)


def fill_tables(owner, table, own_index, own_count, tiles_dev, per_pair, slots):
    across_bits, tile_bits = (own_count // LINE).bit_length() - 1, tiles_dev.bit_length() - 1
    count, step = owner.shape[1], min(256, owner.shape[1])
    lanes = table.shape[1]
    owner_row = owner[...]
    my_z, my_y = own_index // (own_count // LINE), own_index % (own_count // LINE)
    y_mask = (1 << across_bits) - 1
    row_ids = lax.broadcasted_iota(jnp.int32, (step, count), 1)
    out_ids = lax.broadcasted_iota(jnp.int32, (step, lanes), 1)
    totals = None
    for first in range(0, count, step):
        ids = lax.broadcasted_iota(jnp.int32, (step, count), 0) + first
        column = jnp.sum(jnp.where(ids == row_ids, owner_row, 0), axis=1, keepdims=True)
        before = (column == owner_row) & (row_ids < ids)
        near = before & ((row_ids >> tile_bits) == (ids >> tile_bits))
        slot_rank = jnp.sum(before.astype(jnp.int32), axis=1, keepdims=True)
        pair_rank = jnp.sum(near.astype(jnp.int32), axis=1, keepdims=True)
        tile = lax.broadcasted_iota(jnp.int32, (step, 1), 0) + first
        block = tile >> tile_bits
        owner_z, turn = column >> across_bits, (column & y_mask) ^ my_y
        back_key = block * per_pair + pair_rank
        held = column == own_index
        pick_key = jnp.where(
            (owner_z == my_z) & ((block & y_mask) == my_y),
            (turn * LINE + (block >> across_bits)) * per_pair + pair_rank,
            -1,
        )
        merge = jnp.where(
            owner_z == my_z, turn * per_pair + pair_rank, jnp.where(owner_z < my_z, -1, -2)
        )
        pairs = (
            (pick_key, tile & (tiles_dev - 1)),
            (tile, merge),
            (jnp.where(held, slot_rank, -1), back_key + 1),
            (jnp.where(held, back_key, -1), slot_rank),
        )
        found = [
            jnp.sum(jnp.where(key == out_ids, value, 0), axis=0, keepdims=True)
            for key, value in pairs
        ]
        totals = found if totals is None else [a + b for a, b in zip(totals, found)]
    across = own_count // LINE
    limits = (tiles_dev - 1, across * per_pair - 1, own_count * per_pair, slots - 1)
    for n, (total, limit) in enumerate(zip(totals, limits)):
        table[n : n + 1, :] = jnp.minimum(total, limit)


def flip(index, bits):
    out, unit = index, 1
    while unit <= bits:
        if bits & unit:
            out = out + unit - 2 * unit * ((index // unit) % 2)
        unit *= 2
    return out


def step_kernel(
    own_count, per_pair, rank,
    owner, weights, anchor, momentum,
    emb_weights, emb_anchor, emb_momentum, sketch, inv_root,
    new_weights, new_momentum, new_embedding, new_emb_momentum,
    *scratch,
):
    across, chunks = own_count // LINE, CHUNKS
    take = iter(scratch)
    local_sem, mine_sem = next(take), next(take)
    table, table_read = next(take), next(take)
    news = {d: next(take) for d in range(1 - LINE, LINE) if abs(d) > 1}
    held_order = [at[1] for at in ORDER if at[0] == HELD]
    merge_order = {at[2]: at[1] for at in reversed(ORDER) if at[0] == MERGE}
    renew_order = [at[1] for at in ORDER if at[0] == RENEW]
    base_order = [at[1] for at in ORDER if at[0] == BASE]
    anchor_part, momentum_part, anchor_all = next(take), next(take), next(take)
    mine, core_in, chip_out, chip_in = next(take), next(take), next(take), next(take)
    core_send, core_recv, chip_send, chip_recv = next(take), next(take), next(take), next(take)
    line = [{d: next(take) for d in range(1 - LINE, LINE)} for _ in range(chunks)]
    line_send, line_recv = next(take), next(take)
    turned = next(take)
    turn_send, turn_recv = next(take), next(take)
    gathered = [next(take) for _ in range(chunks)]
    cross_send, cross_recv, near_send, near_recv, pass_send, pass_recv = (next(take) for _ in range(6))
    held_out = next(take)
    held_in = {d: next(take) for d in range(1 - LINE, LINE)}
    held_send, held_recv = next(take), next(take)
    merged = {d: next(take) for d in range(1 - LINE, LINE) if d}
    below = {d: next(take) for d in range(LINE - 1)}
    above = {-d: next(take) for d in range(LINE - 1)}
    merge_send, merge_recv = next(take), next(take)
    fresh_send, fresh_recv = next(take), next(take)
    emb_w, emb_a, emb_m, sketch_v = next(take), next(take), next(take), next(take)
    diff, sketch_own, sketch_half, sketch_core, sketch_chip, basis_ref = (next(take) for _ in range(6))
    f_own, f_core, f_turn, f_turn_in, f_line, f_line_in, f_chip, f_chip_in, f_all, f_flat = (
        next(take) for _ in range(10)
    )
    emb_send, emb_recv, f_turn_send, f_turn_recv, f_line_send, f_line_recv = (
        next(take) for _ in range(6)
    )
    g_turn_send, g_turn_recv, g_line_send, g_line_recv = (next(take) for _ in range(4))

    rep = lax.axis_index("rep")
    own = lax.axis_index("own")
    core = rep % 2
    z, y = own // across, own % across
    core_peer, chip_peer, far_peer = flip(rep, 1), flip(rep, 2), flip(rep, 3)
    tiles, slots = weights.shape[1], anchor.shape[0]
    width = anchor.shape[2]
    part = width // 4
    w = part // chunks
    f32, highest = jnp.float32, lax.Precision.HIGHEST

    def columns(quarter, c=None):
        if c is None:
            return pl.ds(pl.multiple_of(quarter * part, 128), part)
        return pl.ds(pl.multiple_of(quarter * part + c * w, 128), w)

    def remote(src, dst, send, recv, to_rep, to_own):
        return pltpu.make_async_remote_copy(
            src_ref=src, dst_ref=dst, send_sem=send, recv_sem=recv,
            device_id=(to_rep, to_own), device_id_type=pl.DeviceIdType.MESH,
        )

    def when(*conditions):
        held = conditions[0]
        for condition in conditions[1:]:
            held = held & condition
        return pl.when(held)

    def inside(d):
        return (z + d >= 0) & (z + d <= LINE - 1)

    mine_loads = [
        pltpu.make_async_copy(
            weights.at[0, :, :, columns(quarter, c)], mine.at[c, j], mine_sem.at[c, j]
        )
        for j, quarter in ((1, chip_peer), (0, rep))
        for c in range(chunks)
    ]
    emb_loads = [
        pltpu.make_async_copy(emb_weights.at[0], emb_w, local_sem.at[0]),
        pltpu.make_async_copy(emb_anchor, emb_a, local_sem.at[1]),
        pltpu.make_async_copy(sketch, sketch_v, local_sem.at[2]),
    ]
    part_loads = [
        pltpu.make_async_copy(anchor.at[:, :, columns(rep)], anchor_part, local_sem.at[3]),
        pltpu.make_async_copy(momentum.at[:, :, columns(rep)], momentum_part, local_sem.at[4]),
    ]
    late_loads = [
        pltpu.make_async_copy(anchor, anchor_all, local_sem.at[5]),
        pltpu.make_async_copy(momentum, new_momentum, local_sem.at[6]),
        pltpu.make_async_copy(emb_momentum, emb_m, local_sem.at[7]),
    ]
    for copy in emb_loads + mine_loads + part_loads:
        copy.start()

    barrier = pltpu.get_barrier_semaphore()
    peers = [(core_peer, own), (chip_peer, own)]
    peers += [(rep, flip(own, k)) for k in range(1, across)]
    for peer in peers:
        pl.semaphore_signal(barrier, inc=1, device_id=peer, device_id_type=pl.DeviceIdType.MESH)
    inner = (z >= 1) & (z <= LINE - 2)

    def tell(sem, step):
        pl.semaphore_signal(
            sem, inc=1, device_id=(rep, own + step * across), device_id_type=pl.DeviceIdType.MESH
        )

    for step in (1, -1):
        @pl.when(inside(step))
        def _(step=step):
            tell(barrier, step)

    fill_tables(owner, table, own, own_count, tiles, per_pair, slots)
    table_load = pltpu.make_async_copy(table, table_read, local_sem.at[8])
    table_load.start()
    table_load.wait()
    pl.semaphore_wait(barrier, len(peers) + 1 + jnp.where(inner, 1, 0))

    core_copies = [
        remote(
            weights.at[0, :, :, columns(quarter, c)], core_in.at[c, j],
            core_send.at[c, j], core_recv.at[c, j], core_peer, own,
        )
        for j, quarter in ((1, far_peer), (0, core_peer))
        for c in range(chunks)
    ]
    sketch_copies = [
        remote(sketch_own, sketch_core, emb_send.at[0], emb_recv.at[0], core_peer, own),
        remote(sketch_half, sketch_chip, emb_send.at[1], emb_recv.at[1], chip_peer, own),
    ]
    for copy in core_copies:
        copy.start()

    def held_copy(d, k):
        return remote(
            held_out.at[z + d, k - 1], held_in[d].at[pl.ds(k * per_pair, per_pair)],
            held_send.at[d + LINE - 1, k], held_recv.at[d + LINE - 1, k], rep, flip(own, k),
        )

    def held_fill(d, k):
        block = flip(own, k) + d * across

        def fill(p, carry):
            slot = table_read[3, block * per_pair + p]
            a = anchor_part[slot]
            value = a - OUTER_RATE * (FIXED * a + SQUARED * momentum_part[slot])
            if k:
                held_out[z + d, k - 1, p] = value
            else:
                held_in[d][p] = value
            return carry

        lax.fori_loop(0, per_pair, fill, 0)

    def held_start(d):
        if d == held_order[0]:
            for copy in part_loads:
                copy.wait()

        @when(inside(d))
        def _():
            for k in range(1, across):
                held_fill(d, k)
                held_copy(d, k).start()
            held_fill(d, 0)

    chip_copies = [
        remote(chip_out.at[c], chip_in.at[c], chip_send.at[c], chip_recv.at[c], chip_peer, own)
        for c in range(chunks)
    ]

    def half_sum(c):
        mine_loads[c].wait()
        core_copies[c].wait_recv()
        chip_out[c] = mine[c, 1] + core_in[c, 1]
        chip_copies[c].start()

    def sketch_start():
        for copy in emb_loads:
            copy.wait()
        diff[...] = emb_a[...] - emb_w[...]
        sketched = jnp.zeros(sketch_own.shape, f32)
        for q in range(4):
            at = slice(q * part, (q + 1) * part)
            sketched = sketched + lax.dot_general(
                sketch_v[:, at], diff[:, at], (((1,), (1,)), ((), ())),
                precision=highest, preferred_element_type=f32,
            )
        sketch_own[...] = sketched
        sketch_copies[0].start()

    def sketch_sum():
        sketch_copies[0].wait_recv()
        sketch_half[...] = sketch_own[...] + sketch_core[...]
        sketch_copies[1].start()

    def late_start():
        for copy in late_loads:
            copy.start()

    def relay(distance):
        for step in (1, -1):
            d = step * distance
            if distance > 2:
                @when(inside(d - step))
                def _(d=d, step=step):
                    pl.semaphore_wait(news[d - step], 1)

            @when(inside(d - step), inside(-step))
            def _(d=d, step=step):
                tell(news[d], -step)

    turn_rows, line_width = rank // across, 2 * part // LINE

    def emb_core():
        return remote(f_own.at[1 - core], f_core, emb_send.at[2], emb_recv.at[2], core_peer, own)

    def emb_turn(k):
        return remote(
            f_turn.at[flip(y, k)], f_turn_in.at[k], f_turn_send.at[k], f_turn_recv.at[k],
            rep, flip(own, k),
        )

    def emb_line(k):
        return remote(
            f_line.at[flip(z, k)], f_line_in.at[k], f_line_send.at[k], f_line_recv.at[k],
            rep, flip(own, k * across),
        )

    def emb_chip():
        return remote(f_chip, f_chip_in, emb_send.at[3], emb_recv.at[3], chip_peer, own)

    def back_line(k):
        here = f_all.at[core, y, z]
        return remote(here, here, g_line_send.at[k], g_line_recv.at[k], rep, flip(own, k * across))

    def back_turn(k):
        here = f_all.at[core, y]
        return remote(here, here, g_turn_send.at[k], g_turn_recv.at[k], rep, flip(own, k))

    def back_core():
        here = f_all.at[core]
        return remote(here, here, emb_send.at[4], emb_recv.at[4], core_peer, own)

    def embed_step(n):
        (emb_0, emb_1, emb_2, emb_3, emb_4, emb_5, emb_6, emb_7)[n]()

    def emb_0():
        sketch_copies[1].wait_recv()
        mean_sketch = (sketch_half[...] + sketch_chip[...]) * 0.25
        basis = jnp.dot(inv_root[...], mean_sketch, precision=highest, preferred_element_type=f32)
        basis_ref[...] = basis
        for q in range(4):
            f_own[q % 2, :, (q // 2) * part : (q // 2 + 1) * part] = jnp.dot(
                basis, diff[:, q * part : (q + 1) * part],
                precision=highest, preferred_element_type=f32,
            )
        emb_core().start()

    def emb_1():
        emb_core().wait_recv()
        for b in range(across):
            rows = slice(b * turn_rows, (b + 1) * turn_rows)
            f_turn[b] = f_own[core, rows] + f_core[rows]
        for k in range(1, across):
            emb_turn(k).start()

    def emb_2():
        for k in range(1, across):
            emb_turn(k).wait_recv()
        total = f_turn[y]
        for k in range(1, across):
            total = total + f_turn_in[k]
        for step in (1, -1):
            @when(inside(step * (LINE - 1)))
            def _(step=step):
                pl.semaphore_wait(news[step * (LINE - 1)], 1)

        for a in range(LINE):
            f_line[a] = total[:, a * line_width : (a + 1) * line_width]
        for k in range(1, LINE):
            emb_line(k).start()

    def emb_3():
        for k in range(1, LINE):
            emb_line(k).wait_recv()
        total = f_line[z]
        for k in range(1, LINE):
            total = total + f_line_in[k]
        f_chip[...] = total
        emb_chip().start()

    def emb_4():
        emb_chip().wait_recv()
        f_all[core, y, z] = (f_chip[...] + f_chip_in[...]) * 0.25
        for k in range(1, LINE):
            back_line(k).start()

    def emb_5():
        for k in range(1, LINE):
            back_line(k).wait_recv()
        for k in range(1, across):
            back_turn(k).start()

    def emb_6():
        for k in range(1, across):
            back_turn(k).wait_recv()
        back_core().start()

    def emb_7():
        late_loads[2].wait()
        back_core().wait_recv()
        for h in range(2):
            for b in range(across):
                for a in range(LINE):
                    quarter = h + 2 * ((a * line_width) // part)
                    at = quarter * part + (a * line_width) % part
                    f_flat[b * turn_rows : (b + 1) * turn_rows, at : at + line_width] = f_all[h, b, a]
        for q in range(4):
            at = slice(q * part, (q + 1) * part)
            approx = lax.dot_general(
                basis_ref[...], f_flat[:, at], (((0,), (0,)), ((), ())),
                precision=highest, preferred_element_type=f32,
            )
            moved = OUTER_MOMENTUM * emb_m[:, at] + approx
            new_emb_momentum[:, at] = moved
            new_embedding[:, at] = emb_a[:, at] - OUTER_RATE * (approx + OUTER_MOMENTUM * moved)

    def line_copy(c, d):
        step = 1 if d > 0 else -1
        return remote(
            line[c][d - step], line[c][d], line_send.at[c, d + LINE - 1],
            line_recv.at[c, d + LINE - 1], rep, own - step * across,
        )

    def line_sends(d):
        step = 1 if d > 0 else -1
        return (z - step >= 0) & (z - step <= LINE - 1) & inside(d - step)

    def rows_of(d, k):
        return pl.ds((flip(own, k) + d * across) * per_pair, per_pair)

    def turn_copy(c, d, k, sending):
        return remote(
            turned.at[c, z + d, k - 1], gathered[c].at[rep, rows_of(d, 0 if sending else k)],
            turn_send.at[c, d + LINE - 1, k], turn_recv.at[c, d + LINE - 1, k], rep, flip(own, k),
        )

    def item_copy(c, d, k, kind):
        at = (c, d + LINE - 1, k)
        if kind == "cross":
            here = gathered[c].at[rep, rows_of(d, k)]
            return remote(here, here, cross_send.at[at], cross_recv.at[at], chip_peer, own)
        rows = pl.ds((z + d) * across * per_pair, across * per_pair)
        if kind == "pass":
            there = gathered[c].at[chip_peer, rows]
            return remote(there, there, pass_send.at[at], pass_recv.at[at], core_peer, own)
        here = gathered[c].at[rep, rows]
        return remote(here, here, near_send.at[at], near_recv.at[at], core_peer, own)

    def choose(c, d, k):
        block = (k * LINE + z + d) * per_pair
        first = (own + d * across) * per_pair

        def fill(p, carry):
            value = line[c][d][table_read[0, block + p]]
            if k:
                turned[c, z + d, k - 1, p] = value
            else:
                gathered[c][rep, first + p] = value
            return carry

        lax.fori_loop(0, per_pair, fill, 0, unroll=True)

    def spread(c, d):
        for k in range(1, across):
            choose(c, d, k)
            turn_copy(c, d, k, True).start()
        choose(c, d, 0)
        item_copy(c, d, 0, "cross").start()

    def mean_ready(c):
        mine_loads[chunks + c].wait()
        core_copies[chunks + c].wait_recv()
        chip_copies[c].wait_recv()
        line[c][0][...] = (mine[c, 0] + core_in[c, 0] + chip_in[c]) * 0.25
        for d in (1, -1):
            @when(line_sends(d))
            def _(d=d):
                line_copy(c, d).start()
        spread(c, 0)

    def line_arrived(c, d):
        step = 1 if d > 0 else -1

        @when(inside(d))
        def _():
            line_copy(c, d).wait_recv()
            if abs(d) < LINE - 1:
                @when(line_sends(d + step))
                def _():
                    line_copy(c, d + step).start()
            spread(c, d)

    def turn_arrived(c, d):
        @when(inside(d))
        def _():
            for k in range(1, across):
                turn_copy(c, d, k, False).wait_recv()
                item_copy(c, d, k, "cross").start()
            item_copy(c, d, 0, "near").start()

    def pass_on(c, d):
        @when(inside(d))
        def _():
            for k in range(across):
                item_copy(c, d, k, "cross").wait_recv()
            item_copy(c, d, 0, "pass").start()

    def base_rows(piece):
        if piece == base_order[0]:
            late_loads[0].wait()
            late_loads[1].wait()
        first = piece * (slots // chunks)
        count = slots - first if piece == chunks - 1 else slots // chunks

        def body(s, carry):
            for q in range(4):
                at = pl.ds(q * part, part)
                new_momentum[s, :, at] = OUTER_MOMENTUM * new_momentum[s, :, at] + anchor_all[s, :, at]
            return carry

        lax.fori_loop(first, first + count, body, 0)

    def advance(c):
        for d in range(1 - LINE, LINE):
            @when(inside(d))
            def _(d=d):
                item_copy(c, d, 0, "near").wait_recv()
                item_copy(c, d, 0, "pass").wait_recv()

        def one(s):
            found = table_read[2, s]
            row = jnp.maximum(found - 1, 0)
            kept = jnp.full((new_momentum.shape[1], w), found, jnp.int32) > 0
            for q in range(4):
                at = pl.ds(q * part + c * w, w)
                new_momentum[s, :, at] = jnp.where(
                    kept, new_momentum[s, :, at] - gathered[c][q, row], 0.0
                )

        unit = 8 if slots % 8 == 0 else 1

        def body(n, carry):
            for i in range(unit):
                one(n * unit + i)
            return carry

        lax.fori_loop(0, slots // unit, body, 0)

    def merge_copy(d, c):
        step = 1 if d > 0 else -1
        target = (below if d > 0 else above)[d - step]
        at = (c, d + LINE - 1)
        return remote(
            merged[d].at[c], target.at[c], merge_send.at[at], merge_recv.at[at], rep, own + step * across
        )

    def merge_tiles(d, c, store, incoming):
        first = (own + d * across) * tiles
        at = pl.ds(c * w, w)

        def body(t, carry):
            key = table_read[1, first + t]
            value = held_in[d][jnp.maximum(key, 0), :, at]
            if incoming is not None:
                keys = jnp.full((value.shape[0], w), key, jnp.int32)
                value = jnp.where(keys >= 0, value, incoming(t, keys))
            store(t, value)
            return carry

        lax.fori_loop(0, tiles, body, 0, unroll=True)

    def merge_step(c, d):
        step = 1 if d > 0 else -1
        source = (below if d > 0 else above).get(d)
        has_source = (z >= 1) if d > 0 else (z <= LINE - 2)

        def store(t, value):
            merged[d][c, t] = value

        def landed():
            if merge_order[d] == c:
                for k in range(1, across):
                    held_copy(d, k).wait_recv()

        @when(inside(d), jnp.logical_not(has_source))
        def _():
            landed()
            merge_tiles(d, c, store, None)
            merge_copy(d, c).start()

        if source is not None:
            @when(inside(d), has_source)
            def _():
                landed()
                merge_copy(d + step, c).wait_recv()
                merge_tiles(d, c, store, lambda t, keys: source[c, t])
                merge_copy(d, c).start()

    def fresh_copy(c, kind):
        at = {"cross": 0, "near": 1, "pass": 2}[kind]
        here = new_weights.at[:, :, columns(chip_peer if kind == "pass" else rep, c)]
        return remote(
            here, here, fresh_send.at[at, c], fresh_recv.at[at, c],
            chip_peer if kind == "cross" else core_peer, own,
        )

    def renew(c):
        @when(z >= 1)
        def _():
            merge_copy(1, c).wait_recv()

        @when(z <= LINE - 2)
        def _():
            merge_copy(-1, c).wait_recv()

        if renew_order[0] == c:
            for k in range(1, across):
                held_copy(0, k).wait_recv()

        def incoming(t, keys):
            return jnp.where(keys == -1, below[0][c, t], above[0][c, t])

        def store(t, value):
            new_weights[t, :, columns(rep, c)] = value + (OUTER_RATE * FIXED) * line[c][0][t]

        merge_tiles(0, c, store, incoming)
        fresh_copy(c, "cross").start()
        fresh_copy(c, "near").start()

    def fresh_pass(c):
        fresh_copy(c, "cross").wait_recv()
        fresh_copy(c, "pass").start()

    def close():
        for copy in core_copies + chip_copies + sketch_copies:
            copy.wait_send()
        for k in range(1, across):
            emb_turn(k).wait_send()
            back_turn(k).wait_send()
        for k in range(1, LINE):
            emb_line(k).wait_send()
            back_line(k).wait_send()
        for copy in (emb_core(), emb_chip(), back_core()):
            copy.wait_send()
        for d in range(1 - LINE, LINE):
            @when(inside(d))
            def _(d=d):
                for k in range(1, across):
                    held_copy(d, k).wait_send()
                for c in range(chunks):
                    for k in range(across):
                        if k:
                            turn_copy(c, d, k, True).wait_send()
                        item_copy(c, d, k, "cross").wait_send()
                    item_copy(c, d, 0, "near").wait_send()
                    item_copy(c, d, 0, "pass").wait_send()
                    if d:
                        merge_copy(d, c).wait_send()

            if d:
                @when(line_sends(d))
                def _(d=d):
                    for c in range(chunks):
                        line_copy(c, d).wait_send()

    steps = {
        HALF: half_sum, DIFF: sketch_start, SKETCH: sketch_sum, HELD: held_start, LATE: late_start, RELAY: relay, MEAN: mean_ready,
        LINED: line_arrived, TURNED: turn_arrived, PASS: pass_on, BASE: base_rows, ADVANCE: advance,
        MERGE: merge_step, RENEW: renew, FRESH: fresh_pass, EMBED: embed_step, CLOSE: close,
    }
    for step, *arguments in ORDER:
        steps[step](*arguments)

    for c in range(chunks):
        fresh_copy(c, "near").wait_recv()
        fresh_copy(c, "pass").wait_recv()
    for c in range(chunks):
        for kind in ("cross", "near", "pass"):
            fresh_copy(c, kind).wait_send()


def step_call(weights, anchor, momentum, embed, owner, own_count, per_pair):
    tiles, rows, width = weights.shape[1:]
    slots, part = anchor.shape[0], width // 4
    across, chunks = own_count // LINE, CHUNKS
    w, span = part // chunks, 2 * LINE - 1
    pairs = own_count * per_pair
    lanes = max(owner.shape[1], -(-max(pairs, slots) // 128) * 128)
    f32, dma = jnp.float32, pltpu.SemaphoreType.DMA
    emb_rows, rank = embed[1].shape[0], embed[3].shape[0]
    vmem = lambda *shape: pltpu.VMEM(shape, f32)
    turn_rows, line_width = rank // across, 2 * part // LINE
    scratch = [
        dma((9,)), dma((chunks, 2)),
        pltpu.VMEM((8, lanes), jnp.int32), pltpu.SMEM((8, lanes), jnp.int32),
        *[pltpu.SemaphoreType.REGULAR for _ in range(2 * (LINE - 2))],
        vmem(slots, rows, part), vmem(slots, rows, part), vmem(slots, rows, width),
        vmem(chunks, 2, tiles, rows, w), vmem(chunks, 2, tiles, rows, w),
        vmem(chunks, tiles, rows, w), vmem(chunks, tiles, rows, w),
        dma((chunks, 2)), dma((chunks, 2)), dma((chunks,)), dma((chunks,)),
    ]
    scratch += [vmem(tiles, rows, w) for _ in range(chunks * span)]
    scratch += [dma((chunks, span)), dma((chunks, span))]
    scratch += [vmem(chunks, LINE, across - 1, per_pair, rows, w)]
    scratch += [dma((chunks, span, across)), dma((chunks, span, across))]
    scratch += [vmem(4, pairs, rows, w) for _ in range(chunks)]
    scratch += [dma((chunks, span, across)) for _ in range(6)]
    scratch += [vmem(LINE, across - 1, per_pair, rows, part)]
    scratch += [vmem(across * per_pair, rows, part) for _ in range(span)]
    scratch += [dma((span, across)), dma((span, across))]
    scratch += [vmem(chunks, tiles, rows, w) for _ in range(span - 1)]
    scratch += [vmem(chunks, tiles, rows, w) for _ in range(2 * (LINE - 1))]
    scratch += [dma((chunks, span)), dma((chunks, span)), dma((3, chunks)), dma((3, chunks))]
    scratch += [
        vmem(emb_rows, width), vmem(emb_rows, width), vmem(emb_rows, width), vmem(rank, width),
        vmem(emb_rows, width),
    ]
    scratch += [vmem(rank, emb_rows) for _ in range(5)]
    scratch += [
        vmem(2, rank, 2 * part), vmem(rank, 2 * part),
        vmem(across, turn_rows, 2 * part), vmem(across, turn_rows, 2 * part),
        vmem(LINE, turn_rows, line_width), vmem(LINE, turn_rows, line_width),
        vmem(turn_rows, line_width), vmem(turn_rows, line_width),
        vmem(2, across, LINE, turn_rows, line_width), vmem(rank, width),
        dma((5,)), dma((5,)), dma((across,)), dma((across,)), dma((LINE,)), dma((LINE,)),
        dma((across,)), dma((across,)), dma((LINE,)), dma((LINE,)),
    ]
    return pl.pallas_call(
        functools.partial(step_kernel, own_count, per_pair, rank),
        out_shape=(
            pltpu.VMEM((tiles, rows, width), f32),
            pltpu.VMEM((slots, rows, width), f32),
            pltpu.VMEM((emb_rows, width), f32),
            pltpu.VMEM((emb_rows, width), f32),
        ),
        in_specs=[pl.BlockSpec(memory_space=pltpu.VMEM)] + [pl.BlockSpec(memory_space=pltpu.HBM)] * 7
        + [pl.BlockSpec(memory_space=pltpu.VMEM)],
        out_specs=(pl.BlockSpec(memory_space=pltpu.VMEM),) * 4,
        scratch_shapes=scratch,
        compiler_params=pltpu.CompilerParams(
            collective_id=0, has_side_effects=True, vmem_limit_bytes=50 * 1024 * 1024
        ),
        cost_estimate=pl.CostEstimate(flops=20000000, bytes_accessed=300000000, transcendentals=0),
    )(owner, weights, anchor, momentum, *embed)


def write_kernel(parts, *refs):
    count = len(parts)
    sources, targets, sem = refs[:count], refs[count : 2 * count], refs[2 * count]
    copies = []
    for source, target, pieces in zip(sources, targets, parts):
        size = source.shape[0] // pieces
        for n in range(pieces):
            at = pl.ds(n * size, size)
            copies.append(pltpu.make_async_copy(source.at[at], target.at[at], sem.at[len(copies)]))
    for copy in copies:
        copy.start()
    for copy in copies:
        copy.wait()


def write_out(results):
    parts = tuple(8 if r.ndim == 3 and r.shape[0] % 8 == 0 else 2 for r in results)
    return pl.pallas_call(
        functools.partial(write_kernel, parts),
        out_shape=tuple(jax.ShapeDtypeStruct(r.shape, r.dtype) for r in results),
        in_specs=[pl.BlockSpec(memory_space=pltpu.VMEM)] * len(results),
        out_specs=(pl.BlockSpec(memory_space=pltpu.HBM),) * len(results),
        scratch_shapes=[pltpu.SemaphoreType.DMA((sum(parts),))],
        compiler_params=pltpu.CompilerParams(vmem_limit_bytes=1024 * 1024),
        cost_estimate=pl.CostEstimate(flops=0, bytes_accessed=11000000, transcendentals=0),
    )(*results)


def local(
    weights, anchor, momentum, owner, emb_weights, emb_anchor, emb_momentum, sketch, inv_root
):
    own_count = lax.axis_size("own")
    tiles_dev = weights.shape[1]
    half_tiles = min(tiles_dev // 2, own_count)
    hot_count = max(own_count // 4, 1)
    per_pair = (tiles_dev - half_tiles) // hot_count + 1
    embed = (emb_weights, emb_anchor, emb_momentum, sketch, inv_root)
    results = step_call(weights, anchor, momentum, embed, owner[None, :], own_count, per_pair)
    return write_out(results)


def solution(mesh):
    placed = (
        P("rep", "own", None, None),
        P("own", None, None),
        P("own", None, None),
        P(),
        P("rep", "own", None),
        P("own", None),
        P("own", None),
        P(),
        P(),
    )
    return jax.shard_map(
        local,
        mesh=mesh,
        in_specs=placed,
        out_specs=(P("own", None, None), P("own", None, None), P("own", None), P("own", None)),
        check_vma=False,
    )
```

```python
import functools

import jax
import jax.numpy as jnp
from jax import lax
from jax.experimental import pallas as pl
from jax.experimental.pallas import tpu as pltpu
from jax.sharding import PartitionSpec as P

OUTER_RATE = 0.7
OUTER_MOMENTUM = 0.9
FIXED = 1.0 + OUTER_MOMENTUM
SQUARED = OUTER_MOMENTUM * OUTER_MOMENTUM
LINE = 4
CHUNKS = 4
(
    HALF, DIFF, SKETCH, HELD, LATE, RELAY, MEAN, LINED, TURNED,
    PASS, BASE, ADVANCE, MERGE, RENEW, FRESH, EMBED, CLOSE,
) = range(17)
ORDER = (
    (LATE,), (HELD, 3), (HALF, 1), (HELD, 2), (HALF, 0), (HALF, 2), (HELD, -3), (HELD, -2), (HELD, 1),
    (DIFF,), (RELAY, 2), (MEAN, 1), (RELAY, 3), (BASE, 0), (SKETCH,), (MEAN, 0), (MERGE, 0, -3), (HALF, 3),
    (MEAN, 2), (LINED, 1, 1), (LINED, 1, -1), (MERGE, 0, 3), (MERGE, 2, -3), (LINED, 0, 1), (EMBED, 0),
    (MERGE, 1, -3), (LINED, 2, -1), (MERGE, 2, 3), (LINED, 0, -1), (TURNED, 1, 0), (EMBED, 1), (BASE, 3),
    (LINED, 2, 1), (MEAN, 3), (MERGE, 3, 3), (HELD, -1), (TURNED, 2, 0), (LINED, 0, 2), (TURNED, 0, 1),
    (BASE, 2), (TURNED, 0, -1), (LINED, 1, -2), (TURNED, 1, 1), (EMBED, 2), (TURNED, 2, -1), (TURNED, 1, -1),
    (MERGE, 0, -2), (BASE, 1), (TURNED, 2, 1), (LINED, 2, 2), (MERGE, 0, 2), (MERGE, 3, -3), (TURNED, 3, 0),
    (LINED, 2, -2), (MERGE, 1, 3), (LINED, 3, -1), (MERGE, 2, 2), (LINED, 0, -2), (LINED, 1, 2),
    (LINED, 1, -3), (LINED, 0, 3), (MERGE, 2, -2), (EMBED, 3), (TURNED, 0, 2), (PASS, 1, 0), (LINED, 3, 1),
    (TURNED, 1, -2), (TURNED, 0, 0), (HELD, 0), (LINED, 2, 3), (PASS, 0, 1), (TURNED, 2, -2), (MERGE, 1, 2),
    (PASS, 2, 0), (LINED, 2, -3), (MERGE, 3, -2), (TURNED, 3, -1), (PASS, 2, -1), (MERGE, 1, -2),
    (PASS, 1, 1), (LINED, 1, 3), (PASS, 0, -1), (TURNED, 1, -3), (TURNED, 2, 2), (MERGE, 3, 2), (PASS, 2, 1),
    (TURNED, 3, 1), (LINED, 3, 2), (PASS, 3, 0), (LINED, 3, -2), (PASS, 1, -1), (TURNED, 0, -2), (EMBED, 4),
    (TURNED, 0, 3), (MERGE, 0, 1), (MERGE, 0, -1), (LINED, 0, -3), (TURNED, 2, -3), (LINED, 3, -3),
    (MERGE, 2, -1), (MERGE, 2, 1), (PASS, 0, 2), (TURNED, 2, 3), (MERGE, 1, -1), (PASS, 1, -2), (MERGE, 1, 1),
    (MERGE, 3, 1), (MERGE, 3, -1), (TURNED, 0, -3), (PASS, 2, -2), (TURNED, 3, 2), (PASS, 3, -1),
    (TURNED, 1, 3), (PASS, 0, 0), (LINED, 3, 3), (PASS, 2, 3), (TURNED, 3, -2), (PASS, 0, 3), (PASS, 2, 2),
    (TURNED, 1, 2), (PASS, 2, -3), (EMBED, 5), (PASS, 3, 1), (RENEW, 0), (ADVANCE, 2), (PASS, 1, -3),
    (PASS, 0, -3), (PASS, 1, 3), (PASS, 0, -2), (PASS, 3, 2), (TURNED, 3, 3), (TURNED, 3, -3), (PASS, 3, -2),
    (RENEW, 2), (PASS, 1, 2), (ADVANCE, 0), (RENEW, 1), (EMBED, 6), (FRESH, 0), (PASS, 3, -3), (PASS, 3, 3),
    (CLOSE,), (RENEW, 3), (ADVANCE, 1), (ADVANCE, 3), (FRESH, 2), (FRESH, 1), (EMBED, 7), (FRESH, 3),
)


def fill_tables(owner, table, own_index, own_count, tiles_dev, per_pair, slots):
    across_bits, tile_bits = (own_count // LINE).bit_length() - 1, tiles_dev.bit_length() - 1
    count, step = owner.shape[1], min(256, owner.shape[1])
    lanes = table.shape[1]
    owner_row = owner[...]
    my_z, my_y = own_index // (own_count // LINE), own_index % (own_count // LINE)
    y_mask = (1 << across_bits) - 1
    row_ids = lax.broadcasted_iota(jnp.int32, (step, count), 1)
    out_ids = lax.broadcasted_iota(jnp.int32, (step, lanes), 1)
    totals = None
    for first in range(0, count, step):
        ids = lax.broadcasted_iota(jnp.int32, (step, count), 0) + first
        column = jnp.sum(jnp.where(ids == row_ids, owner_row, 0), axis=1, keepdims=True)
        before = (column == owner_row) & (row_ids < ids)
        near = before & ((row_ids >> tile_bits) == (ids >> tile_bits))
        slot_rank = jnp.sum(before.astype(jnp.int32), axis=1, keepdims=True)
        pair_rank = jnp.sum(near.astype(jnp.int32), axis=1, keepdims=True)
        tile = lax.broadcasted_iota(jnp.int32, (step, 1), 0) + first
        block = tile >> tile_bits
        owner_z, turn = column >> across_bits, (column & y_mask) ^ my_y
        back_key = block * per_pair + pair_rank
        held = column == own_index
        pick_key = jnp.where(
            (owner_z == my_z) & ((block & y_mask) == my_y),
            (turn * LINE + (block >> across_bits)) * per_pair + pair_rank,
            -1,
        )
        merge = jnp.where(
            owner_z == my_z, turn * per_pair + pair_rank, jnp.where(owner_z < my_z, -1, -2)
        )
        pairs = (
            (pick_key, tile & (tiles_dev - 1)),
            (tile, merge),
            (jnp.where(held, slot_rank, -1), back_key + 1),
            (jnp.where(held, back_key, -1), slot_rank),
        )
        found = [
            jnp.sum(jnp.where(key == out_ids, value, 0), axis=0, keepdims=True)
            for key, value in pairs
        ]
        totals = found if totals is None else [a + b for a, b in zip(totals, found)]
    across = own_count // LINE
    limits = (tiles_dev - 1, across * per_pair - 1, own_count * per_pair, slots - 1)
    for n, (total, limit) in enumerate(zip(totals, limits)):
        table[n : n + 1, :] = jnp.minimum(total, limit)


def flip(index, bits):
    out, unit = index, 1
    while unit <= bits:
        if bits & unit:
            out = out + unit - 2 * unit * ((index // unit) % 2)
        unit *= 2
    return out


def step_kernel(
    own_count, per_pair, rank,
    owner, weights, anchor, momentum,
    emb_weights, emb_anchor, emb_momentum, sketch, inv_root,
    new_weights, new_momentum, new_embedding, new_emb_momentum,
    *scratch,
):
    across, chunks = own_count // LINE, CHUNKS
    take = iter(scratch)
    local_sem, mine_sem = next(take), next(take)
    table, table_read = next(take), next(take)
    news = {d: next(take) for d in range(1 - LINE, LINE) if abs(d) > 1}
    held_order = [at[1] for at in ORDER if at[0] == HELD]
    merge_order = {at[2]: at[1] for at in reversed(ORDER) if at[0] == MERGE}
    renew_order = [at[1] for at in ORDER if at[0] == RENEW]
    base_order = [at[1] for at in ORDER if at[0] == BASE]
    anchor_part, momentum_part, anchor_all = next(take), next(take), next(take)
    mine, core_in, chip_out, chip_in = next(take), next(take), next(take), next(take)
    core_send, core_recv, chip_send, chip_recv = next(take), next(take), next(take), next(take)
    line = [{d: next(take) for d in range(1 - LINE, LINE)} for _ in range(chunks)]
    line_send, line_recv = next(take), next(take)
    turned = next(take)
    turn_send, turn_recv = next(take), next(take)
    gathered = [next(take) for _ in range(chunks)]
    cross_send, cross_recv, near_send, near_recv, pass_send, pass_recv = (next(take) for _ in range(6))
    held_out = next(take)
    held_in = {d: next(take) for d in range(1 - LINE, LINE)}
    held_send, held_recv = next(take), next(take)
    merged = {d: next(take) for d in range(1 - LINE, LINE) if d}
    below = {d: next(take) for d in range(LINE - 1)}
    above = {-d: next(take) for d in range(LINE - 1)}
    merge_send, merge_recv = next(take), next(take)
    fresh_send, fresh_recv = next(take), next(take)
    emb_w, emb_a, emb_m, sketch_v = next(take), next(take), next(take), next(take)
    diff, sketch_own, sketch_half, sketch_core, sketch_chip, basis_ref = (next(take) for _ in range(6))
    f_own, f_core, f_turn, f_turn_in, f_line, f_line_in, f_chip, f_chip_in, f_all, f_flat = (
        next(take) for _ in range(10)
    )
    emb_send, emb_recv, f_turn_send, f_turn_recv, f_line_send, f_line_recv = (
        next(take) for _ in range(6)
    )
    g_turn_send, g_turn_recv, g_line_send, g_line_recv = (next(take) for _ in range(4))

    rep = lax.axis_index("rep")
    own = lax.axis_index("own")
    core = rep % 2
    z, y = own // across, own % across
    core_peer, chip_peer, far_peer = flip(rep, 1), flip(rep, 2), flip(rep, 3)
    tiles, slots = weights.shape[1], anchor.shape[0]
    width = anchor.shape[2]
    part = width // 4
    w = part // chunks
    f32, highest = jnp.float32, lax.Precision.HIGHEST

    def columns(quarter, c=None):
        if c is None:
            return pl.ds(pl.multiple_of(quarter * part, 128), part)
        return pl.ds(pl.multiple_of(quarter * part + c * w, 128), w)

    def remote(src, dst, send, recv, to_rep, to_own):
        return pltpu.make_async_remote_copy(
            src_ref=src, dst_ref=dst, send_sem=send, recv_sem=recv,
            device_id=(to_rep, to_own), device_id_type=pl.DeviceIdType.MESH,
        )

    def when(*conditions):
        held = conditions[0]
        for condition in conditions[1:]:
            held = held & condition
        return pl.when(held)

    def inside(d):
        return (z + d >= 0) & (z + d <= LINE - 1)

    mine_loads = [
        pltpu.make_async_copy(
            weights.at[0, :, :, columns(quarter, c)], mine.at[c, j], mine_sem.at[c, j]
        )
        for j, quarter in ((1, chip_peer), (0, rep))
        for c in range(chunks)
    ]
    emb_loads = [
        pltpu.make_async_copy(emb_weights.at[0], emb_w, local_sem.at[0]),
        pltpu.make_async_copy(emb_anchor, emb_a, local_sem.at[1]),
        pltpu.make_async_copy(sketch, sketch_v, local_sem.at[2]),
    ]
    part_loads = [
        pltpu.make_async_copy(anchor.at[:, :, columns(rep)], anchor_part, local_sem.at[3]),
        pltpu.make_async_copy(momentum.at[:, :, columns(rep)], momentum_part, local_sem.at[4]),
    ]
    late_loads = [
        pltpu.make_async_copy(anchor, anchor_all, local_sem.at[5]),
        pltpu.make_async_copy(momentum, new_momentum, local_sem.at[6]),
        pltpu.make_async_copy(emb_momentum, emb_m, local_sem.at[7]),
    ]

    barrier = pltpu.get_barrier_semaphore()
    peers = [(core_peer, own), (chip_peer, own)]
    peers += [(rep, flip(own, k)) for k in range(1, across)]
    for peer in peers:
        pl.semaphore_signal(barrier, inc=1, device_id=peer, device_id_type=pl.DeviceIdType.MESH)
    inner = (z >= 1) & (z <= LINE - 2)

    def tell(sem, step):
        pl.semaphore_signal(
            sem, inc=1, device_id=(rep, own + step * across), device_id_type=pl.DeviceIdType.MESH
        )

    for step in (1, -1):
        @pl.when(inside(step))
        def _(step=step):
            tell(barrier, step)

    for copy in emb_loads + mine_loads + part_loads:
        copy.start()

    fill_tables(owner, table, own, own_count, tiles, per_pair, slots)
    table_load = pltpu.make_async_copy(table, table_read, local_sem.at[8])
    table_load.start()
    pl.semaphore_wait(barrier, len(peers) + 1 + jnp.where(inner, 1, 0))

    core_copies = [
        remote(
            weights.at[0, :, :, columns(quarter, c)], core_in.at[c, j],
            core_send.at[c, j], core_recv.at[c, j], core_peer, own,
        )
        for j, quarter in ((1, far_peer), (0, core_peer))
        for c in range(chunks)
    ]
    sketch_copies = [
        remote(sketch_own, sketch_core, emb_send.at[0], emb_recv.at[0], core_peer, own),
        remote(sketch_half, sketch_chip, emb_send.at[1], emb_recv.at[1], chip_peer, own),
    ]
    for copy in core_copies:
        copy.start()
    table_load.wait()

    def held_copy(d, k):
        return remote(
            held_out.at[z + d, k - 1], held_in[d].at[pl.ds(k * per_pair, per_pair)],
            held_send.at[d + LINE - 1, k], held_recv.at[d + LINE - 1, k], rep, flip(own, k),
        )

    def held_fill(d, k):
        block = flip(own, k) + d * across

        def fill(p, carry):
            slot = table_read[3, block * per_pair + p]
            a = anchor_part[slot]
            value = a - OUTER_RATE * (FIXED * a + SQUARED * momentum_part[slot])
            if k:
                held_out[z + d, k - 1, p] = value
            else:
                held_in[d][p] = value
            return carry

        lax.fori_loop(0, per_pair, fill, 0)

    def held_start(d):
        if d == held_order[0]:
            for copy in part_loads:
                copy.wait()

        @when(inside(d))
        def _():
            for k in range(1, across):
                held_fill(d, k)
                held_copy(d, k).start()
            held_fill(d, 0)

    chip_copies = [
        remote(chip_out.at[c], chip_in.at[c], chip_send.at[c], chip_recv.at[c], chip_peer, own)
        for c in range(chunks)
    ]

    def half_sum(c):
        mine_loads[c].wait()
        core_copies[c].wait_recv()
        chip_out[c] = mine[c, 1] + core_in[c, 1]
        chip_copies[c].start()

    def sketch_start():
        for copy in emb_loads:
            copy.wait()
        diff[...] = emb_a[...] - emb_w[...]
        sketched = jnp.zeros(sketch_own.shape, f32)
        for q in range(4):
            at = slice(q * part, (q + 1) * part)
            sketched = sketched + lax.dot_general(
                sketch_v[:, at], diff[:, at], (((1,), (1,)), ((), ())),
                precision=highest, preferred_element_type=f32,
            )
        sketch_own[...] = sketched
        sketch_copies[0].start()

    def sketch_sum():
        sketch_copies[0].wait_recv()
        sketch_half[...] = sketch_own[...] + sketch_core[...]
        sketch_copies[1].start()

    def late_start():
        for copy in late_loads:
            copy.start()

    def relay(distance):
        for step in (1, -1):
            d = step * distance
            if distance > 2:
                @when(inside(d - step))
                def _(d=d, step=step):
                    pl.semaphore_wait(news[d - step], 1)

            @when(inside(d - step), inside(-step))
            def _(d=d, step=step):
                tell(news[d], -step)

    turn_rows, line_width = rank // across, 2 * part // LINE

    def emb_core():
        return remote(f_own.at[1 - core], f_core, emb_send.at[2], emb_recv.at[2], core_peer, own)

    def emb_turn(k):
        return remote(
            f_turn.at[flip(y, k)], f_turn_in.at[k], f_turn_send.at[k], f_turn_recv.at[k],
            rep, flip(own, k),
        )

    def emb_line(k):
        return remote(
            f_line.at[flip(z, k)], f_line_in.at[k], f_line_send.at[k], f_line_recv.at[k],
            rep, flip(own, k * across),
        )

    def emb_chip():
        return remote(f_chip, f_chip_in, emb_send.at[3], emb_recv.at[3], chip_peer, own)

    def back_line(k):
        here = f_all.at[core, y, z]
        return remote(here, here, g_line_send.at[k], g_line_recv.at[k], rep, flip(own, k * across))

    def back_turn(k):
        here = f_all.at[core, y]
        return remote(here, here, g_turn_send.at[k], g_turn_recv.at[k], rep, flip(own, k))

    def back_core():
        here = f_all.at[core]
        return remote(here, here, emb_send.at[4], emb_recv.at[4], core_peer, own)

    def embed_step(n):
        (emb_0, emb_1, emb_2, emb_3, emb_4, emb_5, emb_6, emb_7)[n]()

    def emb_0():
        sketch_copies[1].wait_recv()
        mean_sketch = (sketch_half[...] + sketch_chip[...]) * 0.25
        basis = jnp.dot(inv_root[...], mean_sketch, precision=highest, preferred_element_type=f32)
        basis_ref[...] = basis
        for q in range(4):
            f_own[q % 2, :, (q // 2) * part : (q // 2 + 1) * part] = jnp.dot(
                basis, diff[:, q * part : (q + 1) * part],
                precision=highest, preferred_element_type=f32,
            )
        emb_core().start()

    def emb_1():
        emb_core().wait_recv()
        for b in range(across):
            rows = slice(b * turn_rows, (b + 1) * turn_rows)
            f_turn[b] = f_own[core, rows] + f_core[rows]
        for k in range(1, across):
            emb_turn(k).start()

    def emb_2():
        for k in range(1, across):
            emb_turn(k).wait_recv()
        total = f_turn[y]
        for k in range(1, across):
            total = total + f_turn_in[k]
        for step in (1, -1):
            @when(inside(step * (LINE - 1)))
            def _(step=step):
                pl.semaphore_wait(news[step * (LINE - 1)], 1)

        for a in range(LINE):
            f_line[a] = total[:, a * line_width : (a + 1) * line_width]
        for k in range(1, LINE):
            emb_line(k).start()

    def emb_3():
        for k in range(1, LINE):
            emb_line(k).wait_recv()
        total = f_line[z]
        for k in range(1, LINE):
            total = total + f_line_in[k]
        f_chip[...] = total
        emb_chip().start()

    def emb_4():
        emb_chip().wait_recv()
        f_all[core, y, z] = (f_chip[...] + f_chip_in[...]) * 0.25
        for k in range(1, LINE):
            back_line(k).start()

    def emb_5():
        for k in range(1, LINE):
            back_line(k).wait_recv()
        for k in range(1, across):
            back_turn(k).start()

    def emb_6():
        for k in range(1, across):
            back_turn(k).wait_recv()
        back_core().start()

    def emb_7():
        late_loads[2].wait()
        back_core().wait_recv()
        for h in range(2):
            for b in range(across):
                for a in range(LINE):
                    quarter = h + 2 * ((a * line_width) // part)
                    at = quarter * part + (a * line_width) % part
                    f_flat[b * turn_rows : (b + 1) * turn_rows, at : at + line_width] = f_all[h, b, a]
        for q in range(4):
            at = slice(q * part, (q + 1) * part)
            approx = lax.dot_general(
                basis_ref[...], f_flat[:, at], (((0,), (0,)), ((), ())),
                precision=highest, preferred_element_type=f32,
            )
            moved = OUTER_MOMENTUM * emb_m[:, at] + approx
            new_emb_momentum[:, at] = moved
            new_embedding[:, at] = emb_a[:, at] - OUTER_RATE * (approx + OUTER_MOMENTUM * moved)

    def line_copy(c, d):
        step = 1 if d > 0 else -1
        return remote(
            line[c][d - step], line[c][d], line_send.at[c, d + LINE - 1],
            line_recv.at[c, d + LINE - 1], rep, own - step * across,
        )

    def line_sends(d):
        step = 1 if d > 0 else -1
        return (z - step >= 0) & (z - step <= LINE - 1) & inside(d - step)

    def rows_of(d, k):
        return pl.ds((flip(own, k) + d * across) * per_pair, per_pair)

    def turn_copy(c, d, k, sending):
        return remote(
            turned.at[c, z + d, k - 1], gathered[c].at[rep, rows_of(d, 0 if sending else k)],
            turn_send.at[c, d + LINE - 1, k], turn_recv.at[c, d + LINE - 1, k], rep, flip(own, k),
        )

    def item_copy(c, d, k, kind):
        at = (c, d + LINE - 1, k)
        if kind == "cross":
            here = gathered[c].at[rep, rows_of(d, k)]
            return remote(here, here, cross_send.at[at], cross_recv.at[at], chip_peer, own)
        rows = pl.ds((z + d) * across * per_pair, across * per_pair)
        if kind == "pass":
            there = gathered[c].at[chip_peer, rows]
            return remote(there, there, pass_send.at[at], pass_recv.at[at], core_peer, own)
        here = gathered[c].at[rep, rows]
        return remote(here, here, near_send.at[at], near_recv.at[at], core_peer, own)

    def choose(c, d, k):
        block = (k * LINE + z + d) * per_pair
        first = (own + d * across) * per_pair

        def fill(p, carry):
            value = line[c][d][table_read[0, block + p]]
            if k:
                turned[c, z + d, k - 1, p] = value
            else:
                gathered[c][rep, first + p] = value
            return carry

        lax.fori_loop(0, per_pair, fill, 0, unroll=True)

    def spread(c, d):
        for k in range(1, across):
            choose(c, d, k)
            turn_copy(c, d, k, True).start()
        choose(c, d, 0)
        item_copy(c, d, 0, "cross").start()

    def mean_ready(c):
        mine_loads[chunks + c].wait()
        core_copies[chunks + c].wait_recv()
        chip_copies[c].wait_recv()
        line[c][0][...] = (mine[c, 0] + core_in[c, 0] + chip_in[c]) * 0.25
        for d in (1, -1):
            @when(line_sends(d))
            def _(d=d):
                line_copy(c, d).start()
        spread(c, 0)

    def line_arrived(c, d):
        step = 1 if d > 0 else -1

        @when(inside(d))
        def _():
            line_copy(c, d).wait_recv()
            if abs(d) < LINE - 1:
                @when(line_sends(d + step))
                def _():
                    line_copy(c, d + step).start()
            spread(c, d)

    def turn_arrived(c, d):
        @when(inside(d))
        def _():
            for k in range(1, across):
                turn_copy(c, d, k, False).wait_recv()
                item_copy(c, d, k, "cross").start()
            item_copy(c, d, 0, "near").start()

    def pass_on(c, d):
        @when(inside(d))
        def _():
            for k in range(across):
                item_copy(c, d, k, "cross").wait_recv()
            item_copy(c, d, 0, "pass").start()

    def base_rows(piece):
        if piece == base_order[0]:
            late_loads[0].wait()
            late_loads[1].wait()
        first = piece * (slots // chunks)
        count = slots - first if piece == chunks - 1 else slots // chunks

        def body(s, carry):
            for q in range(4):
                at = pl.ds(q * part, part)
                new_momentum[s, :, at] = OUTER_MOMENTUM * new_momentum[s, :, at] + anchor_all[s, :, at]
            return carry

        lax.fori_loop(first, first + count, body, 0)

    def advance(c):
        for d in range(1 - LINE, LINE):
            @when(inside(d))
            def _(d=d):
                item_copy(c, d, 0, "near").wait_recv()
                item_copy(c, d, 0, "pass").wait_recv()

        def one(s):
            found = table_read[2, s]
            row = jnp.maximum(found - 1, 0)
            kept = jnp.full((new_momentum.shape[1], w), found, jnp.int32) > 0
            for q in range(4):
                at = pl.ds(q * part + c * w, w)
                new_momentum[s, :, at] = jnp.where(
                    kept, new_momentum[s, :, at] - gathered[c][q, row], 0.0
                )

        unit = 8 if slots % 8 == 0 else 1

        def body(n, carry):
            for i in range(unit):
                one(n * unit + i)
            return carry

        lax.fori_loop(0, slots // unit, body, 0)

    def merge_copy(d, c):
        step = 1 if d > 0 else -1
        target = (below if d > 0 else above)[d - step]
        at = (c, d + LINE - 1)
        return remote(
            merged[d].at[c], target.at[c], merge_send.at[at], merge_recv.at[at], rep, own + step * across
        )

    def merge_tiles(d, c, store, incoming):
        first = (own + d * across) * tiles
        at = pl.ds(c * w, w)

        def body(t, carry):
            key = table_read[1, first + t]
            value = held_in[d][jnp.maximum(key, 0), :, at]
            if incoming is not None:
                keys = jnp.full((value.shape[0], w), key, jnp.int32)
                value = jnp.where(keys >= 0, value, incoming(t, keys))
            store(t, value)
            return carry

        lax.fori_loop(0, tiles, body, 0, unroll=True)

    def merge_step(c, d):
        step = 1 if d > 0 else -1
        source = (below if d > 0 else above).get(d)
        has_source = (z >= 1) if d > 0 else (z <= LINE - 2)

        def store(t, value):
            merged[d][c, t] = value

        def landed():
            if merge_order[d] == c:
                for k in range(1, across):
                    held_copy(d, k).wait_recv()

        @when(inside(d), jnp.logical_not(has_source))
        def _():
            landed()
            merge_tiles(d, c, store, None)
            merge_copy(d, c).start()

        if source is not None:
            @when(inside(d), has_source)
            def _():
                landed()
                merge_copy(d + step, c).wait_recv()
                merge_tiles(d, c, store, lambda t, keys: source[c, t])
                merge_copy(d, c).start()

    def fresh_copy(c, kind):
        at = {"cross": 0, "near": 1, "pass": 2}[kind]
        here = new_weights.at[:, :, columns(chip_peer if kind == "pass" else rep, c)]
        return remote(
            here, here, fresh_send.at[at, c], fresh_recv.at[at, c],
            chip_peer if kind == "cross" else core_peer, own,
        )

    def renew(c):
        @when(z >= 1)
        def _():
            merge_copy(1, c).wait_recv()

        @when(z <= LINE - 2)
        def _():
            merge_copy(-1, c).wait_recv()

        if renew_order[0] == c:
            for k in range(1, across):
                held_copy(0, k).wait_recv()

        def incoming(t, keys):
            return jnp.where(keys == -1, below[0][c, t], above[0][c, t])

        def store(t, value):
            new_weights[t, :, columns(rep, c)] = value + (OUTER_RATE * FIXED) * line[c][0][t]

        merge_tiles(0, c, store, incoming)
        fresh_copy(c, "cross").start()
        fresh_copy(c, "near").start()

    def fresh_pass(c):
        fresh_copy(c, "cross").wait_recv()
        fresh_copy(c, "pass").start()

    def close():
        for copy in core_copies + chip_copies + sketch_copies:
            copy.wait_send()
        for k in range(1, across):
            emb_turn(k).wait_send()
            back_turn(k).wait_send()
        for k in range(1, LINE):
            emb_line(k).wait_send()
            back_line(k).wait_send()
        for copy in (emb_core(), emb_chip(), back_core()):
            copy.wait_send()
        for d in range(1 - LINE, LINE):
            @when(inside(d))
            def _(d=d):
                for k in range(1, across):
                    held_copy(d, k).wait_send()
                for c in range(chunks):
                    for k in range(across):
                        if k:
                            turn_copy(c, d, k, True).wait_send()
                        item_copy(c, d, k, "cross").wait_send()
                    item_copy(c, d, 0, "near").wait_send()
                    item_copy(c, d, 0, "pass").wait_send()
                    if d:
                        merge_copy(d, c).wait_send()

            if d:
                @when(line_sends(d))
                def _(d=d):
                    for c in range(chunks):
                        line_copy(c, d).wait_send()

    steps = {
        HALF: half_sum, DIFF: sketch_start, SKETCH: sketch_sum, HELD: held_start, LATE: late_start, RELAY: relay, MEAN: mean_ready,
        LINED: line_arrived, TURNED: turn_arrived, PASS: pass_on, BASE: base_rows, ADVANCE: advance,
        MERGE: merge_step, RENEW: renew, FRESH: fresh_pass, EMBED: embed_step, CLOSE: close,
    }
    for step, *arguments in ORDER:
        steps[step](*arguments)

    for c in range(chunks):
        fresh_copy(c, "near").wait_recv()
        fresh_copy(c, "pass").wait_recv()
    for c in range(chunks):
        for kind in ("cross", "near", "pass"):
            fresh_copy(c, kind).wait_send()


def step_call(weights, anchor, momentum, embed, owner, own_count, per_pair):
    tiles, rows, width = weights.shape[1:]
    slots, part = anchor.shape[0], width // 4
    across, chunks = own_count // LINE, CHUNKS
    w, span = part // chunks, 2 * LINE - 1
    pairs = own_count * per_pair
    lanes = max(owner.shape[1], -(-max(pairs, slots) // 128) * 128)
    f32, dma = jnp.float32, pltpu.SemaphoreType.DMA
    emb_rows, rank = embed[1].shape[0], embed[3].shape[0]
    vmem = lambda *shape: pltpu.VMEM(shape, f32)
    turn_rows, line_width = rank // across, 2 * part // LINE
    scratch = [
        dma((9,)), dma((chunks, 2)),
        pltpu.VMEM((8, lanes), jnp.int32), pltpu.SMEM((8, lanes), jnp.int32),
        *[pltpu.SemaphoreType.REGULAR for _ in range(2 * (LINE - 2))],
        vmem(slots, rows, part), vmem(slots, rows, part), vmem(slots, rows, width),
        vmem(chunks, 2, tiles, rows, w), vmem(chunks, 2, tiles, rows, w),
        vmem(chunks, tiles, rows, w), vmem(chunks, tiles, rows, w),
        dma((chunks, 2)), dma((chunks, 2)), dma((chunks,)), dma((chunks,)),
    ]
    scratch += [vmem(tiles, rows, w) for _ in range(chunks * span)]
    scratch += [dma((chunks, span)), dma((chunks, span))]
    scratch += [vmem(chunks, LINE, across - 1, per_pair, rows, w)]
    scratch += [dma((chunks, span, across)), dma((chunks, span, across))]
    scratch += [vmem(4, pairs, rows, w) for _ in range(chunks)]
    scratch += [dma((chunks, span, across)) for _ in range(6)]
    scratch += [vmem(LINE, across - 1, per_pair, rows, part)]
    scratch += [vmem(across * per_pair, rows, part) for _ in range(span)]
    scratch += [dma((span, across)), dma((span, across))]
    scratch += [vmem(chunks, tiles, rows, w) for _ in range(span - 1)]
    scratch += [vmem(chunks, tiles, rows, w) for _ in range(2 * (LINE - 1))]
    scratch += [dma((chunks, span)), dma((chunks, span)), dma((3, chunks)), dma((3, chunks))]
    scratch += [
        vmem(emb_rows, width), vmem(emb_rows, width), vmem(emb_rows, width), vmem(rank, width),
        vmem(emb_rows, width),
    ]
    scratch += [vmem(rank, emb_rows) for _ in range(5)]
    scratch += [
        vmem(2, rank, 2 * part), vmem(rank, 2 * part),
        vmem(across, turn_rows, 2 * part), vmem(across, turn_rows, 2 * part),
        vmem(LINE, turn_rows, line_width), vmem(LINE, turn_rows, line_width),
        vmem(turn_rows, line_width), vmem(turn_rows, line_width),
        vmem(2, across, LINE, turn_rows, line_width), vmem(rank, width),
        dma((5,)), dma((5,)), dma((across,)), dma((across,)), dma((LINE,)), dma((LINE,)),
        dma((across,)), dma((across,)), dma((LINE,)), dma((LINE,)),
    ]
    return pl.pallas_call(
        functools.partial(step_kernel, own_count, per_pair, rank),
        out_shape=(
            pltpu.VMEM((tiles, rows, width), f32),
            pltpu.VMEM((slots, rows, width), f32),
            pltpu.VMEM((emb_rows, width), f32),
            pltpu.VMEM((emb_rows, width), f32),
        ),
        in_specs=[pl.BlockSpec(memory_space=pltpu.VMEM)] + [pl.BlockSpec(memory_space=pltpu.HBM)] * 7
        + [pl.BlockSpec(memory_space=pltpu.VMEM)],
        out_specs=(pl.BlockSpec(memory_space=pltpu.VMEM),) * 4,
        scratch_shapes=scratch,
        compiler_params=pltpu.CompilerParams(
            collective_id=0, has_side_effects=True, vmem_limit_bytes=50 * 1024 * 1024
        ),
        cost_estimate=pl.CostEstimate(flops=20000000, bytes_accessed=300000000, transcendentals=0),
    )(owner, weights, anchor, momentum, *embed)


def write_kernel(parts, *refs):
    count = len(parts)
    sources, targets, sem = refs[:count], refs[count : 2 * count], refs[2 * count]
    copies = []
    for source, target, pieces in zip(sources, targets, parts):
        size = source.shape[0] // pieces
        for n in range(pieces):
            at = pl.ds(n * size, size)
            copies.append(pltpu.make_async_copy(source.at[at], target.at[at], sem.at[len(copies)]))
    for copy in copies:
        copy.start()
    for copy in copies:
        copy.wait()


def write_out(results):
    parts = tuple(4 if r.ndim == 3 and r.shape[0] % 4 == 0 else 1 for r in results)
    return pl.pallas_call(
        functools.partial(write_kernel, parts),
        out_shape=tuple(jax.ShapeDtypeStruct(r.shape, r.dtype) for r in results),
        in_specs=[pl.BlockSpec(memory_space=pltpu.VMEM)] * len(results),
        out_specs=(pl.BlockSpec(memory_space=pltpu.HBM),) * len(results),
        scratch_shapes=[pltpu.SemaphoreType.DMA((sum(parts),))],
        compiler_params=pltpu.CompilerParams(vmem_limit_bytes=1024 * 1024),
        cost_estimate=pl.CostEstimate(flops=0, bytes_accessed=11000000, transcendentals=0),
    )(*results)


def local(
    weights, anchor, momentum, owner, emb_weights, emb_anchor, emb_momentum, sketch, inv_root
):
    own_count = lax.axis_size("own")
    tiles_dev = weights.shape[1]
    half_tiles = min(tiles_dev // 2, own_count)
    hot_count = max(own_count // 4, 1)
    per_pair = (tiles_dev - half_tiles) // hot_count + 1
    embed = (emb_weights, emb_anchor, emb_momentum, sketch, inv_root)
    results = step_call(weights, anchor, momentum, embed, owner[None, :], own_count, per_pair)
    return write_out(results)


def solution(mesh):
    placed = (
        P("rep", "own", None, None),
        P("own", None, None),
        P("own", None, None),
        P(),
        P("rep", "own", None),
        P("own", None),
        P("own", None),
        P(),
        P(),
    )
    return jax.shard_map(
        local,
        mesh=mesh,
        in_specs=placed,
        out_specs=(P("own", None, None), P("own", None, None), P("own", None), P("own", None)),
        check_vma=False,
    )
```
